32 devices in a mesh: dp: 8 (over y, x, core), mp: 4 (over z).
Axes of the slice: x: 2, y: 2, z: 4, core: 2. Of those that a mesh axis runs over, the one named last changes fastest.
Arguments:
- inputs: bfloat16 [8192, 2048], P('dp'), may hold values from -8 to 8
- segment_ids: int32 [8, 1024], P('dp'), may hold values from 0 to 4, as said below
- pad_count: int32 [8], P('dp'), may hold values from 0 to 128, as said below
- layer_norm_gain: float32 [2048], replicated, may hold values from 0.5 to 1.5
- layer_norm_bias: float32 [2048], replicated, may hold values from -1.75 to 1.75
- qkv_weight: bfloat16 [2048, 3, 2048], P(None, None, 'mp'), may hold values from -0.125 to 0.125
- qkv_bias: float32 [3, 2048], P(None, 'mp'), may hold values from -1.75 to 1.75
- out_weight: bfloat16 [2048, 2048], P('mp'), may hold values from -1 to 1
- gateup_weight: bfloat16 [2048, 2, 5632], P(None, None, 'mp'), may hold values from -0.125 to 0.125
- down_weight: bfloat16 [5632, 2048], P('mp'), may hold values from -0.078125 to 0.078125
- y_grad: bfloat16 [8192, 2048], P('dp'), may hold values from -8 to 8
Outputs:
- output: bfloat16 [8192, 2048], P('dp')
- x_grad: bfloat16 [8192, 2048], P('dp')
- ln_gain_grad: float32 [2048], replicated
- ln_bias_grad: float32 [2048], replicated
- qkv_weight_grad: float32 [2048, 3, 2048], P('dp', None, 'mp')
- qkv_bias_grad: float32 [3, 2048], P(None, 'mp')
- out_weight_grad: float32 [2048, 2048], P('mp', 'dp')
- gateup_weight_grad: float32 [2048, 2, 5632], P('dp', None, 'mp')
- down_weight_grad: float32 [5632, 2048], P('mp', 'dp')
The draws below stay inside these ranges and needn't reach their ends.
Inputs may be any that keep to these rules, and one draw needn't show every extreme that they name: `segment_ids`: within a row the ids never fall and run from 0 to 4 - 1 over the row's documents, each of 1 or more tokens and one of exactly 512; the row's last pad_count slots carry id 4. `pad_count`: some row has 128 padded slots and some row has none.
All inputs are finite; a program needn't handle non-finite values.
Results may differ from the reference program's by a relative error of at most 0.012.
The reference program's roundings to bfloat16 on the way count: a program that leaves them out, or rounds other values in their place, can miss the bound.
Values may be sent and summed in bfloat16 or wider, within the bound.
No kernel may reach another device: no remote copies, remote signals or barrier semaphores. Data moves between devices by JAX's collectives and lax.ppermute only.
A program may use at most 256 MiB of HBM per device.

```python
import jax
import jax.numpy as jnp
from jax import lax

D = 2048
HEADS = 32
HEAD_DIM = 64
ROT = 16
FF = 5632
ROW_LEN = 1024
DOCS = 4
DOC_MOST = 512
PAD_MOST = 128
ROWS = 8
TOKENS = 8192


def layout(key):
    base_key = jax.random.fold_in(key, 11)
    key_pad, key_top, key_swing, key_roll = jax.random.split(base_key, 4)
    row_index = jnp.arange(ROWS, dtype=jnp.int32)
    padding = jax.random.randint(key_pad, (ROWS,), 0, PAD_MOST + 1)
    top_row = jax.random.randint(key_top, (), 0, ROWS)
    padding = jnp.where(row_index == top_row, PAD_MOST, padding)
    padding = jnp.where(row_index == (top_row + 1) % ROWS, 0, padding)
    others = DOCS - 1
    remain = ROW_LEN - padding - DOC_MOST
    share = remain // others
    extra = remain - share * others
    slots = jnp.arange(others, dtype=jnp.int32)
    sizes_left = share[:, None] + (slots[None, :] < extra[:, None]).astype(jnp.int32)
    swing = (ROW_LEN - PAD_MOST - DOC_MOST) // others // 3
    pairs = others // 2
    delta = jax.random.randint(key_swing, (ROWS, pairs), -swing, swing + 1)
    moved = jnp.stack([delta, -delta], axis=-1).reshape(ROWS, 2 * pairs)
    moved = jnp.concatenate([moved, jnp.zeros((ROWS, others - 2 * pairs), jnp.int32)], axis=1)
    sizes_left = sizes_left + moved
    full = jnp.concatenate([jnp.full((ROWS, 1), DOC_MOST, jnp.int32), sizes_left], axis=1)
    roll = jax.random.randint(key_roll, (ROWS,), 0, DOCS)
    order = (jnp.arange(DOCS, dtype=jnp.int32)[None, :] + roll[:, None]) % DOCS
    lengths = jnp.take_along_axis(full, order, axis=1).astype(jnp.int32)
    ends = jnp.cumsum(lengths, axis=1)
    steps = jnp.arange(ROW_LEN, dtype=jnp.int32)
    seg = jnp.sum((steps[None, :, None] >= ends[:, None, :]).astype(jnp.int32), axis=-1)
    return (seg.astype(jnp.int32), padding.astype(jnp.int32))


def draw_segment_ids(key, part):
    return layout(key)[0]


def draw_pad_count(key, part):
    return layout(key)[1]


def spiked(values, rng, source, target, shards_of, factor):
    owner, partner = [(jnp.arange(values.shape[dim]) // (values.shape[dim] // shards_of)).reshape([-1 if axis == dim else 1 for axis in range(values.ndim)]) for dim in (source, target)]
    chosen = jax.random.permutation(rng, shards_of)[partner]
    strong = (owner == chosen) | (owner == (partner + shards_of // 2) % shards_of)
    return jnp.where(strong, factor * values, values)


def block_levels(key, shape, cuts, least, largest):
    loudness = 1.0
    for position, shards_of in cuts:
        heights = jax.random.uniform(jax.random.fold_in(jax.random.fold_in(key, 6), position), (shards_of,), jnp.float32, least / len(cuts), largest / len(cuts))
        loudness = loudness * jnp.repeat(jnp.exp(heights), shape[position] // shards_of).reshape((-1,) + (1,) * (len(shape) - 1 - position))
    return loudness


def noise(rng, shape, spread, most, cuts=(), kind=jnp.bfloat16):
    values = spread * jax.random.normal(rng, shape, jnp.float32)
    if cuts:
        values = values * block_levels(rng, shape, cuts, -0.22, 0.18)
    return jnp.clip(values, -most, most).astype(kind)


def noise_with(rng, shape, deviation, most, shards, heavy, held_as=jnp.bfloat16):
    values = deviation * jax.random.normal(rng, shape, jnp.float32)
    if shards:
        values = values * block_levels(rng, shape, shards, -0.22, 0.18)
    return jnp.clip(spiked(values, jax.random.fold_in(rng, 3), *heavy), -most, most).astype(held_as)


def setup_inputs(seed: int = 0) -> dict:
    seeds = jax.random.split(jax.random.key(seed), 12)
    inputs = noise_with(seeds[0], (TOKENS, D), 1.0, 8.0, ((0, 8),), (0, 1, 8, 2.0))
    segment_ids = draw_segment_ids(jax.random.fold_in(seeds[11], 71), 0)
    pad_count = draw_pad_count(jax.random.fold_in(seeds[11], 71), 0)
    layer_norm_gain = jnp.clip(1.0 + 0.1 * jax.random.normal(seeds[3], (D,), jnp.float32), 0.5, 1.5)
    layer_norm_bias = noise(seeds[4], (D,), 0.3, 1.75, (), jnp.float32)
    qkv_weight = noise(seeds[5], (D, 3, D), D ** -0.5, 0.125, ((2, 4),))
    qkv_bias = noise(seeds[6], (3, D), 0.3, 1.75, ((1, 4),), jnp.float32)
    out_weight = noise(seeds[7], (D, D), (D // 64) ** -0.5, 1.0, ((0, 4),))
    gateup_weight = noise(seeds[8], (D, 2, FF), D ** -0.5, 0.125, ((2, 4),))
    down_weight = noise(seeds[9], (FF, D), FF ** -0.5, 0.078125, ((0, 4),))
    y_grad = noise_with(seeds[10], (TOKENS, D), 1.0, 8.0, ((0, 8),), (0, 1, 8, 2.0))
    return {"inputs": inputs, "segment_ids": segment_ids, "pad_count": pad_count, "layer_norm_gain": layer_norm_gain, "layer_norm_bias": layer_norm_bias, "qkv_weight": qkv_weight, "qkv_bias": qkv_bias, "out_weight": out_weight, "gateup_weight": gateup_weight, "down_weight": down_weight, "y_grad": y_grad}


@jax.custom_vjp
def low(v):
    return lax.optimization_barrier(v.astype(jnp.bfloat16)).astype(jnp.float32)

@jax.custom_vjp
def low_back(v):
    return v

def low_keep(v):
    return (low(v), None)

def low_pass(kept, grad):
    return (grad,)

def back_keep(v):
    return (v, None)

def back_low(kept, grad):
    return (low(grad),)
low.defvjp(low_keep, low_pass)
low_back.defvjp(back_keep, back_low)
EPS = 1e-05
HIGH = lax.Precision.HIGHEST

def tables(seg, pad):
    steps = jnp.arange(ROW_LEN, dtype=jnp.int32)
    onehot = (seg[:, None] == jnp.arange(DOCS + 1, dtype=jnp.int32)[None, :]).astype(jnp.int32)
    counts = lax.optimization_barrier(jnp.sum(onehot, axis=0))
    before = jnp.cumsum(counts) - counts
    start = lax.optimization_barrier(jnp.sum(onehot * before[None, :], axis=1))
    half = ROT // 2
    freq = jnp.power(10000.0, -2.0 * jnp.arange(half, dtype=jnp.float32) / ROT)
    angle = (steps - start).astype(jnp.float32)[:, None] * freq[None, :]
    return (jnp.cos(angle)[:, None, :], jnp.sin(angle)[:, None, :], steps < ROW_LEN - pad)

def rotate(value, cosine, sine):
    half = ROT // 2
    first = value[..., :half]
    second = value[..., half:ROT]
    return jnp.concatenate([first * cosine - second * sine, second * cosine + first * sine, value[..., ROT:]], axis=-1)

def attend(start, query, key, value, seg, valid):
    block_rows = min(512, ROW_LEN)
    part = lax.dynamic_slice_in_dim(query, start, block_rows, 0)
    score = jnp.einsum('qhd,khd->hqk', part, key, precision=HIGH) * HEAD_DIM ** (-0.5)
    score = low_back(score)
    rows = start + jnp.arange(block_rows, dtype=jnp.int32)
    cols = jnp.arange(ROW_LEN, dtype=jnp.int32)
    seg_rows = lax.dynamic_slice_in_dim(seg, start, block_rows, 0)
    allowed = (seg_rows[:, None] == seg[None, :]) & (cols[None, :] <= rows[:, None]) & valid[None, :]
    allowed = allowed | (cols[None, :] == rows[:, None])
    score = jnp.where(allowed[None], score, -1e+30)
    top = lax.optimization_barrier(jnp.max(score, axis=-1, keepdims=True))
    expo = jnp.exp(score - top)
    prob = low(expo / lax.optimization_barrier(jnp.sum(expo, axis=-1, keepdims=True)))
    return jnp.einsum('hqk,khd->qhd', prob, value, precision=HIGH)

def row_forward(xrow, seg, pad, gain, shift, wqkv, bqkv, wout, wgu, wdown):
    row_average = lax.optimization_barrier(jnp.mean(xrow, axis=-1, keepdims=True))
    mean_removed = xrow - row_average
    var = lax.optimization_barrier(jnp.mean(mean_removed * mean_removed, axis=-1, keepdims=True))
    norm_output = low(mean_removed * lax.rsqrt(var + EPS) * gain + shift)
    qkv = jnp.dot(norm_output, wqkv.reshape(D, 3 * D), precision=HIGH, preferred_element_type=jnp.float32)
    qkv = low_back(qkv.reshape(ROW_LEN, 3, D) + bqkv)
    cosine, sine, valid = tables(seg, pad)
    query = low(rotate(qkv[:, 0].reshape(ROW_LEN, HEADS, HEAD_DIM), cosine, sine))
    key = low(rotate(qkv[:, 1].reshape(ROW_LEN, HEADS, HEAD_DIM), cosine, sine))
    value = low(qkv[:, 2].reshape(ROW_LEN, HEADS, HEAD_DIM))
    block_rows = min(512, ROW_LEN)
    starts = jnp.arange(ROW_LEN // block_rows, dtype=jnp.int32) * block_rows
    checked = jax.checkpoint(attend)
    blocks = lax.map(lambda st: checked(st, query, key, value, seg, valid), starts)
    attn = blocks.reshape(ROW_LEN, D) * valid.astype(jnp.float32)[:, None]
    attn = low(low_back(attn))
    branch = jnp.dot(attn, wout, precision=HIGH, preferred_element_type=jnp.float32)
    gateup = jnp.dot(norm_output, wgu.reshape(D, 2 * FF), precision=HIGH, preferred_element_type=jnp.float32)
    gateup = low_back(gateup.reshape(ROW_LEN, 2, FF))
    gate = gateup[:, 0]
    hidden = low(gate * jax.nn.sigmoid(gate) * gateup[:, 1])
    branch = branch + jnp.dot(hidden, wdown, precision=HIGH, preferred_element_type=jnp.float32)
    return xrow + branch

def reference(inputs, segment_ids, pad_count, layer_norm_gain, layer_norm_bias, qkv_weight, qkv_bias, out_weight, gateup_weight, down_weight, y_grad):
    row_checked = jax.checkpoint(row_forward)

    def forward(xf, gain, shift, wqkv, bqkv, wout, wgu, wdown):
        rows_in = xf.reshape(ROWS, ROW_LEN, D)
        outs = lax.map(lambda item: row_checked(item[0], item[1], item[2], gain, shift, wqkv, bqkv, wout, wgu, wdown), (rows_in, segment_ids, pad_count))
        return outs.reshape(TOKENS, D)
    primals = (inputs.astype(jnp.float32), layer_norm_gain, layer_norm_bias, qkv_weight.astype(jnp.float32), qkv_bias, out_weight.astype(jnp.float32), gateup_weight.astype(jnp.float32), down_weight.astype(jnp.float32))
    result, pullback = jax.vjp(forward, *primals)
    grads = pullback(y_grad.astype(jnp.float32))
    return (result.astype(jnp.bfloat16), grads[0].astype(jnp.bfloat16), grads[1], grads[2], grads[3], grads[4], grads[5], grads[6], grads[7])
```

```python
import functools
import math

import jax
import jax.numpy as jnp
import numpy as np
from jax import lax
from jax.experimental import pallas as pl
from jax.experimental.pallas import tpu as pltpu
from jax.sharding import PartitionSpec as P

HEAD_DIM = 64
ROT = 16
DOCS = 4
DOC_MOST = 512
EPS = 1e-05
BQ = 256
LOG2E = math.log2(math.e)
SCALE2 = HEAD_DIM ** (-0.5) * LOG2E
F32 = jnp.float32
BF16 = jnp.bfloat16
NT = (((1,), (1,)), ((), ()))
TN = (((0,), (0,)), ((), ()))


def dot(a, b, dims=(((1,), (0,)), ((), ()))):
    return lax.dot_general(a, b, dims, preferred_element_type=F32)


def turn(x, cosine, sine):
    lane = lax.broadcasted_iota(jnp.int32, x.shape, 1) % HEAD_DIM
    other = jnp.where(
        lane < ROT // 2, pltpu.roll(x, 128 - ROT // 2, 1), pltpu.roll(x, ROT // 2, 1)
    )
    return x * cosine + other * sine


def head_masks(x):
    low = lax.broadcasted_iota(jnp.int32, x.shape, 1) < HEAD_DIM
    zero = jnp.zeros_like(x)
    return (jnp.where(low, x, zero), jnp.where(low, zero, x))


def key_range(block):
    first = max(0, block - DOC_MOST // BQ)
    return first * BQ, (block + 1) * BQ


def masked_scores(keys, query, first, block, low_row):
    score = dot(keys, query, NT) * SCALE2
    index = first + lax.broadcasted_iota(jnp.int32, score.shape, 0)
    column = block * BQ + lax.broadcasted_iota(jnp.int32, score.shape, 1)
    allowed = (index >= low_row) & (index <= column)
    return score, allowed


def attn_fwd_body(before, q_in, k_in, v_in, bias, cosine, sine, low, valid, *rest):
    if before:
        old_k, old_v, q_out, k_out, v_out, o_out, lse_out, k_all, vt_all = rest
    else:
        q_out, k_out, v_out, o_out, lse_out, k_all, vt_all = rest
    count = q_in.shape[0]
    cos_t, sin_t = cosine[...], sine[...]
    query = turn(q_in[...] + bias[0:1], cos_t, sin_t).astype(BF16)
    key = turn(k_in[...] + bias[1:2], cos_t, sin_t).astype(BF16)
    value = (v_in[...] + bias[2:3]).astype(BF16)
    q_out[...] = query
    k_out[...] = key
    v_out[...] = value
    if before:
        k_all[:before] = old_k[...]
        vt_all[:, :before] = old_v[...].T
    k_all[before:] = key
    vt_all[:, before:] = value.T
    for local in range(count // BQ):
        block = before // BQ + local
        first, last = key_range(block)
        span = slice(local * BQ, (local + 1) * BQ)
        low_row = low[:, span]
        outs = []
        for head, part in enumerate(head_masks(q_out[span])):
            score, allowed = masked_scores(k_all[first:last], part, first, block, low_row)
            score = jnp.where(allowed, score, -1e30)
            top = jnp.max(score, axis=0, keepdims=True)
            expo = jnp.exp2(score - top)
            total = jnp.sum(expo, axis=0, keepdims=True)
            prob = (expo * (1.0 / total)).astype(BF16)
            outs.append(dot(vt_all[:, first:last], prob))
            lse_out[0, head : head + 1, span] = top + jnp.log2(total)
        upper = lax.broadcasted_iota(jnp.int32, outs[0].shape, 0) < HEAD_DIM
        joined = jnp.where(upper, outs[0], outs[1]) * valid[:, span]
        o_out[span] = joined.T.astype(BF16)


def attn_fwd(qkv, bias, cosine, sine, low, valid, old):
    count, local = qkv[0].shape
    before = 0 if old is None else old[0].shape[0]
    pairs = local // 128
    row = lambda n: pl.BlockSpec((n, 128), lambda i: (0, i))
    whole = lambda a: pl.BlockSpec(a.shape, lambda i: (0,) * a.ndim)
    args = list(qkv) + [bias, cosine, sine, low, valid] + ([] if old is None else list(old))
    specs = [row(count)] * 3 + [row(3), whole(cosine), whole(sine), whole(low), whole(valid)]
    specs += [row(before)] * (0 if old is None else 2)
    flat = jax.ShapeDtypeStruct((count, local), BF16)
    return pl.pallas_call(
        functools.partial(attn_fwd_body, before),
        grid=(pairs,),
        in_specs=specs,
        out_specs=[row(count)] * 4 + [pl.BlockSpec((1, 2, count), lambda i: (i, 0, 0))],
        out_shape=[flat] * 4 + [jax.ShapeDtypeStruct((pairs, 2, count), F32)],
        scratch_shapes=[
            pltpu.VMEM((before + count, 128), BF16),
            pltpu.VMEM((128, before + count), BF16),
        ],
        cost_estimate=pl.CostEstimate(
            flops=8 * count * 768 * local, bytes_accessed=20 * count * local, transcendentals=0
        ),
        name="attn_fwd",
    )(*args)


def attn_bwd_body(parts, *refs):
    qs, ks, vs = refs[:parts], refs[parts : 2 * parts], refs[2 * parts : 3 * parts]
    lses = refs[3 * parts : 4 * parts]
    do_in, cosine, sine, low, dq_out, dk_out, dv_out, bias_out, kt_all, dk_acc, dv_acc = refs[
        4 * parts :
    ]
    each = qs[0].shape[0]

    def rows(refs_of, first, last):
        pieces = []
        for part, ref in enumerate(refs_of):
            lo, hi = max(first, part * each), min(last, (part + 1) * each)
            if lo < hi:
                pieces.append(ref[lo - part * each : hi - part * each])
        return pieces[0] if len(pieces) == 1 else jnp.concatenate(pieces, axis=0)

    for part in range(parts):
        kt_all[:, part * each : (part + 1) * each] = ks[part][...].T
    dk_acc[...] = jnp.zeros_like(dk_acc)
    dv_acc[...] = jnp.zeros_like(dv_acc)
    sums = [jnp.zeros((1, 128), F32) for _ in range(3)]
    blocks = parts * each // BQ
    for block in range(blocks):
        first, last = key_range(block)
        span = slice(block * BQ, (block + 1) * BQ)
        low_row = low[:, span]
        part, inside = block * BQ // each, block * BQ % each
        queries = head_masks(rows(qs, span.start, span.stop))
        d_outs = head_masks(do_in[span])
        keys, values = rows(ks, first, last), rows(vs, first, last)
        probs, d_scores, d_queries = [], [], []
        for head in range(2):
            score, allowed = masked_scores(keys, queries[head], first, block, low_row)
            lse = lses[part][0, head : head + 1, inside : inside + BQ]
            prob = jnp.where(allowed, jnp.exp2(score - lse), 0.0)
            d_prob = dot(values, d_outs[head], NT)
            delta = jnp.sum(prob * d_prob, axis=0, keepdims=True)
            d_score = (prob * (d_prob - delta)).astype(BF16)
            probs.append(prob.astype(BF16))
            d_scores.append(d_score)
            d_queries.append(dot(kt_all[:, first:last], d_score))
        wide = slice(first, last)
        dv_acc[wide] += dot(jnp.concatenate(probs, 1), jnp.concatenate(d_outs, 0))
        dk_acc[wide] += dot(jnp.concatenate(d_scores, 1), jnp.concatenate(queries, 0))
        upper = lax.broadcasted_iota(jnp.int32, d_queries[0].shape, 0) < HEAD_DIM
        d_query = jnp.where(upper, d_queries[0], d_queries[1]).T * HEAD_DIM ** (-0.5)
        d_query = turn(d_query, cosine[span], -sine[span]).astype(BF16)
        dq_out[span] = d_query
        sums[0] += jnp.sum(d_query.astype(F32), axis=0, keepdims=True)
        done = [block - DOC_MOST // BQ] if block + 1 < blocks else range(block - DOC_MOST // BQ, blocks)
        for old in done:
            if old < 0:
                continue
            there = slice(old * BQ, (old + 1) * BQ)
            d_key = dk_acc[there] * HEAD_DIM ** (-0.5)
            d_key = turn(d_key, cosine[there], -sine[there]).astype(BF16)
            d_value = dv_acc[there].astype(BF16)
            dk_out[there] = d_key
            dv_out[there] = d_value
            sums[1] += jnp.sum(d_key.astype(F32), axis=0, keepdims=True)
            sums[2] += jnp.sum(d_value.astype(F32), axis=0, keepdims=True)
    bias_out[...] = jnp.concatenate(sums, axis=0)


def attn_bwd(qs, ks, vs, lses, d_out, cosine, sine, low):
    parts = len(qs)
    each, local = qs[0].shape
    count = parts * each
    row = lambda n: pl.BlockSpec((n, 128), lambda i: (0, i))
    whole = lambda a: pl.BlockSpec(a.shape, lambda i: (0,) * a.ndim)
    flat = jax.ShapeDtypeStruct((count, local), BF16)
    return pl.pallas_call(
        functools.partial(attn_bwd_body, parts),
        grid=(local // 128,),
        in_specs=[row(each)] * (3 * parts)
        + [pl.BlockSpec((1, 2, each), lambda i: (i, 0, 0))] * parts
        + [row(count), whole(cosine), whole(sine), whole(low)],
        out_specs=[row(count)] * 3 + [row(3)],
        out_shape=[flat] * 3 + [jax.ShapeDtypeStruct((3, local), F32)],
        scratch_shapes=[
            pltpu.VMEM((128, count), BF16),
            pltpu.VMEM((count, 128), F32),
            pltpu.VMEM((count, 128), F32),
        ],
        cost_estimate=pl.CostEstimate(
            flops=20 * count * 768 * local, bytes_accessed=20 * count * local, transcendentals=0
        ),
        name="attn_bwd",
    )(*qs, *ks, *vs, *lses, d_out, cosine, sine, low)


def mlp_body(x_in, dy_in, w_in, down_in, h_out, dg_out, du_out):
    for start in range(0, x_in.shape[0], 256):
        span = slice(start, start + 256)
        gate = dot(x_in[span], w_in[0])
        upper = dot(x_in[span], w_in[1])
        d_hidden = dot(dy_in[span], down_in[...], NT)
        sigma = jax.nn.sigmoid(gate)
        active = gate * sigma
        h_out[span] = (active * upper).astype(BF16)
        du_out[span] = (d_hidden * active).astype(BF16)
        dg_out[span] = (d_hidden * upper * sigma * (1.0 + gate * (1.0 - sigma))).astype(BF16)


def mlp(normed, y_grad, weight, down, part, parts):
    count, width = normed.shape
    rows = count // parts
    hidden = down.shape[0]
    step = min(256, hidden)
    fixed = pl.BlockSpec((rows, width), lambda i: (part, 0))
    return pl.pallas_call(
        mlp_body,
        grid=(pl.cdiv(hidden, step),),
        in_specs=[
            fixed,
            fixed,
            pl.BlockSpec((2, width, step), lambda i: (0, 0, i)),
            pl.BlockSpec((step, width), lambda i: (i, 0)),
        ],
        out_specs=[pl.BlockSpec((rows, step), lambda i: (0, i))] * 3,
        out_shape=[jax.ShapeDtypeStruct((rows, hidden), BF16)] * 3,
        cost_estimate=pl.CostEstimate(
            flops=6 * rows * width * hidden, bytes_accessed=6 * width * hidden, transcendentals=0
        ),
        name="mlp",
    )(normed, y_grad, weight, down)


def out_body(o_in, h_in, wo_in, wd_in, out):
    out[...] = (dot(o_in[...], wo_in[...]) + dot(h_in[...], wd_in[...])).astype(BF16)


def out_partial(o, h, out_weight, down, start, cols):
    rows, local = o.shape
    hidden = h.shape[1]
    step = min(512, cols)
    base = start // step
    return pl.pallas_call(
        out_body,
        grid=(cols // step,),
        in_specs=[
            pl.BlockSpec((rows, local), lambda i: (0, 0)),
            pl.BlockSpec((rows, hidden), lambda i: (0, 0)),
            pl.BlockSpec((local, step), lambda i: (0, base + i)),
            pl.BlockSpec((hidden, step), lambda i: (0, base + i)),
        ],
        out_specs=pl.BlockSpec((rows, step), lambda i: (0, i)),
        out_shape=jax.ShapeDtypeStruct((rows, cols), BF16),
        cost_estimate=pl.CostEstimate(
            flops=2 * rows * cols * (local + hidden),
            bytes_accessed=2 * (rows + cols) * (local + hidden),
            transcendentals=0,
        ),
        name="out_partial",
    )(o, h, out_weight, down)


def dxn_body(parts, bounds, *refs):
    dq_in, dk_in, dv_in = refs[:3]
    dgs, dus = refs[3 : 3 + parts], refs[3 + parts : 3 + 2 * parts]
    wqkv_in, w_in, x_in, mean_in, inv_in, gain_in, *outs, col_out, r1_out, r2_out = refs[
        3 + 2 * parts :
    ]
    step = pl.program_id(0)
    count = x_in.shape[0]
    each = count // parts
    first = pl.program_id(0) == 0
    gain = gain_in[...]
    shift_sum = jnp.zeros(gain.shape, F32)
    gain_sum = jnp.zeros(gain.shape, F32)
    for start in range(0, count, 256):
        span = slice(start, start + 256)
        part = start // each
        inside = slice(start - part * each, start - part * each + 256)
        total = dot(dq_in[span], wqkv_in[0], NT)
        total += dot(dk_in[span], wqkv_in[1], NT)
        total += dot(dv_in[span], wqkv_in[2], NT)
        total += dot(dgs[part][inside], w_in[0], NT)
        total += dot(dus[part][inside], w_in[1], NT)
        for out, (low, high) in zip(outs, bounds):

            @pl.when((step >= low) & (step < high))
            def _(out=out, span=span, total=total):
                out[span] = total.astype(BF16)

        hat = (x_in[span].astype(F32) - mean_in[span]) * inv_in[span]
        product = total * hat
        shift_sum += jnp.sum(total, axis=0, keepdims=True)
        gain_sum += jnp.sum(product, axis=0, keepdims=True)
        row1 = jnp.sum(total * gain, axis=1, keepdims=True)
        row2 = jnp.sum(product * gain, axis=1, keepdims=True)
        r1_out[span] = row1 + jnp.where(first, 0.0, r1_out[span])
        r2_out[span] = row2 + jnp.where(first, 0.0, r2_out[span])
    col_out[...] = jnp.concatenate([gain_sum, shift_sum], axis=0)


def dxn_partial(dqkv, dgs, dus, wqkv, weight, x, mean, inv, gain, start, widths):
    parts = len(dgs)
    cols = sum(widths)
    count = x.shape[0]
    local, hidden = dqkv[0].shape[1], dgs[0].shape[1]
    each = count // parts
    step = 256
    base = start // step
    ends = np.cumsum([w // step for w in widths])
    bounds = [(int(e) - w // step, int(e)) for e, w in zip(ends, widths)]
    whole = lambda a: pl.BlockSpec(a.shape, lambda i: (0,) * a.ndim)
    return pl.pallas_call(
        functools.partial(dxn_body, parts, bounds),
        grid=(cols // step,),
        in_specs=[whole(a) for a in (*dqkv, *dgs, *dus)]
        + [
            pl.BlockSpec((3, step, local), lambda i: (0, base + i, 0)),
            pl.BlockSpec((2, step, hidden), lambda i: (0, base + i, 0)),
            pl.BlockSpec((count, step), lambda i: (0, base + i)),
            whole(mean),
            whole(inv),
            pl.BlockSpec((1, step), lambda i: (0, base + i)),
        ],
        out_specs=[
            pl.BlockSpec((count, step), lambda i, b=b: (0, jnp.clip(i - b[0], 0, b[1] - b[0] - 1)))
            for b in bounds
        ]
        + [
            pl.BlockSpec((2, step), lambda i: (0, i)),
            pl.BlockSpec((count, 1), lambda i: (0, 0)),
            pl.BlockSpec((count, 1), lambda i: (0, 0)),
        ],
        out_shape=[
            *(jax.ShapeDtypeStruct((count, w), BF16) for w in widths),
            jax.ShapeDtypeStruct((2, cols), F32),
            jax.ShapeDtypeStruct((count, 1), F32),
            jax.ShapeDtypeStruct((count, 1), F32),
        ],
        cost_estimate=pl.CostEstimate(
            flops=2 * count * cols * (3 * local + 2 * hidden),
            bytes_accessed=2 * (count + cols) * (3 * local + 2 * hidden),
            transcendentals=0,
        ),
        name="dxn_partial",
    )(*dqkv, *dgs, *dus, wqkv, weight, x, mean, inv, gain)


def dw_sum(groups, lhs, rhs):
    position = 0
    for parts in groups:
        each = lhs.shape[0] // parts
        total = None
        for part in range(parts):
            piece = dot(lhs[part * each : (part + 1) * each], rhs[position][...], TN)
            total = piece if total is None else total + piece
            position += 1
        yield total


def dw_send_body(groups, order, lhs, *refs):
    rhs, outs = refs[: sum(groups)], refs[sum(groups) :]
    for total, out in zip(dw_sum(groups, lhs, rhs), outs):
        out[0] = total.astype(BF16)


def dw_keep_body(groups, order, slots, lhs, *refs):
    rhs, refs = refs[: sum(groups)], refs[sum(groups) :]
    number = len(groups)
    received, sends, keeps = refs[:number], refs[number : 2 * number], refs[2 * number :]
    step = pl.program_id(0)
    for group, total in enumerate(dw_sum(groups, lhs, rhs)):
        total = (total + received[group][0].astype(F32)).astype(BF16)
        away = slots[3 * group, step] == 1

        @pl.when(away)
        def _(group=group, total=total):
            sends[group][0] = total

        @pl.when(jnp.logical_not(away))
        def _(group=group, total=total):
            keeps[group][0] = total


def dw_call(order, lhs, rhs, number, received=None, slots=None):
    count, width = lhs.shape
    step = width // (2 * number)
    groups = tuple(len(group) for group in rhs)
    flat = [part for group in rhs for part in group]
    columns = [group[0].shape[1] for group in rhs]
    scalars = [order] if slots is None else [order, slots]
    args = scalars + [lhs, *flat]
    specs = [pl.BlockSpec((count, step), lambda i, order, *_: (0, order[i]))]
    specs += [pl.BlockSpec(a.shape, lambda i, *_: (0, 0)) for a in flat]
    if received is None:
        body = functools.partial(dw_send_body, groups)
        out_specs = [pl.BlockSpec((1, step, c), lambda i, *_: (i, 0, 0)) for c in columns]
        shapes = [jax.ShapeDtypeStruct((number, step, c), BF16) for c in columns]
    else:
        body = functools.partial(dw_keep_body, groups)
        args += received
        specs += [pl.BlockSpec((1, step, c), lambda i, *_: (i, 0, 0)) for c in columns]
        out_specs = [
            pl.BlockSpec((1, step, c), lambda i, order, slots, r=3 * g + kind: (slots[r, i], 0, 0))
            for kind in (1, 2)
            for g, c in enumerate(columns)
        ]
        shapes = [jax.ShapeDtypeStruct((number // 2, step, c), BF16) for c in columns] * 2
    total = number * step * sum(columns)
    return pl.pallas_call(
        body,
        grid_spec=pltpu.PrefetchScalarGridSpec(
            num_scalar_prefetch=len(scalars), grid=(number,), in_specs=specs, out_specs=out_specs
        ),
        out_shape=shapes,
        cost_estimate=pl.CostEstimate(
            flops=2 * count * total, bytes_accessed=2 * (count * sum(columns) + total), transcendentals=0
        ),
        name="weight_grad",
    )(*args)


def flip(size, bit):
    return [(i, i ^ bit) for i in range(size)]


class Order:
    def __init__(self):
        self.token = None

    def __call__(self, function, *args):
        if self.token is not None:
            args, _ = lax.optimization_barrier((args, self.token))
        out = function(*args)
        self.token = jax.tree.leaves(out)[0]
        return out


def halving_order(bits):
    order = [0]
    for bit in reversed(bits):
        order = [offset ^ bit for offset in order] + order
    return order


class Scatter:
    def __init__(self, run, devices, lhs, rhs, swaps):
        self.run, self.devices, self.lhs, self.rhs = run, devices, lhs, rhs
        bits = [1 << i for i in range(devices.bit_length() - 1)]
        self.offsets = halving_order(bits)
        self.order = lax.axis_index("dp").astype(jnp.int32) ^ jnp.asarray(self.offsets, jnp.int32)
        self.bits = []
        for swap in swaps:
            rest = bits[1:]
            if swap and len(rest) > 1:
                rest[0], rest[1] = rest[1], rest[0]
            self.bits.append(rest)

    def send(self):
        half = self.devices // 2
        call = lambda lhs, rhs: dw_call(self.order[:half], lhs, rhs, half)
        sent = self.run(call, self.lhs, self.rhs)
        self.received = [lax.ppermute(s, "dp", flip(self.devices, 1)) for s in sent]

    def keep(self):
        half = self.devices // 2
        kept = self.offsets[half:]
        rows, self.left = [], []
        for bits in self.bits:
            away = [int(offset & bits[0] != 0) for offset in kept]
            place = lambda flags: [max(0, sum(flags[: i + 1]) - 1) for i in range(half)]
            rows += [away, place(away), place([1 - a for a in away])]
            self.left.append([offset for offset in kept if not offset & bits[0]])
        slots = jnp.asarray(np.array(rows), jnp.int32)
        call = lambda lhs, rhs, received: dw_call(self.order[half:], lhs, rhs, half, received, slots)
        outs = self.run(call, self.lhs, self.rhs, self.received)
        number = len(self.bits)
        self.kept = outs[number:]
        self.received = [
            lax.ppermute(s, "dp", flip(self.devices, bits[0])) for s, bits in zip(outs, self.bits)
        ]
        self.stage = 1

    def next(self):
        def step(kept, received):
            sends, keeps = [], []
            for group, bits in enumerate(self.bits):
                bit = bits[self.stage]
                for away, stack in ((True, sends), (False, keeps)):
                    where = [i for i, o in enumerate(self.left[group]) if bool(o & bit) == away]
                    pick = lambda a: jnp.stack([a[i] for i in where]).astype(F32)
                    stack.append((pick(kept[group]) + pick(received[group])).astype(BF16))
            return sends, keeps

        sends, self.kept = self.run(step, self.kept, self.received)
        self.received = []
        for group, bits in enumerate(self.bits):
            bit = bits[self.stage]
            self.left[group] = [o for o in self.left[group] if not o & bit]
            self.received.append(lax.ppermute(sends[group], "dp", flip(self.devices, bit)))
        self.stage += 1

    def last(self, shape=lambda a: a):
        while self.stage < len(self.bits[0]):
            self.next()
        add = lambda kept, received: shape(
            [k[0].astype(F32) + r[0].astype(F32) for k, r in zip(kept, received)]
        )
        return self.run(add, self.kept, self.received)


LINE = 4


class Line:
    def __init__(self, run, size, partial, finish, corner):
        self.run, self.size, self.partial, self.finish, self.corner = run, size, partial, finish, corner
        lines = range(0, size, LINE)
        inward = [(b, b + 1) for b in lines] + [(b + 3, b + 2) for b in lines]
        self.across = [(b + 1, b + 2) for b in lines] + [(b + 2, b + 1) for b in lines]
        self.outward = [(b + 1, b) for b in lines] + [(b + 2, b + 3) for b in lines]
        self.received = lax.ppermute(partial, "mp", inward)

    def mid(self):
        add = lambda a, b: (a.astype(F32) + b.astype(F32)).astype(BF16)
        self.total = self.run(add, self.partial, self.received)
        self.received = lax.ppermute(self.total, "mp", self.across)

    def back(self):
        def step(total, received):
            total = total.astype(F32) + received.astype(F32)
            bit = LINE
            while bit < self.size:
                total = total.astype(BF16)
                pairs = [(i, i ^ bit) for i in range(self.size) if i % LINE in (1, 2)]
                total = total.astype(F32) + lax.ppermute(total, "mp", pairs).astype(F32)
                bit *= 2
            return self.finish(total)

        self.mine = self.run(step, self.total, self.received)
        self.received = lax.ppermute(self.mine, "mp", self.outward)

    def store(self, target):
        place = lax.axis_index("mp") % LINE
        inner = (place == 1) | (place == 2)
        step = lambda target, mine, received: lax.dynamic_update_slice(
            target, jnp.where(inner, mine, received), self.corner
        )
        return self.run(step, target, self.mine, self.received)


def small_sum(value, axis, size):
    bit = 1
    while bit < size:
        value = value + lax.ppermute(value, axis, flip(size, bit))
        bit *= 2
    return value


def shards(
    dp,
    mp,
    inputs,
    segment_ids,
    pad_count,
    layer_norm_gain,
    layer_norm_bias,
    qkv_weight,
    qkv_bias,
    out_weight,
    gateup_weight,
    down_weight,
    y_grad,
):
    count, width = inputs.shape
    local = qkv_weight.shape[2]
    parts = 2
    rows = count // parts

    seg = segment_ids[0]
    steps = jnp.arange(count, dtype=jnp.int32)
    start = jnp.sum((seg[None, :] < seg[:, None]).astype(jnp.int32), axis=1)
    valid = steps < count - pad_count[0]
    low = jnp.where(valid, start, steps)[None, :]
    valid_row = valid.astype(F32)[None, :]
    lane = jnp.arange(128, dtype=jnp.int32) % HEAD_DIM
    half = ROT // 2
    freq = jnp.power(10000.0, -2.0 * (lane % half).astype(F32) / ROT)
    freq = jnp.where(lane < ROT, freq, 0.0)
    angle = (steps - start).astype(F32)[:, None] * freq[None, :]
    sign = jnp.where(lane < half, -1.0, 1.0)
    cosine = jnp.cos(angle)
    sine = jnp.sin(angle) * sign[None, :]

    xf = inputs.astype(F32)
    mean = jnp.mean(xf, axis=-1, keepdims=True)
    removed = xf - mean
    inv = lax.rsqrt(jnp.mean(removed * removed, axis=-1, keepdims=True) + EPS)
    normed = (removed * inv * layer_norm_gain + layer_norm_bias).astype(BF16)

    wqkv = jnp.transpose(qkv_weight, (1, 0, 2))
    weight = jnp.transpose(gateup_weight, (1, 0, 2))

    run = Order()
    old = None
    qs, ks, vs, os, lses, hs, dgs, dus = ([] for _ in range(8))
    firsts = []
    for part in range(parts):
        span = slice(part * rows, (part + 1) * rows)

        def attend(normed, old, span=span):
            xs = normed[span]
            qkv = [jnp.dot(xs, wqkv[j], preferred_element_type=F32) for j in range(3)]
            return attn_fwd(
                qkv, qkv_bias, cosine[span], sine[span], low[:, span], valid_row[:, span], old
            )

        q, k, v, o, lse = run(attend, normed, old)
        old = (k, v)
        h, dg, du = run(
            lambda *a, part=part: mlp(*a, part, parts), normed, y_grad, weight, down_weight
        )
        for stack, item in zip((qs, ks, vs, os, lses, hs, dgs, dus), (q, k, v, o, lse, h, dg, du)):
            stack.append(item)
        partial = run(lambda *a: out_partial(*a, 0, width), o, h, out_weight, down_weight)
        x_here = inputs[span].astype(F32)
        finish = lambda total, x_here=x_here: (x_here + total).astype(BF16)
        firsts.append(Line(run, mp, partial, finish, (part * rows, 0)))
    result = jnp.zeros((count, width), BF16)
    x_grad = jnp.zeros((count, width), BF16)

    gateup = Scatter(run, dp, normed, [dgs, dus], (False, True))
    down = Scatter(run, dp, y_grad, [hs], (True,))
    outer = Scatter(run, dp, y_grad, [os], (True,))

    firsts[0].mid()
    gateup.send()

    def cotangent(y_grad, out_weight):
        d_attn = lax.dot_general(y_grad, out_weight, NT, preferred_element_type=F32).astype(BF16)
        return d_attn * valid.astype(BF16)[:, None]

    d_attn = run(cotangent, y_grad, out_weight)
    gateup.keep()
    *dqkv, bias_grad = run(
        lambda *a: attn_bwd(*a, cosine, sine, low), qs, ks, vs, lses, d_attn
    )
    inner = Scatter(run, dp, normed, [[a] for a in dqkv], (False, False, False))

    gain_row = layer_norm_gain[None, :]
    averages = []
    seconds = []
    sums = []

    def finish(total, span):
        average, slope = averages[0]
        hat = (inputs[:, span].astype(F32) - mean) * inv
        inner = total * layer_norm_gain[span] - average - hat * slope
        return (y_grad[:, span].astype(F32) + inv * inner).astype(BF16)

    def emit(start, widths):
        call = lambda dqkv, dgs, dus: dxn_partial(
            dqkv, dgs, dus, wqkv, weight, inputs, mean, inv, gain_row, start, widths
        )
        *chunks, column, row1, row2 = run(call, dqkv, dgs, dus)
        sums.append((column, row1, row2))
        for chunk, cols in zip(chunks, widths):
            span = slice(start, start + cols)
            seconds.append(
                Line(run, mp, chunk, functools.partial(finish, span=span), (0, start))
            )
            start += cols

    emit(0, (512, 512))
    firsts[1].mid()
    firsts[0].back()
    emit(1024, (512, 512))

    def gather(sums):
        columns = jnp.concatenate([c[0] for c in sums], axis=1)
        row1 = sum(c[1] for c in sums).reshape(count)
        row2 = sum(c[2] for c in sums).reshape(count)
        return jnp.concatenate([row1, row2, columns.reshape(2 * width)])

    small = small_sum(run(gather, sums), "mp", mp)
    gateup.next()
    down.send()
    average = (small[:count] / width).reshape(count, 1)
    slope = (small[count : 2 * count] / width).reshape(count, 1)
    averages.append((average, slope))
    small = jnp.concatenate([small[2 * count :], bias_grad.reshape(-1)])
    seconds[0].mid()
    outer.send()
    down.keep()
    outer.keep()
    seconds[1].mid()
    firsts[1].back()
    result = firsts[0].store(result)
    inner.send()
    seconds[0].back()
    inner.keep()
    seconds[2].mid()
    flat = lambda a: jnp.transpose(a[0])
    gateup_grad = gateup.last(lambda a: jnp.stack(a, axis=1))
    down.next()
    seconds[1].back()
    outer.next()
    x_grad = seconds[0].store(x_grad)
    result = firsts[1].store(result)
    seconds[3].mid()
    inner.next()
    small = small_sum(small, "dp", dp)
    column_sums = small[: 2 * width].reshape(2, width)
    bias_sum = small[2 * width :].reshape(bias_grad.shape)
    down_grad = down.last(flat)
    seconds[2].back()
    x_grad = seconds[1].store(x_grad)
    out_grad = outer.last(flat)
    qkv_grad = inner.last(lambda a: jnp.transpose(jnp.stack(a), (1, 0, 2)))
    seconds[3].back()
    x_grad = seconds[2].store(x_grad)
    x_grad = seconds[3].store(x_grad)
    return (
        result,
        x_grad,
        column_sums[0],
        column_sums[1],
        qkv_grad,
        bias_sum,
        out_grad,
        gateup_grad,
        down_grad,
    )


def solution(mesh):
    placed = (
        P("dp", None),
        P("dp", None),
        P("dp"),
        P(),
        P(),
        P(None, None, "mp"),
        P(None, "mp"),
        P("mp", None),
        P(None, None, "mp"),
        P("mp", None),
        P("dp", None),
    )
    return jax.shard_map(
        functools.partial(shards, mesh.shape["dp"], mesh.shape["mp"]),
        mesh=mesh,
        in_specs=placed,
        out_specs=(
            P("dp", None),
            P("dp", None),
            P(),
            P(),
            P("dp", None, "mp"),
            P(None, "mp"),
            P("mp", "dp"),
            P("dp", None, "mp"),
            P("mp", "dp"),
        ),
        check_vma=False,
    )
```

```python
import functools
import math

import jax
import jax.numpy as jnp
import numpy as np
from jax import lax
from jax.experimental import pallas as pl
from jax.experimental.pallas import tpu as pltpu
from jax.sharding import PartitionSpec as P

HEAD_DIM = 64
ROT = 16
DOCS = 4
DOC_MOST = 512
EPS = 1e-05
BQ = 256
LOG2E = math.log2(math.e)
SCALE2 = HEAD_DIM ** (-0.5) * LOG2E
F32 = jnp.float32
BF16 = jnp.bfloat16
NT = (((1,), (1,)), ((), ()))
TN = (((0,), (0,)), ((), ()))
COST = pl.CostEstimate(flops=1000, bytes_accessed=1000, transcendentals=0)


def dot(a, b, dims=(((1,), (0,)), ((), ()))):
    return lax.dot_general(a, b, dims, preferred_element_type=F32)


def turn(x, cosine, sine):
    lane = lax.broadcasted_iota(jnp.int32, x.shape, 1) % HEAD_DIM
    other = jnp.where(
        lane < ROT // 2, pltpu.roll(x, 128 - ROT // 2, 1), pltpu.roll(x, ROT // 2, 1)
    )
    return x * cosine + other * sine


def head_masks(x):
    low = lax.broadcasted_iota(jnp.int32, x.shape, 1) < HEAD_DIM
    zero = jnp.zeros_like(x)
    return (jnp.where(low, x, zero), jnp.where(low, zero, x))


def key_range(block):
    first = max(0, block - DOC_MOST // BQ)
    return first * BQ, (block + 1) * BQ


def masked_scores(keys, query, first, block, low_row):
    score = dot(keys, query, NT) * SCALE2
    index = first + lax.broadcasted_iota(jnp.int32, score.shape, 0)
    column = block * BQ + lax.broadcasted_iota(jnp.int32, score.shape, 1)
    allowed = (index >= low_row) & (index <= column)
    return score, allowed


def attn_fwd_body(before, x_in, w_in, bias, cosine, sine, low, valid, *rest):
    if before:
        old_k, old_v, q_out, k_out, v_out, o_out, lse_out, k_all, vt_all = rest
    else:
        q_out, k_out, v_out, o_out, lse_out, k_all, vt_all = rest
    count = x_in.shape[0]
    qkv = dot(x_in[...], jnp.concatenate([w_in[0], w_in[1], w_in[2]], axis=1))
    cos_t, sin_t = cosine[...], sine[...]
    query = turn(qkv[:, :128] + bias[0:1], cos_t, sin_t).astype(BF16)
    key = turn(qkv[:, 128:256] + bias[1:2], cos_t, sin_t).astype(BF16)
    value = (qkv[:, 256:] + bias[2:3]).astype(BF16)
    q_out[...] = query
    k_out[...] = key
    v_out[...] = value
    if before:
        k_all[:before] = old_k[...]
        vt_all[:, :before] = old_v[...].T
    k_all[before:] = key
    vt_all[:, before:] = value.T
    for local in range(count // BQ):
        block = before // BQ + local
        first, last = key_range(block)
        span = slice(local * BQ, (local + 1) * BQ)
        low_row = low[:, span]
        outs = []
        for head, part in enumerate(head_masks(q_out[span])):
            score, allowed = masked_scores(k_all[first:last], part, first, block, low_row)
            score = jnp.where(allowed, score, -1e30)
            top = jnp.max(score, axis=0, keepdims=True)
            expo = jnp.exp2(score - top)
            total = jnp.sum(expo, axis=0, keepdims=True)
            prob = (expo * (1.0 / total)).astype(BF16)
            outs.append(dot(vt_all[:, first:last], prob))
            lse_out[0, head : head + 1, span] = top + jnp.log2(total)
        upper = lax.broadcasted_iota(jnp.int32, outs[0].shape, 0) < HEAD_DIM
        joined = jnp.where(upper, outs[0], outs[1]) * valid[:, span]
        o_out[span] = joined.T.astype(BF16)


def attn_fwd(normed, weight, bias, cosine, sine, low, valid, old, part):
    width, local = weight.shape[1:]
    count = cosine.shape[0]
    before = 0 if old is None else old[0].shape[0]
    pairs = local // 128
    row = lambda n: pl.BlockSpec((n, 128), lambda i: (0, i))
    whole = lambda a: pl.BlockSpec(a.shape, lambda i: (0,) * a.ndim)
    args = [normed, weight, bias, cosine, sine, low, valid] + ([] if old is None else list(old))
    specs = [
        pl.BlockSpec((count, width), lambda i: (part, 0)),
        pl.BlockSpec((3, width, 128), lambda i: (0, 0, i)),
        row(3),
        *map(whole, (cosine, sine, low, valid)),
    ]
    specs += [row(before)] * (0 if old is None else 2)
    flat = jax.ShapeDtypeStruct((count, local), BF16)
    return pl.pallas_call(
        functools.partial(attn_fwd_body, before),
        grid=(pairs,),
        in_specs=specs,
        out_specs=[row(count)] * 4 + [pl.BlockSpec((1, 2, count), lambda i: (i, 0, 0))],
        out_shape=[flat] * 4 + [jax.ShapeDtypeStruct((pairs, 2, count), F32)],
        scratch_shapes=[
            pltpu.VMEM((before + count, 128), BF16),
            pltpu.VMEM((128, before + count), BF16),
        ],
        cost_estimate=COST,
        name="attn_fwd",
    )(*args)


def attn_bwd_body(parts, *refs):
    qs, ks, vs = refs[:parts], refs[parts : 2 * parts], refs[2 * parts : 3 * parts]
    lses = refs[3 * parts : 4 * parts]
    do_in, cosine, sine, low, dq_out, dk_out, dv_out, bias_out, kt_all, dk_acc, dv_acc = refs[
        4 * parts :
    ]
    each = qs[0].shape[0]

    def rows(refs_of, first, last):
        pieces = []
        for part, ref in enumerate(refs_of):
            lo, hi = max(first, part * each), min(last, (part + 1) * each)
            if lo < hi:
                pieces.append(ref[lo - part * each : hi - part * each])
        return pieces[0] if len(pieces) == 1 else jnp.concatenate(pieces, axis=0)

    for part in range(parts):
        kt_all[:, part * each : (part + 1) * each] = ks[part][...].T
    dk_acc[...] = jnp.zeros_like(dk_acc)
    dv_acc[...] = jnp.zeros_like(dv_acc)
    sums = [jnp.zeros((1, 128), F32) for _ in range(3)]
    blocks = parts * each // BQ
    for block in range(blocks):
        first, last = key_range(block)
        span = slice(block * BQ, (block + 1) * BQ)
        low_row = low[:, span]
        part, inside = block * BQ // each, block * BQ % each
        queries = head_masks(rows(qs, span.start, span.stop))
        d_outs = head_masks(do_in[span])
        keys, values = rows(ks, first, last), rows(vs, first, last)
        probs, d_scores, d_queries = [], [], []
        for head in range(2):
            score, allowed = masked_scores(keys, queries[head], first, block, low_row)
            lse = lses[part][0, head : head + 1, inside : inside + BQ]
            prob = jnp.where(allowed, jnp.exp2(score - lse), 0.0)
            d_prob = dot(values, d_outs[head], NT)
            delta = jnp.sum(prob * d_prob, axis=0, keepdims=True)
            d_score = (prob * (d_prob - delta)).astype(BF16)
            probs.append(prob.astype(BF16))
            d_scores.append(d_score)
            d_queries.append(dot(kt_all[:, first:last], d_score))
        wide = slice(first, last)
        dv_acc[wide] += dot(jnp.concatenate(probs, 1), jnp.concatenate(d_outs, 0))
        dk_acc[wide] += dot(jnp.concatenate(d_scores, 1), jnp.concatenate(queries, 0))
        upper = lax.broadcasted_iota(jnp.int32, d_queries[0].shape, 0) < HEAD_DIM
        d_query = jnp.where(upper, d_queries[0], d_queries[1]).T * HEAD_DIM ** (-0.5)
        d_query = turn(d_query, cosine[span], -sine[span]).astype(BF16)
        dq_out[span] = d_query
        sums[0] += jnp.sum(d_query.astype(F32), axis=0, keepdims=True)
        done = [block - DOC_MOST // BQ] if block + 1 < blocks else range(block - DOC_MOST // BQ, blocks)
        for old in done:
            if old < 0:
                continue
            there = slice(old * BQ, (old + 1) * BQ)
            d_key = dk_acc[there] * HEAD_DIM ** (-0.5)
            d_key = turn(d_key, cosine[there], -sine[there]).astype(BF16)
            d_value = dv_acc[there].astype(BF16)
            dk_out[there] = d_key
            dv_out[there] = d_value
            sums[1] += jnp.sum(d_key.astype(F32), axis=0, keepdims=True)
            sums[2] += jnp.sum(d_value.astype(F32), axis=0, keepdims=True)
    bias_out[...] = jnp.concatenate(sums, axis=0)


def attn_bwd(qs, ks, vs, lses, d_out, cosine, sine, low):
    parts = len(qs)
    each, local = qs[0].shape
    count = parts * each
    row = lambda n: pl.BlockSpec((n, 128), lambda i: (0, i))
    whole = lambda a: pl.BlockSpec(a.shape, lambda i: (0,) * a.ndim)
    flat = jax.ShapeDtypeStruct((count, local), BF16)
    return pl.pallas_call(
        functools.partial(attn_bwd_body, parts),
        grid=(local // 128,),
        in_specs=[row(each)] * (3 * parts)
        + [pl.BlockSpec((1, 2, each), lambda i: (i, 0, 0))] * parts
        + [row(count), whole(cosine), whole(sine), whole(low)],
        out_specs=[row(count)] * 3 + [row(3)],
        out_shape=[flat] * 3 + [jax.ShapeDtypeStruct((3, local), F32)],
        scratch_shapes=[
            pltpu.VMEM((128, count), BF16),
            pltpu.VMEM((count, 128), F32),
            pltpu.VMEM((count, 128), F32),
        ],
        cost_estimate=COST,
        name="attn_bwd",
    )(*qs, *ks, *vs, *lses, d_out, cosine, sine, low)


def mlp_body(x_in, dy_in, w_in, down_in, h_out, dg_out, du_out):
    for start in range(0, x_in.shape[0], 256):
        span = slice(start, start + 256)
        gate = dot(x_in[span], w_in[0])
        upper = dot(x_in[span], w_in[1])
        d_hidden = dot(dy_in[span], down_in[...], NT)
        sigma = jax.nn.sigmoid(gate)
        active = gate * sigma
        h_out[span] = (active * upper).astype(BF16)
        du_out[span] = (d_hidden * active).astype(BF16)
        dg_out[span] = (d_hidden * upper * sigma * (1.0 + gate * (1.0 - sigma))).astype(BF16)


def mlp(normed, y_grad, weight, down, part, parts):
    count, width = normed.shape
    rows = count // parts
    hidden = down.shape[0]
    step = min(256, hidden)
    fixed = pl.BlockSpec((rows, width), lambda i: (part, 0))
    return pl.pallas_call(
        mlp_body,
        grid=(pl.cdiv(hidden, step),),
        in_specs=[
            fixed,
            fixed,
            pl.BlockSpec((2, width, step), lambda i: (0, 0, i)),
            pl.BlockSpec((step, width), lambda i: (i, 0)),
        ],
        out_specs=[pl.BlockSpec((rows, step), lambda i: (0, i))] * 3,
        out_shape=[jax.ShapeDtypeStruct((rows, hidden), BF16)] * 3,
        cost_estimate=COST,
        name="mlp",
    )(normed, y_grad, weight, down)


def out_body(o_in, h_in, wo_in, wd_in, out):
    out[...] = (dot(o_in[...], wo_in[...]) + dot(h_in[...], wd_in[...])).astype(BF16)


def out_partial(o, h, out_weight, down, start, cols):
    rows, local = o.shape
    hidden = h.shape[1]
    step = min(512, cols)
    base = start // step
    return pl.pallas_call(
        out_body,
        grid=(cols // step,),
        in_specs=[
            pl.BlockSpec((rows, local), lambda i: (0, 0)),
            pl.BlockSpec((rows, hidden), lambda i: (0, 0)),
            pl.BlockSpec((local, step), lambda i: (0, base + i)),
            pl.BlockSpec((hidden, step), lambda i: (0, base + i)),
        ],
        out_specs=pl.BlockSpec((rows, step), lambda i: (0, i)),
        out_shape=jax.ShapeDtypeStruct((rows, cols), BF16),
        cost_estimate=COST,
        name="out_partial",
    )(o, h, out_weight, down)


def dxn_body(*refs):
    dq_in, dk_in, dv_in, dg_in, du_in = refs[:5]
    wqkv_in, w_in, x_in, mean_in, inv_in, out, col_out = refs[5:]
    shift_sum = jnp.zeros((1, x_in.shape[1]), F32)
    gain_sum = jnp.zeros((1, x_in.shape[1]), F32)
    for start in range(0, x_in.shape[0], 256):
        span = slice(start, start + 256)
        total = dot(dq_in[span], wqkv_in[0], NT)
        total += dot(dk_in[span], wqkv_in[1], NT)
        total += dot(dv_in[span], wqkv_in[2], NT)
        total += dot(dg_in[span], w_in[0], NT)
        total += dot(du_in[span], w_in[1], NT)
        out[span] = total.astype(BF16)
        hat = (x_in[span].astype(F32) - mean_in[span]) * inv_in[span]
        shift_sum += jnp.sum(total, axis=0, keepdims=True)
        gain_sum += jnp.sum(total * hat, axis=0, keepdims=True)
    col_out[...] = jnp.concatenate([gain_sum, shift_sum], axis=0)


def dxn_partial(dqkv, dg, du, wqkv, weight, x, mean, inv, part):
    rows, hidden = dg.shape
    local, width = dqkv[0].shape[1], x.shape[1]
    step = min(256, width)
    whole = lambda a: pl.BlockSpec(a.shape, lambda i: (0,) * a.ndim)
    column = lambda: pl.BlockSpec((rows, 1), lambda i: (part, 0))
    return pl.pallas_call(
        dxn_body,
        grid=(width // step,),
        in_specs=[pl.BlockSpec((rows, local), lambda i: (part, 0))] * 3
        + [
            whole(dg),
            whole(du),
            pl.BlockSpec((3, step, local), lambda i: (0, i, 0)),
            pl.BlockSpec((2, step, hidden), lambda i: (0, i, 0)),
            pl.BlockSpec((rows, step), lambda i: (part, i)),
            column(),
            column(),
        ],
        out_specs=[
            pl.BlockSpec((rows, step), lambda i: (0, i)),
            pl.BlockSpec((2, step), lambda i: (0, i)),
        ],
        out_shape=[
            jax.ShapeDtypeStruct((rows, width), BF16),
            jax.ShapeDtypeStruct((2, width), F32),
        ],
        cost_estimate=COST,
        name="dxn_partial",
    )(*dqkv, dg, du, wqkv, weight, x, mean, inv)


def dw_sum(groups, lefts, rhs):
    position = 0
    for which, parts in groups:
        lhs = lefts[which]
        each = lhs.shape[0] // parts
        total = None
        for part in range(parts):
            piece = dot(lhs[part * each : (part + 1) * each], rhs[position][...], TN)
            total = piece if total is None else total + piece
            position += 1
        yield total


def dw_send_body(groups, order, *refs):
    *refs, out = refs
    number = len({which for which, _ in groups})
    start = 0
    for total in dw_sum(groups, refs[:number], refs[number:]):
        out[0, :, start : start + total.shape[1]] = total.astype(BF16)
        start += total.shape[1]


def dw_keep_body(groups, bundles, order, slots, *refs):
    number = len({which for which, _ in groups})
    lefts, refs = refs[:number], refs[number:]
    number = sum(parts for _, parts in groups)
    rhs, (received, *refs) = refs[:number], refs[number:]
    sends, keeps = refs[: len(bundles)], refs[len(bundles) :]
    step = pl.program_id(0)
    totals = dw_sum(groups, lefts, rhs)
    start = 0
    for number, bundle in enumerate(bundles):
        away = slots[3 * number, step] == 1
        pieces = []
        for _ in range(bundle):
            total = next(totals)
            stop = start + total.shape[1]
            pieces.append((total + received[0, :, start:stop].astype(F32)).astype(BF16))
            start = stop
        total = pieces[0] if bundle == 1 else jnp.concatenate(pieces, axis=1)

        @pl.when(away)
        def _(number=number, total=total):
            sends[number][0] = total

        @pl.when(jnp.logical_not(away))
        def _(number=number, total=total):
            keeps[number][0] = total


def dw_call(order, lefts, rhs, which, number, bundles, received=None, slots=None):
    count, width = lefts[0].shape
    step = width // (2 * number)
    groups = tuple((w, len(group)) for w, group in zip(which, rhs))
    flat = [part for group in rhs for part in group]
    columns = [group[0].shape[1] for group in rhs]
    scalars = [order] if slots is None else [order, slots]
    args = scalars + [*lefts, *flat]
    specs = [pl.BlockSpec((count, step), lambda i, order, *_: (0, order[i])) for _ in lefts]
    specs += [pl.BlockSpec(a.shape, lambda i, *_: (0, 0)) for a in flat]
    block = pl.BlockSpec((1, step, sum(columns)), lambda i, *_: (i, 0, 0))
    if received is None:
        body = functools.partial(dw_send_body, groups)
        out_specs = [block]
        shapes = [jax.ShapeDtypeStruct((number, step, sum(columns)), BF16)]
    else:
        body = functools.partial(dw_keep_body, groups, bundles)
        args.append(received)
        specs.append(block)
        ends = np.cumsum([0, *bundles])
        joined = [sum(columns[a:b]) for a, b in zip(ends, ends[1:])]
        out_specs = [
            pl.BlockSpec((1, step, c), lambda i, order, slots, r=3 * g + kind: (slots[r, i], 0, 0))
            for kind in (1, 2)
            for g, c in enumerate(joined)
        ]
        shapes = [jax.ShapeDtypeStruct((number // 2, step, c), BF16) for c in joined] * 2
    return pl.pallas_call(
        body,
        grid_spec=pltpu.PrefetchScalarGridSpec(
            num_scalar_prefetch=len(scalars), grid=(number,), in_specs=specs, out_specs=out_specs
        ),
        out_shape=shapes,
        cost_estimate=COST,
        name="weight_grad",
    )(*args)


def flip(size, bit):
    return [(i, i ^ bit) for i in range(size)]


class Order:
    def __init__(self):
        self.token = jnp.zeros((8, 128), F32)

    def __call__(self, function, *args):
        args, token = lax.optimization_barrier((args, self.token))
        out, self.token = lax.optimization_barrier((function(*args), token))
        return out

    def mark(self):
        self.token = mark(self.token)


def mark_body(seen, out):
    out[...] = seen[...]


def mark(seen):
    return pl.pallas_call(
        mark_body,
        out_shape=jax.ShapeDtypeStruct(seen.shape, seen.dtype),
        cost_estimate=pl.CostEstimate(flops=10**12, bytes_accessed=10**9, transcendentals=0),
        name="mark",
    )(seen)


def after_body(value, seen, out):
    out[...] = value[...]


def after(value, seen):
    return pl.pallas_call(
        after_body,
        out_shape=jax.ShapeDtypeStruct(value.shape, value.dtype),
        cost_estimate=COST,
        name="after",
    )(value, seen)


def halving_order(bits):
    order = [0]
    for bit in reversed(bits):
        order = [offset ^ bit for offset in order] + order
    return order


class Scatter:
    def __init__(self, run, devices, lefts, rhs, which, bundles, swaps):
        self.run, self.devices, self.lefts, self.rhs = run, devices, lefts, rhs
        self.which, self.bundles = which, bundles
        bits = [1 << i for i in range(devices.bit_length() - 1)]
        self.offsets = halving_order(bits)
        self.order = lax.axis_index("dp").astype(jnp.int32) ^ jnp.asarray(self.offsets, jnp.int32)
        self.bits = []
        for swap in swaps:
            rest = bits[1:]
            if swap and len(rest) > 1:
                rest[0], rest[1] = rest[1], rest[0]
            self.bits.append(rest)

    def send(self):
        half = self.devices // 2
        call = lambda lefts, rhs: dw_call(
            self.order[:half], lefts, rhs, self.which, half, self.bundles
        )
        (sent,) = self.run(call, self.lefts, self.rhs)
        self.received = lax.ppermute(sent, "dp", flip(self.devices, 1))

    def keep(self):
        half = self.devices // 2
        kept = self.offsets[half:]
        rows, self.left = [], []
        for bits in self.bits:
            away = [int(offset & bits[0] != 0) for offset in kept]
            place = lambda flags: [max(0, sum(flags[: i + 1]) - 1) for i in range(half)]
            rows += [away, place(away), place([1 - a for a in away])]
            self.left.append([offset for offset in kept if not offset & bits[0]])
        slots = jnp.asarray(np.array(rows), jnp.int32)
        call = lambda lefts, rhs, received: dw_call(
            self.order[half:], lefts, rhs, self.which, half, self.bundles, received, slots
        )
        outs = self.run(call, self.lefts, self.rhs, self.received)
        number = len(self.bits)
        self.kept = outs[number:]
        self.received = [
            lax.ppermute(s, "dp", flip(self.devices, bits[0])) for s, bits in zip(outs, self.bits)
        ]
        self.stage = 1

    def next(self):
        def step(kept, received):
            sends, keeps = [], []
            for group, bits in enumerate(self.bits):
                bit = bits[self.stage]
                for away, stack in ((True, sends), (False, keeps)):
                    where = [i for i, o in enumerate(self.left[group]) if bool(o & bit) == away]
                    pick = lambda a: jnp.stack([a[i] for i in where]).astype(F32)
                    stack.append((pick(kept[group]) + pick(received[group])).astype(BF16))
            return sends, keeps

        sends, self.kept = self.run(step, self.kept, self.received)
        self.received = []
        for group, bits in enumerate(self.bits):
            bit = bits[self.stage]
            self.left[group] = [o for o in self.left[group] if not o & bit]
            self.received.append(lax.ppermute(sends[group], "dp", flip(self.devices, bit)))
        self.stage += 1

    def last(self, shape=lambda a: a):
        while self.stage < len(self.bits[0]):
            self.next()
        add = lambda kept, received: shape(
            [k[0].astype(F32) + r[0].astype(F32) for k, r in zip(kept, received)]
        )
        return self.run(add, self.kept, self.received)


LINE = 4


def move_body(has, finish, inner, *refs):
    refs = iter(refs)
    partial, old, swapped, sum_, crossed = (next(refs) if given else None for given in has)
    *extra, send, total = refs if old is not None else (*refs, None)
    if old is not None:
        total[...] = (old[...].astype(F32) + swapped[...].astype(F32)).astype(BF16)
    if crossed is not None:
        mine = finish(sum_[...].astype(F32) + crossed[...].astype(F32), *extra).astype(BF16)
        if partial is not None:
            mine = jnp.where(inner[0] == 1, mine, partial[...])
        send[...] = mine


def move_call(inner, arrays, finish, extra, part):
    has = [a is not None for a in arrays]
    given = [a for a in arrays if a is not None]
    rows, width = given[0].shape
    step = min(64, rows)
    base = part * (rows // step)

    def spec(a):
        if a.shape[0] == 1:
            return pl.BlockSpec(a.shape, lambda i, _: (0, 0))
        return pl.BlockSpec((step, a.shape[1]), lambda i, _: (base + i, 0))

    block = pl.BlockSpec((step, width), lambda i, _: (i, 0))
    number = 2 if has[1] else 1
    return pl.pallas_call(
        functools.partial(move_body, has, finish),
        grid_spec=pltpu.PrefetchScalarGridSpec(
            num_scalar_prefetch=1,
            grid=(rows // step,),
            in_specs=[block] * len(given) + [spec(a) for a in extra],
            out_specs=[block] * number,
        ),
        out_shape=[jax.ShapeDtypeStruct((rows, width), BF16)] * number,
        cost_estimate=COST,
        name="move",
    )(inner, *given, *extra)


class Lines:
    def __init__(self, run, size, number):
        self.run, self.size, self.number, self.stage = run, size, number, 0
        lines = range(0, size, LINE)
        self.inward = [(b, b + 1) for b in lines] + [(b + 3, b + 2) for b in lines]
        self.across = [(b + 1, b + 2) for b in lines] + [(b + 2, b + 1) for b in lines]
        self.outward = [(b + 1, b) for b in lines] + [(b + 2, b + 3) for b in lines]
        place = lax.axis_index("mp") % LINE
        self.inner = (place == 1) | (place == 2)
        self.flag = self.inner.astype(jnp.int32).reshape(1)
        self.partial = self.sum = self.crossed = self.swapped = None
        self.done = []

    def step(self, partial=None, finish=None, extra=(), part=0):
        stage, number = self.stage, self.number
        self.stage += 1

        def move(partial, old, swapped, sum_, crossed):
            if crossed is None:
                add = lambda a, b: (a.astype(F32) + b.astype(F32)).astype(BF16)
                return partial, None if old is None else add(old, swapped)
            bit = LINE
            while bit < self.size:
                sum_ = (sum_.astype(F32) + crossed.astype(F32)).astype(BF16)
                pairs = [(i, i ^ bit) for i in range(self.size) if i % LINE in (1, 2)]
                crossed = lax.ppermute(sum_, "mp", pairs)
                bit *= 2
            arrays = (partial, old, None if old is None else swapped, sum_, crossed)
            outs = move_call(self.flag, arrays, finish, extra, part)
            return outs if len(outs) == 2 else (outs[0], None)

        old = self.partial if 1 <= stage <= number else None
        crossed = self.crossed if 2 <= stage else None
        send, total = self.run(move, partial, old, self.swapped, self.sum, crossed)
        pairs = (self.inward if stage < number else []) + (self.outward if stage >= 2 else [])
        self.swapped = lax.ppermute(send, "mp", pairs)
        if total is not None:
            self.crossed = lax.ppermute(total, "mp", self.across)
        self.partial, self.sum = partial, total
        if stage >= 2:
            self.done.append((send, self.swapped))


def shards(
    dp,
    mp,
    inputs,
    segment_ids,
    pad_count,
    layer_norm_gain,
    layer_norm_bias,
    qkv_weight,
    qkv_bias,
    out_weight,
    gateup_weight,
    down_weight,
    y_grad,
):
    count, width = inputs.shape
    local = qkv_weight.shape[2]
    parts = 2
    rows = count // parts

    seg = segment_ids[0]
    steps = jnp.arange(count, dtype=jnp.int32)
    start = jnp.sum((seg[None, :] < seg[:, None]).astype(jnp.int32), axis=1)
    valid = steps < count - pad_count[0]
    low = jnp.where(valid, start, steps)[None, :]
    valid_row = valid.astype(F32)[None, :]
    lane = jnp.arange(128, dtype=jnp.int32) % HEAD_DIM
    half = ROT // 2
    freq = jnp.power(10000.0, -2.0 * (lane % half).astype(F32) / ROT)
    freq = jnp.where(lane < ROT, freq, 0.0)
    angle = (steps - start).astype(F32)[:, None] * freq[None, :]
    sign = jnp.where(lane < half, -1.0, 1.0)
    cosine = jnp.cos(angle)
    sine = jnp.sin(angle) * sign[None, :]

    xf = inputs.astype(F32)
    mean = jnp.mean(xf, axis=-1, keepdims=True)
    removed = xf - mean
    inv = lax.rsqrt(jnp.mean(removed * removed, axis=-1, keepdims=True) + EPS)
    normed = (removed * inv * layer_norm_gain + layer_norm_bias).astype(BF16)

    wqkv = jnp.transpose(qkv_weight, (1, 0, 2))
    weight = jnp.transpose(gateup_weight, (1, 0, 2))

    run = Order()
    lines = Lines(run, mp, 2 * parts)
    old = None
    qs, ks, vs, os, lses, hs, dgs, dus = ([] for _ in range(8))
    for part in range(parts):
        span = slice(part * rows, (part + 1) * rows)

        def attend(normed, old, span=span, part=part):
            tables = cosine[span], sine[span], low[:, span], valid_row[:, span]
            return attn_fwd(normed, wqkv, qkv_bias, *tables, old, part)

        q, k, v, o, lse = run(attend, normed, old)
        old = (k, v)
        h, dg, du = run(
            lambda *a, part=part: mlp(*a, part, parts), normed, y_grad, weight, down_weight
        )
        for stack, item in zip((qs, ks, vs, os, lses, hs, dgs, dus), (q, k, v, o, lse, h, dg, du)):
            stack.append(item)
        lines.step(run(lambda *a: out_partial(*a, 0, width), o, h, out_weight, down_weight))

    def finish_out(total, x):
        return x[...].astype(F32) + total

    gateup = Scatter(run, dp, [normed], [dgs, dus], (0, 0), (1, 1), (False, True))

    def cotangent(y_grad, out_weight):
        d_attn = lax.dot_general(y_grad, out_weight, NT, preferred_element_type=F32).astype(BF16)
        return d_attn * valid.astype(BF16)[:, None]

    def emit(part):
        call = lambda dqkv, dg, du: dxn_partial(
            dqkv, dg, du, wqkv, weight, inputs, mean, inv, part
        )
        return run(call, dqkv, dgs[part], dus[part])

    def finish_grad(total, x, dy, mean, inv, gain):
        hat = (x[...].astype(F32) - mean[...]) * inv[...]
        scaled = total * gain[...]
        average = jnp.mean(scaled, axis=1, keepdims=True)
        slope = jnp.mean(scaled * hat, axis=1, keepdims=True)
        return dy[...].astype(F32) + inv[...] * (scaled - average - hat * slope)

    grad_extra = (inputs, y_grad, mean, inv, layer_norm_gain[None, :])

    def store(target, part, mine, received):
        step = lambda target, mine, received: lax.dynamic_update_slice(
            target, jnp.where(lines.inner, mine, received), (part * rows, 0)
        )
        return run(step, target, mine, received)

    blank = jnp.zeros((count, width), BF16)
    hidden = down_weight.shape[0]
    run.mark()
    d_attn = run(cotangent, y_grad, out_weight)
    *dqkv, bias_grad = run(lambda *a: attn_bwd(*a, cosine, sine, low), qs, ks, vs, lses, d_attn)
    rest = Scatter(
        run,
        dp,
        [y_grad, normed],
        [hs, os] + [[a] for a in dqkv],
        (0, 0, 1, 1, 1),
        (2, 3),
        (True, False),
    )
    gateup.send()
    partial, columns = emit(0)
    lines.step(partial, finish_out, (inputs,), 0)
    run.mark()
    partial, columns1 = emit(1)

    def small_step(value, axis, bit):
        size = {"dp": dp, "mp": mp}[axis]
        return run(jnp.add, value, lax.ppermute(value, axis, flip(size, bit)))

    small = run(
        lambda a, b, c: jnp.concatenate([(a + b).reshape(-1), c.reshape(-1)]),
        columns,
        columns1,
        bias_grad,
    )
    small = small_step(small, "dp", 1)
    gateup.keep()
    bit = 2
    while bit < dp:
        small = small_step(small, "dp", bit)
        bit *= 2
    rest.send()
    column_sums = small[: 2 * width]
    bias_sum = small[2 * width :].reshape(bias_grad.shape)
    lines.step(partial, finish_out, (inputs,), 1)
    run.mark()
    result = store(blank, 0, *lines.done[0])
    rest.keep()
    gateup.next()
    column_sums = small_step(column_sums, "mp", 1)
    lines.step(None, finish_grad, grad_extra, 0)
    run.mark()
    result = store(result, 1, *lines.done[1])
    rest.next()
    bit = 2
    while bit < mp:
        column_sums = small_step(column_sums, "mp", bit)
        bit *= 2
    column_sums = column_sums.reshape(2, width)
    lines.step(None, finish_grad, grad_extra, 1)
    run.mark()
    x_grad = store(blank, 0, *lines.done[2])
    gateup_grad = gateup.last(lambda a: jnp.stack(a, axis=1))
    down_grad, out_grad, qkv_grad = rest.last(
        lambda a: (a[0][:, :hidden].T, a[0][:, hidden:].T, a[1].reshape(-1, 3, local))
    )
    x_grad = store(x_grad, 1, *lines.done[3])
    column_sums = after(column_sums, run.token)
    return (
        result,
        x_grad,
        column_sums[0],
        column_sums[1],
        qkv_grad,
        bias_sum,
        out_grad,
        gateup_grad,
        down_grad,
    )


def solution(mesh):
    placed = (
        P("dp", None),
        P("dp", None),
        P("dp"),
        P(),
        P(),
        P(None, None, "mp"),
        P(None, "mp"),
        P("mp", None),
        P(None, None, "mp"),
        P("mp", None),
        P("dp", None),
    )
    return jax.shard_map(
        functools.partial(shards, mesh.shape["dp"], mesh.shape["mp"]),
        mesh=mesh,
        in_specs=placed,
        out_specs=(
            P("dp", None),
            P("dp", None),
            P(),
            P(),
            P("dp", None, "mp"),
            P(None, "mp"),
            P("mp", "dp"),
            P("dp", None, "mp"),
            P("mp", "dp"),
        ),
        check_vma=False,
    )
```

```python
import functools
import math

import jax
import jax.numpy as jnp
import numpy as np
from jax import lax
from jax.experimental import pallas as pl
from jax.experimental.pallas import tpu as pltpu
from jax.sharding import PartitionSpec as P

HEAD_DIM = 64
ROT = 16
DOCS = 4
DOC_MOST = 512
EPS = 1e-05
BQ = 256
LOG2E = math.log2(math.e)
SCALE2 = HEAD_DIM ** (-0.5) * LOG2E
F32 = jnp.float32
BF16 = jnp.bfloat16
NT = (((1,), (1,)), ((), ()))
TN = (((0,), (0,)), ((), ()))
COST = pl.CostEstimate(flops=1000, bytes_accessed=1000, transcendentals=0)
MARK = pl.CostEstimate(flops=10**12, bytes_accessed=10**9, transcendentals=0)


def dot(a, b, dims=(((1,), (0,)), ((), ()))):
    return lax.dot_general(a, b, dims, preferred_element_type=F32)


def turn(x, cosine, sine):
    lane = lax.broadcasted_iota(jnp.int32, x.shape, 1) % HEAD_DIM
    other = jnp.where(
        lane < ROT // 2, pltpu.roll(x, 128 - ROT // 2, 1), pltpu.roll(x, ROT // 2, 1)
    )
    return x * cosine + other * sine


def head_masks(x):
    low = lax.broadcasted_iota(jnp.int32, x.shape, 1) < HEAD_DIM
    zero = jnp.zeros_like(x)
    return (jnp.where(low, x, zero), jnp.where(low, zero, x))


def key_range(block):
    first = max(0, block - DOC_MOST // BQ)
    return first * BQ, (block + 1) * BQ


def masked_scores(keys, query, first, block, low_row):
    score = dot(keys, query, NT) * SCALE2
    index = first + lax.broadcasted_iota(jnp.int32, score.shape, 0)
    column = block * BQ + lax.broadcasted_iota(jnp.int32, score.shape, 1)
    allowed = (index >= low_row) & (index <= column)
    return score, allowed


def attn_fwd_body(before, x_in, w_in, bias, cosine, sine, low, valid, *rest):
    if before:
        old_k, old_v, q_out, k_out, v_out, o_out, lse_out, k_all, vt_all = rest
    else:
        q_out, k_out, v_out, o_out, lse_out, k_all, vt_all = rest
    count = x_in.shape[0]
    qkv = dot(x_in[...], jnp.concatenate([w_in[0], w_in[1], w_in[2]], axis=1))
    cos_t, sin_t = cosine[...], sine[...]
    query = turn(qkv[:, :128] + bias[0:1], cos_t, sin_t).astype(BF16)
    key = turn(qkv[:, 128:256] + bias[1:2], cos_t, sin_t).astype(BF16)
    value = (qkv[:, 256:] + bias[2:3]).astype(BF16)
    q_out[...] = query
    k_out[...] = key
    v_out[...] = value
    if before:
        k_all[:before] = old_k[...]
        vt_all[:, :before] = old_v[...].T
    k_all[before:] = key
    vt_all[:, before:] = value.T
    for local in range(count // BQ):
        block = before // BQ + local
        first, last = key_range(block)
        span = slice(local * BQ, (local + 1) * BQ)
        low_row = low[:, span]
        outs = []
        for head, part in enumerate(head_masks(q_out[span])):
            score, allowed = masked_scores(k_all[first:last], part, first, block, low_row)
            score = jnp.where(allowed, score, -1e30)
            top = jnp.max(score, axis=0, keepdims=True)
            expo = jnp.exp2(score - top)
            total = jnp.sum(expo, axis=0, keepdims=True)
            prob = (expo * (1.0 / total)).astype(BF16)
            outs.append(dot(vt_all[:, first:last], prob))
            lse_out[0, head : head + 1, span] = top + jnp.log2(total)
        upper = lax.broadcasted_iota(jnp.int32, outs[0].shape, 0) < HEAD_DIM
        joined = jnp.where(upper, outs[0], outs[1]) * valid[:, span]
        o_out[span] = joined.T.astype(BF16)


def attn_fwd(normed, weight, bias, cosine, sine, low, valid, old, part):
    width, local = weight.shape[1:]
    count = cosine.shape[0]
    before = 0 if old is None else old[0].shape[0]
    pairs = local // 128
    row = lambda n: pl.BlockSpec((n, 128), lambda i: (0, i))
    whole = lambda a: pl.BlockSpec(a.shape, lambda i: (0,) * a.ndim)
    args = [normed, weight, bias, cosine, sine, low, valid] + ([] if old is None else list(old))
    specs = [
        pl.BlockSpec((count, width), lambda i: (part, 0)),
        pl.BlockSpec((3, width, 128), lambda i: (0, 0, i)),
        row(3),
        *map(whole, (cosine, sine, low, valid)),
    ]
    specs += [row(before)] * (0 if old is None else 2)
    flat = jax.ShapeDtypeStruct((count, local), BF16)
    return pl.pallas_call(
        functools.partial(attn_fwd_body, before),
        grid=(pairs,),
        in_specs=specs,
        out_specs=[row(count)] * 4 + [pl.BlockSpec((1, 2, count), lambda i: (i, 0, 0))],
        out_shape=[flat] * 4 + [jax.ShapeDtypeStruct((pairs, 2, count), F32)],
        scratch_shapes=[
            pltpu.VMEM((before + count, 128), BF16),
            pltpu.VMEM((128, before + count), BF16),
        ],
        cost_estimate=COST,
        name="attn_fwd",
    )(*args)


def attn_bwd_body(parts, *refs):
    qs, ks, vs = refs[:parts], refs[parts : 2 * parts], refs[2 * parts : 3 * parts]
    lses = refs[3 * parts : 4 * parts]
    do_in, cosine, sine, low, dq_out, dk_out, dv_out, bias_out, kt_all, dk_acc, dv_acc = refs[
        4 * parts :
    ]
    each = qs[0].shape[0]

    def rows(refs_of, first, last):
        pieces = []
        for part, ref in enumerate(refs_of):
            lo, hi = max(first, part * each), min(last, (part + 1) * each)
            if lo < hi:
                pieces.append(ref[lo - part * each : hi - part * each])
        return pieces[0] if len(pieces) == 1 else jnp.concatenate(pieces, axis=0)

    for part in range(parts):
        kt_all[:, part * each : (part + 1) * each] = ks[part][...].T
    dk_acc[...] = jnp.zeros_like(dk_acc)
    dv_acc[...] = jnp.zeros_like(dv_acc)
    sums = [jnp.zeros((1, 128), F32) for _ in range(3)]
    blocks = parts * each // BQ
    for block in range(blocks):
        first, last = key_range(block)
        span = slice(block * BQ, (block + 1) * BQ)
        low_row = low[:, span]
        part, inside = block * BQ // each, block * BQ % each
        queries = head_masks(rows(qs, span.start, span.stop))
        d_outs = head_masks(do_in[span])
        keys, values = rows(ks, first, last), rows(vs, first, last)
        probs, d_scores, d_queries = [], [], []
        for head in range(2):
            score, allowed = masked_scores(keys, queries[head], first, block, low_row)
            lse = lses[part][0, head : head + 1, inside : inside + BQ]
            prob = jnp.where(allowed, jnp.exp2(score - lse), 0.0)
            d_prob = dot(values, d_outs[head], NT)
            delta = jnp.sum(prob * d_prob, axis=0, keepdims=True)
            d_score = (prob * (d_prob - delta)).astype(BF16)
            probs.append(prob.astype(BF16))
            d_scores.append(d_score)
            d_queries.append(dot(kt_all[:, first:last], d_score))
        wide = slice(first, last)
        dv_acc[wide] += dot(jnp.concatenate(probs, 1), jnp.concatenate(d_outs, 0))
        dk_acc[wide] += dot(jnp.concatenate(d_scores, 1), jnp.concatenate(queries, 0))
        upper = lax.broadcasted_iota(jnp.int32, d_queries[0].shape, 0) < HEAD_DIM
        d_query = jnp.where(upper, d_queries[0], d_queries[1]).T * HEAD_DIM ** (-0.5)
        d_query = turn(d_query, cosine[span], -sine[span]).astype(BF16)
        dq_out[span] = d_query
        sums[0] += jnp.sum(d_query.astype(F32), axis=0, keepdims=True)
        done = [block - DOC_MOST // BQ] if block + 1 < blocks else range(block - DOC_MOST // BQ, blocks)
        for old in done:
            if old < 0:
                continue
            there = slice(old * BQ, (old + 1) * BQ)
            d_key = dk_acc[there] * HEAD_DIM ** (-0.5)
            d_key = turn(d_key, cosine[there], -sine[there]).astype(BF16)
            d_value = dv_acc[there].astype(BF16)
            dk_out[there] = d_key
            dv_out[there] = d_value
            sums[1] += jnp.sum(d_key.astype(F32), axis=0, keepdims=True)
            sums[2] += jnp.sum(d_value.astype(F32), axis=0, keepdims=True)
    bias_out[...] = jnp.concatenate(sums, axis=0)


def attn_bwd(qs, ks, vs, lses, d_out, cosine, sine, low):
    parts = len(qs)
    each, local = qs[0].shape
    count = parts * each
    row = lambda n: pl.BlockSpec((n, 128), lambda i: (0, i))
    whole = lambda a: pl.BlockSpec(a.shape, lambda i: (0,) * a.ndim)
    flat = jax.ShapeDtypeStruct((count, local), BF16)
    return pl.pallas_call(
        functools.partial(attn_bwd_body, parts),
        grid=(local // 128,),
        in_specs=[row(each)] * (3 * parts)
        + [pl.BlockSpec((1, 2, each), lambda i: (i, 0, 0))] * parts
        + [row(count), whole(cosine), whole(sine), whole(low)],
        out_specs=[row(count)] * 3 + [row(3)],
        out_shape=[flat] * 3 + [jax.ShapeDtypeStruct((3, local), F32)],
        scratch_shapes=[
            pltpu.VMEM((128, count), BF16),
            pltpu.VMEM((count, 128), F32),
            pltpu.VMEM((count, 128), F32),
        ],
        cost_estimate=MARK,
        name="attn_bwd",
    )(*qs, *ks, *vs, *lses, d_out, cosine, sine, low)


def mlp_body(x_in, dy_in, w_in, down_in, h_out, dg_out, du_out):
    for start in range(0, x_in.shape[0], 256):
        span = slice(start, start + 256)
        gate = dot(x_in[span], w_in[0])
        upper = dot(x_in[span], w_in[1])
        d_hidden = dot(dy_in[span], down_in[...], NT)
        sigma = jax.nn.sigmoid(gate)
        active = gate * sigma
        h_out[span] = (active * upper).astype(BF16)
        du_out[span] = (d_hidden * active).astype(BF16)
        dg_out[span] = (d_hidden * upper * sigma * (1.0 + gate * (1.0 - sigma))).astype(BF16)


def mlp(normed, y_grad, weight, down, part, parts):
    count, width = normed.shape
    rows = count // parts
    hidden = down.shape[0]
    step = min(256, hidden)
    fixed = pl.BlockSpec((rows, width), lambda i: (part, 0))
    return pl.pallas_call(
        mlp_body,
        grid=(pl.cdiv(hidden, step),),
        in_specs=[
            fixed,
            fixed,
            pl.BlockSpec((2, width, step), lambda i: (0, 0, i)),
            pl.BlockSpec((step, width), lambda i: (i, 0)),
        ],
        out_specs=[pl.BlockSpec((rows, step), lambda i: (0, i))] * 3,
        out_shape=[jax.ShapeDtypeStruct((rows, hidden), BF16)] * 3,
        cost_estimate=COST,
        name="mlp",
    )(normed, y_grad, weight, down)


def out_body(o_in, h_in, wo_in, wd_in, out):
    out[...] = (dot(o_in[...], wo_in[...]) + dot(h_in[...], wd_in[...])).astype(BF16)


def out_partial(o, h, out_weight, down, start, cols):
    rows, local = o.shape
    hidden = h.shape[1]
    step = min(512, cols)
    base = start // step
    return pl.pallas_call(
        out_body,
        grid=(cols // step,),
        in_specs=[
            pl.BlockSpec((rows, local), lambda i: (0, 0)),
            pl.BlockSpec((rows, hidden), lambda i: (0, 0)),
            pl.BlockSpec((local, step), lambda i: (0, base + i)),
            pl.BlockSpec((hidden, step), lambda i: (0, base + i)),
        ],
        out_specs=pl.BlockSpec((rows, step), lambda i: (0, i)),
        out_shape=jax.ShapeDtypeStruct((rows, cols), BF16),
        cost_estimate=COST,
        name="out_partial",
    )(o, h, out_weight, down)


def dxn_body(*refs):
    dq_in, dk_in, dv_in, dg_in, du_in = refs[:5]
    wqkv_in, w_in, x_in, stats_in, out, col_out = refs[5:]
    shift_sum = jnp.zeros((1, x_in.shape[1]), F32)
    gain_sum = jnp.zeros((1, x_in.shape[1]), F32)
    for start in range(0, x_in.shape[0], 256):
        span = slice(start, start + 256)
        total = dot(dq_in[span], wqkv_in[0], NT)
        total += dot(dk_in[span], wqkv_in[1], NT)
        total += dot(dv_in[span], wqkv_in[2], NT)
        total += dot(dg_in[span], w_in[0], NT)
        total += dot(du_in[span], w_in[1], NT)
        out[span] = total.astype(BF16)
        hat = (x_in[span].astype(F32) - stats_in[span, :1]) * stats_in[span, 1:]
        shift_sum += jnp.sum(total, axis=0, keepdims=True)
        gain_sum += jnp.sum(total * hat, axis=0, keepdims=True)
    col_out[...] = jnp.concatenate([gain_sum, shift_sum], axis=0)


def dxn_partial(dqkv, dg, du, wqkv, weight, x, stats, part):
    rows, hidden = dg.shape
    local, width = dqkv[0].shape[1], x.shape[1]
    step = min(256, width)
    whole = lambda a: pl.BlockSpec(a.shape, lambda i: (0,) * a.ndim)
    return pl.pallas_call(
        dxn_body,
        grid=(width // step,),
        in_specs=[pl.BlockSpec((rows, local), lambda i: (part, 0))] * 3
        + [
            whole(dg),
            whole(du),
            pl.BlockSpec((3, step, local), lambda i: (0, i, 0)),
            pl.BlockSpec((2, step, hidden), lambda i: (0, i, 0)),
            pl.BlockSpec((rows, step), lambda i: (part, i)),
            pl.BlockSpec((rows, 2), lambda i: (part, 0)),
        ],
        out_specs=[
            pl.BlockSpec((rows, step), lambda i: (0, i)),
            pl.BlockSpec((2, step), lambda i: (0, i)),
        ],
        out_shape=[
            jax.ShapeDtypeStruct((rows, width), BF16),
            jax.ShapeDtypeStruct((2, width), F32),
        ],
        cost_estimate=MARK if part else COST,
        name="dxn_partial",
    )(*dqkv, dg, du, wqkv, weight, x, stats)


def dw_sum(groups, lefts, rhs):
    position = 0
    for which, parts in groups:
        lhs = lefts[which]
        each = lhs.shape[0] // parts
        total = None
        for part in range(parts):
            piece = dot(lhs[part * each : (part + 1) * each], rhs[position][...], TN)
            total = piece if total is None else total + piece
            position += 1
        yield total


def dw_send_body(groups, order, *refs):
    *refs, out = refs
    number = len({which for which, _ in groups})
    start = 0
    for total in dw_sum(groups, refs[:number], refs[number:]):
        out[0, :, start : start + total.shape[1]] = total.astype(BF16)
        start += total.shape[1]


def dw_keep_body(groups, bundles, order, slots, *refs):
    number = len({which for which, _ in groups})
    lefts, refs = refs[:number], refs[number:]
    number = sum(parts for _, parts in groups)
    rhs, (received, *refs) = refs[:number], refs[number:]
    sends, keeps = refs[: len(bundles)], refs[len(bundles) :]
    step = pl.program_id(0)
    totals = dw_sum(groups, lefts, rhs)
    start = 0
    for number, bundle in enumerate(bundles):
        away = slots[3 * number, step] == 1
        pieces = []
        for _ in range(bundle):
            total = next(totals)
            stop = start + total.shape[1]
            pieces.append((total + received[0, :, start:stop].astype(F32)).astype(BF16))
            start = stop
        total = pieces[0] if bundle == 1 else jnp.concatenate(pieces, axis=1)

        @pl.when(away)
        def _(number=number, total=total):
            sends[number][0] = total

        @pl.when(jnp.logical_not(away))
        def _(number=number, total=total):
            keeps[number][0] = total


def dw_call(order, lefts, rhs, which, number, bundles, received=None, slots=None):
    count, width = lefts[0].shape
    step = width // (2 * number)
    groups = tuple((w, len(group)) for w, group in zip(which, rhs))
    flat = [part for group in rhs for part in group]
    columns = [group[0].shape[1] for group in rhs]
    scalars = [order] if slots is None else [order, slots]
    args = scalars + [*lefts, *flat]
    specs = [pl.BlockSpec((count, step), lambda i, order, *_: (0, order[i])) for _ in lefts]
    specs += [pl.BlockSpec(a.shape, lambda i, *_: (0, 0)) for a in flat]
    block = pl.BlockSpec((1, step, sum(columns)), lambda i, *_: (i, 0, 0))
    if received is None:
        body = functools.partial(dw_send_body, groups)
        out_specs = [block]
        shapes = [jax.ShapeDtypeStruct((number, step, sum(columns)), BF16)]
    else:
        body = functools.partial(dw_keep_body, groups, bundles)
        args.append(received)
        specs.append(block)
        ends = np.cumsum([0, *bundles])
        joined = [sum(columns[a:b]) for a, b in zip(ends, ends[1:])]
        out_specs = [
            pl.BlockSpec((1, step, c), lambda i, order, slots, r=3 * g + kind: (slots[r, i], 0, 0))
            for kind in (1, 2)
            for g, c in enumerate(joined)
        ]
        shapes = [jax.ShapeDtypeStruct((number // 2, step, c), BF16) for c in joined] * 2
    return pl.pallas_call(
        body,
        grid_spec=pltpu.PrefetchScalarGridSpec(
            num_scalar_prefetch=len(scalars), grid=(number,), in_specs=specs, out_specs=out_specs
        ),
        out_shape=shapes,
        cost_estimate=COST,
        name="weight_grad",
    )(*args)


def flip(size, bit):
    return [(i, i ^ bit) for i in range(size)]


class Order:
    def __init__(self):
        self.token = jnp.zeros((8, 128), F32)

    def __call__(self, function, *args):
        args, token = lax.optimization_barrier((args, self.token))
        out, self.token = lax.optimization_barrier((function(*args), token))
        return out

    def mark(self):
        self.token = mark(self.token)


def mark_body(seen, out):
    out[...] = seen[...]


def mark(seen):
    return pl.pallas_call(
        mark_body,
        out_shape=jax.ShapeDtypeStruct(seen.shape, seen.dtype),
        cost_estimate=MARK,
        name="mark",
    )(seen)


def after_body(value, seen, out):
    out[...] = value[...]


def after(value, seen):
    return pl.pallas_call(
        after_body,
        out_shape=jax.ShapeDtypeStruct(value.shape, value.dtype),
        cost_estimate=COST,
        name="after",
    )(value, seen)


def halving_order(bits):
    order = [0]
    for bit in reversed(bits):
        order = [offset ^ bit for offset in order] + order
    return order


class Scatter:
    def __init__(self, run, devices, lefts, rhs, which, bundles, swaps):
        self.run, self.devices, self.lefts, self.rhs = run, devices, lefts, rhs
        self.which, self.bundles = which, bundles
        bits = [1 << i for i in range(devices.bit_length() - 1)]
        self.offsets = halving_order(bits)
        self.order = lax.axis_index("dp").astype(jnp.int32) ^ jnp.asarray(self.offsets, jnp.int32)
        self.bits = []
        for swap in swaps:
            rest = bits[1:]
            if swap and len(rest) > 1:
                rest[0], rest[1] = rest[1], rest[0]
            self.bits.append(rest)

    def send(self):
        half = self.devices // 2
        call = lambda lefts, rhs: dw_call(
            self.order[:half], lefts, rhs, self.which, half, self.bundles
        )
        (sent,) = self.run(call, self.lefts, self.rhs)
        self.received = lax.ppermute(sent, "dp", flip(self.devices, 1))

    def keep(self):
        half = self.devices // 2
        kept = self.offsets[half:]
        rows, self.left = [], []
        for bits in self.bits:
            away = [int(offset & bits[0] != 0) for offset in kept]
            place = lambda flags: [max(0, sum(flags[: i + 1]) - 1) for i in range(half)]
            rows += [away, place(away), place([1 - a for a in away])]
            self.left.append([offset for offset in kept if not offset & bits[0]])
        slots = jnp.asarray(np.array(rows), jnp.int32)
        call = lambda lefts, rhs, received: dw_call(
            self.order[half:], lefts, rhs, self.which, half, self.bundles, received, slots
        )
        outs = self.run(call, self.lefts, self.rhs, self.received)
        number = len(self.bits)
        self.kept = outs[number:]
        self.received = [
            lax.ppermute(s, "dp", flip(self.devices, bits[0])) for s, bits in zip(outs, self.bits)
        ]
        self.stage = 1

    def next(self):
        rows = []
        for group, bits in enumerate(self.bits):
            bit = bits[self.stage]
            for away in (True, False):
                rows.append([i for i, o in enumerate(self.left[group]) if bool(o & bit) == away])
            self.left[group] = [o for o in self.left[group] if not o & bit]
        slots = jnp.asarray(np.array(rows), jnp.int32)
        call = lambda kept, received: next_call(kept, received, slots, len(rows[0]))
        outs = self.run(call, self.kept, self.received)
        number = len(self.bits)
        self.kept = outs[number:]
        self.received = [
            lax.ppermute(s, "dp", flip(self.devices, bits[self.stage]))
            for s, bits in zip(outs, self.bits)
        ]
        self.stage += 1

    def last(self, pieces):
        while self.stage < len(self.bits[0]):
            self.next()
        call = lambda kept, received: last_call(kept, received, pieces)
        return self.run(call, self.kept, self.received)


def next_body(slots, *refs):
    number = len(refs) // 6
    for n in range(2 * number):
        pair, out = refs[2 * n : 2 * n + 2], refs[4 * number + n]
        out[0] = (pair[0][0].astype(F32) + pair[1][0].astype(F32)).astype(BF16)


def next_call(kept, received, slots, pieces):
    rows = kept[0].shape[1]
    step = min(64, rows)
    args, specs, outs, shapes = [], [], [], []
    for away in (0, 1):
        for group, pair in enumerate(zip(kept, received)):
            columns = pair[0].shape[2]
            place = lambda i, j, slots, r=2 * group + away: (slots[r, i], j, 0)
            args += pair
            specs += [pl.BlockSpec((1, step, columns), place)] * 2
            outs.append(pl.BlockSpec((1, step, columns), lambda i, j, slots: (i, j, 0)))
            shapes.append(jax.ShapeDtypeStruct((pieces, rows, columns), BF16))
    return pl.pallas_call(
        next_body,
        grid_spec=pltpu.PrefetchScalarGridSpec(
            num_scalar_prefetch=1, grid=(pieces, rows // step), in_specs=specs, out_specs=outs
        ),
        out_shape=shapes,
        cost_estimate=COST,
        name="next",
    )(slots, *args)


def last_body(pieces, *refs):
    outs = iter(refs[2 * len(pieces) :])
    stacked = None
    place = 0
    for n, widths in enumerate(pieces):
        kept, received = refs[2 * n], refs[2 * n + 1]
        start = 0
        for width, turned in widths:
            span = slice(start, start + width)
            start += width
            total = kept[0, :, span].astype(F32) + received[0, :, span].astype(F32)
            if turned:
                next(outs)[...] = total.T
                continue
            stacked = next(outs) if stacked is None else stacked
            if stacked.shape[0] == total.shape[0]:
                stacked[:, place] = total
            else:
                stacked[place] = total
            place += 1


def last_call(kept, received, pieces):
    rows = kept[0].shape[1]
    step = min(128, rows)
    args, specs, outs, shapes, stacked = [], [], [], [], []
    for pair, widths in zip(zip(kept, received), pieces):
        args += pair
        specs += [pl.BlockSpec((1, step, pair[0].shape[2]), lambda i: (0, i, 0))] * 2
        for width, turned in widths:
            if turned:
                outs.append(pl.BlockSpec((width, step), lambda i: (0, i)))
                shapes.append(jax.ShapeDtypeStruct((width, rows), F32))
            else:
                stacked.append(width)
    if len(stacked) == 2:
        outs.append(pl.BlockSpec((step, 2, stacked[0]), lambda i: (i, 0, 0)))
        shapes.append(jax.ShapeDtypeStruct((rows, 2, stacked[0]), F32))
    elif stacked:
        outs.append(pl.BlockSpec((len(stacked), step, stacked[0]), lambda i: (0, i, 0)))
        shapes.append(jax.ShapeDtypeStruct((len(stacked), rows, stacked[0]), F32))
    return pl.pallas_call(
        functools.partial(last_body, pieces),
        grid=(rows // step,),
        in_specs=specs,
        out_specs=outs,
        out_shape=shapes,
        cost_estimate=COST,
        name="last",
    )(*args)


LINE = 4


def move_body(has, finish, inner, *refs):
    refs = iter(refs)
    partial, old, swapped, sum_, crossed = (next(refs) if given else None for given in has)
    *extra, send, total = refs if old is not None else (*refs, None)
    slab = 16

    def rows(i, carry):
        span = pl.ds(pl.multiple_of(i * slab, slab), slab)
        if old is not None:
            total[span] = (old[span].astype(F32) + swapped[span].astype(F32)).astype(BF16)
        added = sum_[span].astype(F32) + crossed[span].astype(F32)
        mine = finish(added, *(e[...] if e.shape[0] == 1 else e[span] for e in extra)).astype(BF16)
        if partial is not None:
            mine = jnp.where(inner[0] == 1, mine, partial[span])
        send[span] = mine
        return carry

    lax.fori_loop(0, send.shape[0] // slab, rows, 0, unroll=2)


def move_call(inner, arrays, finish, extra, part):
    has = [a is not None for a in arrays]
    given = [a for a in arrays if a is not None]
    rows, width = given[0].shape
    step = min(128, rows)
    base = part * (rows // step)
    fixed = lambda i, inner: jnp.where(inner[0] == 1, i, 0)

    def spec(a):
        if a.shape[0] == 1:
            return pl.BlockSpec(a.shape, lambda i, inner: (0, 0))
        return pl.BlockSpec((step, a.shape[1]), lambda i, inner: (base + fixed(i, inner), 0))

    block = pl.BlockSpec((step, width), lambda i, inner: (i, 0))
    in_block = pl.BlockSpec((step, width), lambda i, inner: (fixed(i, inner), 0))
    out_block = pl.BlockSpec((step, width), lambda i, inner: (jnp.where(inner[0] == 1, 0, i), 0))
    in_specs = [out_block if a is arrays[0] else in_block for a in given]
    number = 2 if has[1] else 1
    return pl.pallas_call(
        functools.partial(move_body, has, finish),
        grid_spec=pltpu.PrefetchScalarGridSpec(
            num_scalar_prefetch=1,
            grid=(rows // step,),
            in_specs=in_specs + [spec(a) for a in extra],
            out_specs=[block] * number,
        ),
        out_shape=[jax.ShapeDtypeStruct((rows, width), BF16)] * number,
        cost_estimate=COST,
        name="move",
    )(inner, *given, *extra)


class Lines:
    def __init__(self, run, size, number):
        self.run, self.size, self.number, self.stage = run, size, number, 0
        lines = range(0, size, LINE)
        self.inward = [(b, b + 1) for b in lines] + [(b + 3, b + 2) for b in lines]
        self.across = [(b + 1, b + 2) for b in lines] + [(b + 2, b + 1) for b in lines]
        self.outward = [(b + 1, b) for b in lines] + [(b + 2, b + 3) for b in lines]
        place = lax.axis_index("mp") % LINE
        self.inner = (place == 1) | (place == 2)
        self.flag = self.inner.astype(jnp.int32).reshape(1)
        self.partial = self.sum = self.crossed = self.swapped = None
        self.done = []

    def step(self, partial=None, finish=None, extra=(), part=0):
        stage, number = self.stage, self.number
        self.stage += 1

        def move(partial, old, swapped, sum_, crossed):
            if crossed is None:
                add = lambda a, b: (a.astype(F32) + b.astype(F32)).astype(BF16)
                return partial, None if old is None else add(old, swapped)
            bit = LINE
            while bit < self.size:
                sum_ = (sum_.astype(F32) + crossed.astype(F32)).astype(BF16)
                pairs = [(i, i ^ bit) for i in range(self.size) if i % LINE in (1, 2)]
                crossed = lax.ppermute(sum_, "mp", pairs)
                bit *= 2
            arrays = (partial, old, None if old is None else swapped, sum_, crossed)
            outs = move_call(self.flag, arrays, finish, extra, part)
            return outs if len(outs) == 2 else (outs[0], None)

        old = self.partial if 1 <= stage <= number else None
        crossed = self.crossed if 2 <= stage else None
        send, total = self.run(move, partial, old, self.swapped, self.sum, crossed)
        pairs = (self.inward if stage < number else []) + (self.outward if stage >= 2 else [])
        self.swapped = lax.ppermute(send, "mp", pairs)
        if total is not None:
            self.crossed = lax.ppermute(total, "mp", self.across)
        self.partial, self.sum = partial, total
        if stage >= 2:
            self.done.append((send, self.swapped))


def shards(
    dp,
    mp,
    inputs,
    segment_ids,
    pad_count,
    layer_norm_gain,
    layer_norm_bias,
    qkv_weight,
    qkv_bias,
    out_weight,
    gateup_weight,
    down_weight,
    y_grad,
):
    count, width = inputs.shape
    local = qkv_weight.shape[2]
    parts = 2
    rows = count // parts

    seg = segment_ids[0]
    steps = jnp.arange(count, dtype=jnp.int32)
    start = jnp.sum((seg[None, :] < seg[:, None]).astype(jnp.int32), axis=1)
    valid = steps < count - pad_count[0]
    low = jnp.where(valid, start, steps)[None, :]
    valid_row = valid.astype(F32)[None, :]
    lane = jnp.arange(128, dtype=jnp.int32) % HEAD_DIM
    half = ROT // 2
    freq = jnp.power(10000.0, -2.0 * (lane % half).astype(F32) / ROT)
    freq = jnp.where(lane < ROT, freq, 0.0)
    angle = (steps - start).astype(F32)[:, None] * freq[None, :]
    sign = jnp.where(lane < half, -1.0, 1.0)
    cosine = jnp.cos(angle)
    sine = jnp.sin(angle) * sign[None, :]

    xf = inputs.astype(F32)
    mean = jnp.mean(xf, axis=-1, keepdims=True)
    removed = xf - mean
    inv = lax.rsqrt(jnp.mean(removed * removed, axis=-1, keepdims=True) + EPS)
    normed = (removed * inv * layer_norm_gain + layer_norm_bias).astype(BF16)

    stats = jnp.concatenate([mean, inv], axis=1)

    wqkv = jnp.transpose(qkv_weight, (1, 0, 2))

    def cotangent(y_grad, out_weight):
        d_attn = lax.dot_general(y_grad, out_weight, NT, preferred_element_type=F32).astype(BF16)
        return d_attn * valid.astype(BF16)[:, None]

    run = Order()
    weight = run(lambda a: jnp.transpose(a, (1, 0, 2)), gateup_weight)
    lines = Lines(run, mp, 2 * parts)
    old = None
    qs, ks, vs, os, lses, hs, dgs, dus = ([] for _ in range(8))
    for part in range(parts):
        span = slice(part * rows, (part + 1) * rows)

        def attend(normed, old, span=span, part=part):
            tables = cosine[span], sine[span], low[:, span], valid_row[:, span]
            return attn_fwd(normed, wqkv, qkv_bias, *tables, old, part)

        q, k, v, o, lse = run(attend, normed, old)
        old = (k, v)
        h, dg, du = run(
            lambda *a, part=part: mlp(*a, part, parts), normed, y_grad, weight, down_weight
        )
        for stack, item in zip((qs, ks, vs, os, lses, hs, dgs, dus), (q, k, v, o, lse, h, dg, du)):
            stack.append(item)
        partial = run(lambda *a: out_partial(*a, 0, width), o, h, out_weight, down_weight)
        if part == parts - 1:
            d_attn = run(cotangent, y_grad, out_weight)
        lines.step(partial)

    def finish_out(total, x):
        return x.astype(F32) + total

    gateup = Scatter(run, dp, [normed], [dgs, dus], (0, 0), (1, 1), (False, True))

    def emit(part):
        call = lambda dqkv, dg, du: dxn_partial(
            dqkv, dg, du, wqkv, weight, inputs, stats, part
        )
        return run(call, dqkv, dgs[part], dus[part])

    def finish_grad(total, x, dy, stats, gain):
        mean, inv = stats[:, :1], stats[:, 1:]
        hat = (x.astype(F32) - mean) * inv
        scaled = total * gain
        average = jnp.mean(scaled, axis=1, keepdims=True)
        slope = jnp.mean(scaled * hat, axis=1, keepdims=True)
        return dy.astype(F32) + inv * (scaled - average - hat * slope)

    grad_extra = (inputs, y_grad, stats, layer_norm_gain[None, :])

    def store(target, part, mine, received):
        step = lambda target, mine, received: lax.dynamic_update_slice(
            target, jnp.where(lines.inner, mine, received), (part * rows, 0)
        )
        return run(step, target, mine, received)

    blank = jnp.zeros((count, width), BF16)
    hidden = down_weight.shape[0]
    *dqkv, bias_grad = run(lambda *a: attn_bwd(*a, cosine, sine, low), qs, ks, vs, lses, d_attn)
    rest = Scatter(
        run,
        dp,
        [y_grad, normed],
        [hs, os] + [[a] for a in dqkv],
        (0, 0, 1, 1, 1),
        (2, 3),
        (True, False),
    )
    partial, columns = emit(0)
    lines.step(partial, finish_out, (inputs,), 0)
    partial, columns1 = emit(1)

    def small_step(value, axis, bit):
        size = {"dp": dp, "mp": mp}[axis]
        return run(jnp.add, value, lax.ppermute(value, axis, flip(size, bit)))

    small = run(
        lambda a, b, c: jnp.concatenate([(a + b).reshape(-1), c.reshape(-1)]),
        columns,
        columns1,
        bias_grad,
    )
    small = small_step(small, "dp", 1)
    gateup.send()
    bit = 2
    while bit < dp // 2:
        small = small_step(small, "dp", bit)
        bit *= 2
    rest.send()
    while bit < dp:
        small = small_step(small, "dp", bit)
        bit *= 2
    column_sums = small[: 2 * width]
    bias_sum = small[2 * width :].reshape(bias_grad.shape)
    lines.step(partial, finish_out, (inputs,), 1)
    run.mark()
    gateup.keep()
    rest.keep()
    result = store(blank, 0, *lines.done[0])
    gateup.next()
    column_sums = small_step(column_sums, "mp", 1)
    lines.step(None, finish_grad, grad_extra, 0)
    run.mark()
    result = store(result, 1, *lines.done[1])
    rest.next()
    bit = 2
    while bit < mp:
        column_sums = small_step(column_sums, "mp", bit)
        bit *= 2
    column_sums = column_sums.reshape(2, width)
    lines.step(None, finish_grad, grad_extra, 1)
    x_grad = store(blank, 0, *lines.done[2])
    (gateup_grad,) = gateup.last((((hidden, False),), ((hidden, False),)))
    down_grad, out_grad, qkv_grad = rest.last(
        (((hidden, True), (local, True)), ((local, False),) * 3)
    )
    qkv_grad = jnp.transpose(qkv_grad, (1, 0, 2))
    column_sums = after(column_sums, run.token)
    x_grad = store(x_grad, 1, *lines.done[3])
    return (
        result,
        x_grad,
        column_sums[0],
        column_sums[1],
        qkv_grad,
        bias_sum,
        out_grad,
        gateup_grad,
        down_grad,
    )


def solution(mesh):
    placed = (
        P("dp", None),
        P("dp", None),
        P("dp"),
        P(),
        P(),
        P(None, None, "mp"),
        P(None, "mp"),
        P("mp", None),
        P(None, None, "mp"),
        P("mp", None),
        P("dp", None),
    )
    return jax.shard_map(
        functools.partial(shards, mesh.shape["dp"], mesh.shape["mp"]),
        mesh=mesh,
        in_specs=placed,
        out_specs=(
            P("dp", None),
            P("dp", None),
            P(),
            P(),
            P("dp", None, "mp"),
            P(None, "mp"),
            P("mp", "dp"),
            P("dp", None, "mp"),
            P("mp", "dp"),
        ),
        check_vma=False,
    )
```

```python
import functools
import math

import jax
import jax.numpy as jnp
import numpy as np
from jax import lax
from jax.experimental import pallas as pl
from jax.experimental.pallas import tpu as pltpu
from jax.sharding import PartitionSpec as P

HEAD_DIM = 64
ROT = 16
DOCS = 4
DOC_MOST = 512
EPS = 1e-05
BQ = 256
LOG2E = math.log2(math.e)
SCALE2 = HEAD_DIM ** (-0.5) * LOG2E
F32 = jnp.float32
BF16 = jnp.bfloat16
NT = (((1,), (1,)), ((), ()))
TN = (((0,), (0,)), ((), ()))
COST = pl.CostEstimate(flops=1000, bytes_accessed=1000, transcendentals=0)
MARK = pl.CostEstimate(flops=10**12, bytes_accessed=10**9, transcendentals=0)


def dot(a, b, dims=(((1,), (0,)), ((), ()))):
    return lax.dot_general(a, b, dims, preferred_element_type=F32)


def turn(x, cosine, sine):
    lane = lax.broadcasted_iota(jnp.int32, x.shape, 1) % HEAD_DIM
    other = jnp.where(
        lane < ROT // 2, pltpu.roll(x, 128 - ROT // 2, 1), pltpu.roll(x, ROT // 2, 1)
    )
    return x * cosine + other * sine


def head_masks(x):
    low = lax.broadcasted_iota(jnp.int32, x.shape, 1) < HEAD_DIM
    zero = jnp.zeros_like(x)
    return (jnp.where(low, x, zero), jnp.where(low, zero, x))


def key_range(block):
    first = max(0, block - DOC_MOST // BQ)
    return first * BQ, (block + 1) * BQ


def masked_scores(keys, query, first, block, low_row):
    score = dot(keys, query, NT) * SCALE2
    before = score.shape[0] - BQ

    def mask(values, other):
        row = lax.broadcasted_iota(jnp.int32, (BQ, BQ), 0)
        column = lax.broadcasted_iota(jnp.int32, (BQ, BQ), 1)
        last = (row >= low_row - block * BQ) & (row <= column)
        pieces = [jnp.where(last, values[before:], other)]
        if before:
            row = lax.broadcasted_iota(jnp.int32, (before, BQ), 0)
            pieces.insert(0, jnp.where(row >= low_row - first, values[:before], other))
        return pieces[0] if len(pieces) == 1 else jnp.concatenate(pieces, axis=0)

    return score, mask


def attn_fwd_body(before, x_in, w_in, bias, cosine, sine, low, valid, *rest):
    if before:
        old_k, old_v, q_out, k_out, v_out, o_out, lse_out, k_all, vt_all = rest
    else:
        q_out, k_out, v_out, o_out, lse_out, k_all, vt_all = rest
    count = x_in.shape[0]
    qkv = dot(x_in[...], jnp.concatenate([w_in[0], w_in[1], w_in[2]], axis=1))
    cos_t, sin_t = cosine[...], sine[...]
    query = turn(qkv[:, :128] + bias[0:1], cos_t, sin_t).astype(BF16)
    key = turn(qkv[:, 128:256] + bias[1:2], cos_t, sin_t).astype(BF16)
    value = (qkv[:, 256:] + bias[2:3]).astype(BF16)
    q_out[...] = query
    k_out[...] = key
    v_out[...] = value
    if before:
        k_all[:before] = old_k[...]
        vt_all[:, :before] = old_v[...].T
    k_all[before:] = key
    vt_all[:, before:] = value.T
    for local in range(count // BQ):
        block = before // BQ + local
        first, last = key_range(block)
        span = slice(local * BQ, (local + 1) * BQ)
        low_row = low[:, span]
        outs = []
        for head, part in enumerate(head_masks(q_out[span])):
            score, mask = masked_scores(k_all[first:last], part, first, block, low_row)
            score = mask(score, -1e30)
            top = jnp.max(score, axis=0, keepdims=True)
            expo = jnp.exp2(score - top)
            total = jnp.sum(expo, axis=0, keepdims=True)
            prob = (expo * (1.0 / total)).astype(BF16)
            outs.append(dot(vt_all[:, first:last], prob))
            lse_out[0, head : head + 1, span] = top + jnp.log2(total)
        upper = lax.broadcasted_iota(jnp.int32, outs[0].shape, 0) < HEAD_DIM
        joined = jnp.where(upper, outs[0], outs[1]) * valid[:, span]
        o_out[span] = joined.T.astype(BF16)


def attn_fwd(normed, weight, bias, cosine, sine, low, valid, old, part):
    width, local = weight.shape[1:]
    count = cosine.shape[0]
    before = 0 if old is None else old[0].shape[0]
    pairs = local // 128
    row = lambda n: pl.BlockSpec((n, 128), lambda i: (0, i))
    whole = lambda a: pl.BlockSpec(a.shape, lambda i: (0,) * a.ndim)
    args = [normed, weight, bias, cosine, sine, low, valid] + ([] if old is None else list(old))
    specs = [
        pl.BlockSpec((count, width), lambda i: (part, 0)),
        pl.BlockSpec((3, width, 128), lambda i: (0, 0, i)),
        row(3),
        *map(whole, (cosine, sine, low, valid)),
    ]
    specs += [row(before)] * (0 if old is None else 2)
    flat = jax.ShapeDtypeStruct((count, local), BF16)
    return pl.pallas_call(
        functools.partial(attn_fwd_body, before),
        grid=(pairs,),
        in_specs=specs,
        out_specs=[row(count)] * 4 + [pl.BlockSpec((1, 2, count), lambda i: (i, 0, 0))],
        out_shape=[flat] * 4 + [jax.ShapeDtypeStruct((pairs, 2, count), F32)],
        scratch_shapes=[
            pltpu.VMEM((before + count, 128), BF16),
            pltpu.VMEM((128, before + count), BF16),
        ],
        cost_estimate=COST,
        name="attn_fwd",
    )(*args)


def attn_bwd_body(parts, *refs):
    qs, ks, vs = refs[:parts], refs[parts : 2 * parts], refs[2 * parts : 3 * parts]
    lses = refs[3 * parts : 4 * parts]
    do_in, cosine, sine, low, dq_out, dk_out, dv_out, bias_out, kt_all, dk_acc, dv_acc = refs[
        4 * parts :
    ]
    each = qs[0].shape[0]

    def rows(refs_of, first, last):
        pieces = []
        for part, ref in enumerate(refs_of):
            lo, hi = max(first, part * each), min(last, (part + 1) * each)
            if lo < hi:
                pieces.append(ref[lo - part * each : hi - part * each])
        return pieces[0] if len(pieces) == 1 else jnp.concatenate(pieces, axis=0)

    for part in range(parts):
        kt_all[:, part * each : (part + 1) * each] = ks[part][...].T
    dk_acc[...] = jnp.zeros_like(dk_acc)
    dv_acc[...] = jnp.zeros_like(dv_acc)
    sums = [jnp.zeros((1, 128), F32) for _ in range(3)]
    blocks = parts * each // BQ
    for block in range(blocks):
        first, last = key_range(block)
        span = slice(block * BQ, (block + 1) * BQ)
        low_row = low[:, span]
        part, inside = block * BQ // each, block * BQ % each
        queries = head_masks(rows(qs, span.start, span.stop))
        d_outs = head_masks(do_in[span])
        keys, values = rows(ks, first, last), rows(vs, first, last)
        probs, d_scores, d_queries = [], [], []
        for head in range(2):
            score, mask = masked_scores(keys, queries[head], first, block, low_row)
            lse = lses[part][0, head : head + 1, inside : inside + BQ]
            prob = mask(jnp.exp2(score - lse), 0.0)
            d_prob = dot(values, d_outs[head], NT)
            delta = jnp.sum(prob * d_prob, axis=0, keepdims=True)
            d_score = (prob * (d_prob - delta)).astype(BF16)
            probs.append(prob.astype(BF16))
            d_scores.append(d_score)
            d_queries.append(dot(kt_all[:, first:last], d_score))
        wide = slice(first, last)
        dv_acc[wide] += dot(jnp.concatenate(probs, 1), jnp.concatenate(d_outs, 0))
        dk_acc[wide] += dot(jnp.concatenate(d_scores, 1), jnp.concatenate(queries, 0))
        upper = lax.broadcasted_iota(jnp.int32, d_queries[0].shape, 0) < HEAD_DIM
        d_query = jnp.where(upper, d_queries[0], d_queries[1]).T * HEAD_DIM ** (-0.5)
        d_query = turn(d_query, cosine[span], -sine[span]).astype(BF16)
        dq_out[span] = d_query
        sums[0] += jnp.sum(d_query.astype(F32), axis=0, keepdims=True)
        done = [block - DOC_MOST // BQ] if block + 1 < blocks else range(block - DOC_MOST // BQ, blocks)
        for old in done:
            if old < 0:
                continue
            there = slice(old * BQ, (old + 1) * BQ)
            d_key = dk_acc[there] * HEAD_DIM ** (-0.5)
            d_key = turn(d_key, cosine[there], -sine[there]).astype(BF16)
            d_value = dv_acc[there].astype(BF16)
            dk_out[there] = d_key
            dv_out[there] = d_value
            sums[1] += jnp.sum(d_key.astype(F32), axis=0, keepdims=True)
            sums[2] += jnp.sum(d_value.astype(F32), axis=0, keepdims=True)
    bias_out[...] = jnp.concatenate(sums, axis=0)


def attn_bwd(qs, ks, vs, lses, d_out, cosine, sine, low):
    parts = len(qs)
    each, local = qs[0].shape
    count = parts * each
    row = lambda n: pl.BlockSpec((n, 128), lambda i: (0, i))
    whole = lambda a: pl.BlockSpec(a.shape, lambda i: (0,) * a.ndim)
    flat = jax.ShapeDtypeStruct((count, local), BF16)
    return pl.pallas_call(
        functools.partial(attn_bwd_body, parts),
        grid=(local // 128,),
        in_specs=[row(each)] * (3 * parts)
        + [pl.BlockSpec((1, 2, each), lambda i: (i, 0, 0))] * parts
        + [row(count), whole(cosine), whole(sine), whole(low)],
        out_specs=[row(count)] * 3 + [row(3)],
        out_shape=[flat] * 3 + [jax.ShapeDtypeStruct((3, local), F32)],
        scratch_shapes=[
            pltpu.VMEM((128, count), BF16),
            pltpu.VMEM((count, 128), F32),
            pltpu.VMEM((count, 128), F32),
        ],
        cost_estimate=MARK,
        name="attn_bwd",
    )(*qs, *ks, *vs, *lses, d_out, cosine, sine, low)


def mlp_body(x_in, dy_in, w_in, down_in, h_out, dg_out, du_out):
    for start in range(0, x_in.shape[0], 256):
        span = slice(start, start + 256)
        gate = dot(x_in[span], w_in[0])
        upper = dot(x_in[span], w_in[1])
        d_hidden = dot(dy_in[span], down_in[...], NT)
        sigma = jax.nn.sigmoid(gate)
        active = gate * sigma
        h_out[span] = (active * upper).astype(BF16)
        du_out[span] = (d_hidden * active).astype(BF16)
        dg_out[span] = (d_hidden * upper * sigma * (1.0 + gate * (1.0 - sigma))).astype(BF16)


def mlp(normed, y_grad, weight, down, part, parts):
    count, width = normed.shape
    rows = count // parts
    hidden = down.shape[0]
    step = min(256, hidden)
    fixed = pl.BlockSpec((rows, width), lambda i: (part, 0))
    return pl.pallas_call(
        mlp_body,
        grid=(pl.cdiv(hidden, step),),
        in_specs=[
            fixed,
            fixed,
            pl.BlockSpec((2, width, step), lambda i: (0, 0, i)),
            pl.BlockSpec((step, width), lambda i: (i, 0)),
        ],
        out_specs=[pl.BlockSpec((rows, step), lambda i: (0, i))] * 3,
        out_shape=[jax.ShapeDtypeStruct((rows, hidden), BF16)] * 3,
        cost_estimate=COST,
        name="mlp",
    )(normed, y_grad, weight, down)


def out_body(o_in, h_in, wo_in, wd_in, out):
    out[...] = (dot(o_in[...], wo_in[...]) + dot(h_in[...], wd_in[...])).astype(BF16)


def out_partial(o, h, out_weight, down, start, cols):
    rows, local = o.shape
    hidden = h.shape[1]
    step = min(512, cols)
    base = start // step
    return pl.pallas_call(
        out_body,
        grid=(cols // step,),
        in_specs=[
            pl.BlockSpec((rows, local), lambda i: (0, 0)),
            pl.BlockSpec((rows, hidden), lambda i: (0, 0)),
            pl.BlockSpec((local, step), lambda i: (0, base + i)),
            pl.BlockSpec((hidden, step), lambda i: (0, base + i)),
        ],
        out_specs=pl.BlockSpec((rows, step), lambda i: (0, i)),
        out_shape=jax.ShapeDtypeStruct((rows, cols), BF16),
        cost_estimate=COST,
        name="out_partial",
    )(o, h, out_weight, down)


def dxn_body(*refs):
    dq_in, dk_in, dv_in, dg_in, du_in = refs[:5]
    wqkv_in, w_in, x_in, stats_in, out, col_out = refs[5:]
    shift_sum = jnp.zeros((1, x_in.shape[1]), F32)
    gain_sum = jnp.zeros((1, x_in.shape[1]), F32)
    for start in range(0, x_in.shape[0], 256):
        span = slice(start, start + 256)
        total = dot(dq_in[span], wqkv_in[0], NT)
        total += dot(dk_in[span], wqkv_in[1], NT)
        total += dot(dv_in[span], wqkv_in[2], NT)
        total += dot(dg_in[span], w_in[0], NT)
        total += dot(du_in[span], w_in[1], NT)
        out[span] = total.astype(BF16)
        hat = (x_in[span].astype(F32) - stats_in[span, :1]) * stats_in[span, 1:]
        shift_sum += jnp.sum(total, axis=0, keepdims=True)
        gain_sum += jnp.sum(total * hat, axis=0, keepdims=True)
    col_out[...] = jnp.concatenate([gain_sum, shift_sum], axis=0)


def dxn_partial(dqkv, dg, du, wqkv, weight, x, stats, part):
    rows, hidden = dg.shape
    local, width = dqkv[0].shape[1], x.shape[1]
    step = min(256, width)
    whole = lambda a: pl.BlockSpec(a.shape, lambda i: (0,) * a.ndim)
    return pl.pallas_call(
        dxn_body,
        grid=(width // step,),
        in_specs=[pl.BlockSpec((rows, local), lambda i: (part, 0))] * 3
        + [
            whole(dg),
            whole(du),
            pl.BlockSpec((3, step, local), lambda i: (0, i, 0)),
            pl.BlockSpec((2, step, hidden), lambda i: (0, i, 0)),
            pl.BlockSpec((rows, step), lambda i: (part, i)),
            pl.BlockSpec((rows, 2), lambda i: (part, 0)),
        ],
        out_specs=[
            pl.BlockSpec((rows, step), lambda i: (0, i)),
            pl.BlockSpec((2, step), lambda i: (0, i)),
        ],
        out_shape=[
            jax.ShapeDtypeStruct((rows, width), BF16),
            jax.ShapeDtypeStruct((2, width), F32),
        ],
        cost_estimate=MARK if part else COST,
        name="dxn_partial",
    )(*dqkv, dg, du, wqkv, weight, x, stats)


def dw_sum(groups, lefts, rhs):
    position = 0
    for which, parts in groups:
        lhs = lefts[which]
        each = lhs.shape[0] // parts
        total = None
        for part in range(parts):
            piece = dot(lhs[part * each : (part + 1) * each], rhs[position][...], TN)
            total = piece if total is None else total + piece
            position += 1
        yield total


def dw_send_body(groups, order, *refs):
    *refs, out = refs
    number = len({which for which, _ in groups})
    start = 0
    for total in dw_sum(groups, refs[:number], refs[number:]):
        out[0, :, start : start + total.shape[1]] = total.astype(BF16)
        start += total.shape[1]


def dw_keep_body(groups, bundles, order, slots, *refs):
    number = len({which for which, _ in groups})
    lefts, refs = refs[:number], refs[number:]
    number = sum(parts for _, parts in groups)
    rhs, (received, *refs) = refs[:number], refs[number:]
    sends, keeps = refs[: len(bundles)], refs[len(bundles) :]
    step = pl.program_id(0)
    totals = dw_sum(groups, lefts, rhs)
    start = 0
    for number, bundle in enumerate(bundles):
        away = slots[3 * number, step] == 1
        pieces = []
        for _ in range(bundle):
            total = next(totals)
            stop = start + total.shape[1]
            pieces.append((total + received[0, :, start:stop].astype(F32)).astype(BF16))
            start = stop
        total = pieces[0] if bundle == 1 else jnp.concatenate(pieces, axis=1)

        @pl.when(away)
        def _(number=number, total=total):
            sends[number][0] = total

        @pl.when(jnp.logical_not(away))
        def _(number=number, total=total):
            keeps[number][0] = total


def dw_call(order, lefts, rhs, which, number, bundles, received=None, slots=None):
    count, width = lefts[0].shape
    step = width // (2 * number)
    groups = tuple((w, len(group)) for w, group in zip(which, rhs))
    flat = [part for group in rhs for part in group]
    columns = [group[0].shape[1] for group in rhs]
    scalars = [order] if slots is None else [order, slots]
    args = scalars + [*lefts, *flat]
    specs = [pl.BlockSpec((count, step), lambda i, order, *_: (0, order[i])) for _ in lefts]
    specs += [pl.BlockSpec(a.shape, lambda i, *_: (0, 0)) for a in flat]
    block = pl.BlockSpec((1, step, sum(columns)), lambda i, *_: (i, 0, 0))
    if received is None:
        body = functools.partial(dw_send_body, groups)
        out_specs = [block]
        shapes = [jax.ShapeDtypeStruct((number, step, sum(columns)), BF16)]
    else:
        body = functools.partial(dw_keep_body, groups, bundles)
        args.append(received)
        specs.append(block)
        ends = np.cumsum([0, *bundles])
        joined = [sum(columns[a:b]) for a, b in zip(ends, ends[1:])]
        out_specs = [
            pl.BlockSpec((1, step, c), lambda i, order, slots, r=3 * g + kind: (slots[r, i], 0, 0))
            for kind in (1, 2)
            for g, c in enumerate(joined)
        ]
        shapes = [jax.ShapeDtypeStruct((number // 2, step, c), BF16) for c in joined] * 2
    return pl.pallas_call(
        body,
        grid_spec=pltpu.PrefetchScalarGridSpec(
            num_scalar_prefetch=len(scalars), grid=(number,), in_specs=specs, out_specs=out_specs
        ),
        out_shape=shapes,
        cost_estimate=COST,
        name="weight_grad",
    )(*args)


def flip(size, bit):
    return [(i, i ^ bit) for i in range(size)]


class Order:
    def __init__(self):
        self.token = jnp.zeros((8, 128), F32)

    def __call__(self, function, *args):
        args, token = lax.optimization_barrier((args, self.token))
        out, self.token = lax.optimization_barrier((function(*args), token))
        return out

    def mark(self):
        self.token = mark(self.token)


def mark_body(seen, out):
    out[...] = seen[...]


def mark(seen):
    return pl.pallas_call(
        mark_body,
        out_shape=jax.ShapeDtypeStruct(seen.shape, seen.dtype),
        cost_estimate=MARK,
        name="mark",
    )(seen)


def after_body(value, seen, out):
    out[...] = value[...]


def after(value, seen):
    return pl.pallas_call(
        after_body,
        out_shape=jax.ShapeDtypeStruct(value.shape, value.dtype),
        cost_estimate=COST,
        name="after",
    )(value, seen)


def halving_order(bits):
    order = [0]
    for bit in reversed(bits):
        order = [offset ^ bit for offset in order] + order
    return order


class Scatter:
    def __init__(self, run, devices, lefts, rhs, which, bundles, swaps):
        self.run, self.devices, self.lefts, self.rhs = run, devices, lefts, rhs
        self.which, self.bundles = which, bundles
        bits = [1 << i for i in range(devices.bit_length() - 1)]
        self.offsets = halving_order(bits)
        self.order = lax.axis_index("dp").astype(jnp.int32) ^ jnp.asarray(self.offsets, jnp.int32)
        self.bits = []
        for swap in swaps:
            rest = bits[1:]
            if swap and len(rest) > 1:
                rest[0], rest[1] = rest[1], rest[0]
            self.bits.append(rest)

    def send(self):
        half = self.devices // 2
        call = lambda lefts, rhs: dw_call(
            self.order[:half], lefts, rhs, self.which, half, self.bundles
        )
        (sent,) = self.run(call, self.lefts, self.rhs)
        self.received = lax.ppermute(sent, "dp", flip(self.devices, 1))

    def keep(self):
        half = self.devices // 2
        kept = self.offsets[half:]
        rows, self.left = [], []
        for bits in self.bits:
            away = [int(offset & bits[0] != 0) for offset in kept]
            place = lambda flags: [max(0, sum(flags[: i + 1]) - 1) for i in range(half)]
            rows += [away, place(away), place([1 - a for a in away])]
            self.left.append([offset for offset in kept if not offset & bits[0]])
        slots = jnp.asarray(np.array(rows), jnp.int32)
        call = lambda lefts, rhs, received: dw_call(
            self.order[half:], lefts, rhs, self.which, half, self.bundles, received, slots
        )
        outs = self.run(call, self.lefts, self.rhs, self.received)
        number = len(self.bits)
        self.kept = outs[number:]
        self.received = [
            lax.ppermute(s, "dp", flip(self.devices, bits[0])) for s, bits in zip(outs, self.bits)
        ]
        self.stage = 1

    def next(self, cost=COST):
        rows = []
        for group, bits in enumerate(self.bits):
            bit = bits[self.stage]
            for away in (True, False):
                rows.append([i for i, o in enumerate(self.left[group]) if bool(o & bit) == away])
            self.left[group] = [o for o in self.left[group] if not o & bit]
        slots = jnp.asarray(np.array(rows), jnp.int32)
        call = lambda kept, received: next_call(kept, received, slots, len(rows[0]), cost)
        outs = self.run(call, self.kept, self.received)
        number = len(self.bits)
        self.kept = outs[number:]
        self.received = [
            lax.ppermute(s, "dp", flip(self.devices, bits[self.stage]))
            for s, bits in zip(outs, self.bits)
        ]
        self.stage += 1

    def last(self, pieces):
        while self.stage < len(self.bits[0]):
            self.next()
        call = lambda kept, received: last_call(kept, received, pieces)
        return self.run(call, self.kept, self.received)


def next_body(slots, *refs):
    number = len(refs) // 6
    for n in range(2 * number):
        pair, out = refs[2 * n : 2 * n + 2], refs[4 * number + n]
        out[0] = (pair[0][0].astype(F32) + pair[1][0].astype(F32)).astype(BF16)


def next_call(kept, received, slots, pieces, cost):
    rows = kept[0].shape[1]
    step = min(64, rows)
    args, specs, outs, shapes = [], [], [], []
    for away in (0, 1):
        for group, pair in enumerate(zip(kept, received)):
            columns = pair[0].shape[2]
            place = lambda i, j, slots, r=2 * group + away: (slots[r, i], j, 0)
            args += pair
            specs += [pl.BlockSpec((1, step, columns), place)] * 2
            outs.append(pl.BlockSpec((1, step, columns), lambda i, j, slots: (i, j, 0)))
            shapes.append(jax.ShapeDtypeStruct((pieces, rows, columns), BF16))
    return pl.pallas_call(
        next_body,
        grid_spec=pltpu.PrefetchScalarGridSpec(
            num_scalar_prefetch=1, grid=(pieces, rows // step), in_specs=specs, out_specs=outs
        ),
        out_shape=shapes,
        cost_estimate=cost,
        name="next",
    )(slots, *args)


def last_body(pieces, *refs):
    outs = iter(refs[2 * len(pieces) :])
    stacked = None
    place = 0
    for n, widths in enumerate(pieces):
        kept, received = refs[2 * n], refs[2 * n + 1]
        start = 0
        for width, turned in widths:
            span = slice(start, start + width)
            start += width
            total = kept[0, :, span].astype(F32) + received[0, :, span].astype(F32)
            if turned:
                next(outs)[...] = total.T
                continue
            stacked = next(outs) if stacked is None else stacked
            if stacked.shape[0] == total.shape[0]:
                stacked[:, place] = total
            else:
                stacked[place] = total
            place += 1


def last_call(kept, received, pieces):
    rows = kept[0].shape[1]
    step = min(128, rows)
    args, specs, outs, shapes, stacked = [], [], [], [], []
    for pair, widths in zip(zip(kept, received), pieces):
        args += pair
        specs += [pl.BlockSpec((1, step, pair[0].shape[2]), lambda i: (0, i, 0))] * 2
        for width, turned in widths:
            if turned:
                outs.append(pl.BlockSpec((width, step), lambda i: (0, i)))
                shapes.append(jax.ShapeDtypeStruct((width, rows), F32))
            else:
                stacked.append(width)
    if len(stacked) == 2:
        outs.append(pl.BlockSpec((step, 2, stacked[0]), lambda i: (i, 0, 0)))
        shapes.append(jax.ShapeDtypeStruct((rows, 2, stacked[0]), F32))
    elif stacked:
        outs.append(pl.BlockSpec((len(stacked), step, stacked[0]), lambda i: (0, i, 0)))
        shapes.append(jax.ShapeDtypeStruct((len(stacked), rows, stacked[0]), F32))
    return pl.pallas_call(
        functools.partial(last_body, pieces),
        grid=(rows // step,),
        in_specs=specs,
        out_specs=outs,
        out_shape=shapes,
        cost_estimate=COST,
        name="last",
    )(*args)


LINE = 4


def move_body(has, finish, inner, *refs):
    refs = iter(refs)
    partial, old, swapped, sum_, crossed = (next(refs) if given else None for given in has)
    *extra, send, total = refs if old is not None else (*refs, None)
    slab = 16

    def rows(i, carry):
        span = pl.ds(pl.multiple_of(i * slab, slab), slab)
        if old is not None:
            total[span] = (old[span].astype(F32) + swapped[span].astype(F32)).astype(BF16)
        added = sum_[span].astype(F32) + crossed[span].astype(F32)
        mine = finish(added, *(e[...] if e.shape[0] == 1 else e[span] for e in extra)).astype(BF16)
        if partial is not None:
            mine = jnp.where(inner[0] == 1, mine, partial[span])
        send[span] = mine
        return carry

    lax.fori_loop(0, send.shape[0] // slab, rows, 0, unroll=2)


def move_call(inner, arrays, finish, extra, part):
    has = [a is not None for a in arrays]
    given = [a for a in arrays if a is not None]
    rows, width = given[0].shape
    step = min(128, rows)
    base = part * (rows // step)
    fixed = lambda i, inner: jnp.where(inner[0] == 1, i, 0)

    def spec(a):
        if a.shape[0] == 1:
            return pl.BlockSpec(a.shape, lambda i, inner: (0, 0))
        return pl.BlockSpec((step, a.shape[1]), lambda i, inner: (base + fixed(i, inner), 0))

    block = pl.BlockSpec((step, width), lambda i, inner: (i, 0))
    in_block = pl.BlockSpec((step, width), lambda i, inner: (fixed(i, inner), 0))
    out_block = pl.BlockSpec((step, width), lambda i, inner: (jnp.where(inner[0] == 1, 0, i), 0))
    in_specs = [out_block if a is arrays[0] else in_block for a in given]
    number = 2 if has[1] else 1
    return pl.pallas_call(
        functools.partial(move_body, has, finish),
        grid_spec=pltpu.PrefetchScalarGridSpec(
            num_scalar_prefetch=1,
            grid=(rows // step,),
            in_specs=in_specs + [spec(a) for a in extra],
            out_specs=[block] * number,
        ),
        out_shape=[jax.ShapeDtypeStruct((rows, width), BF16)] * number,
        cost_estimate=COST,
        name="move",
    )(inner, *given, *extra)


class Lines:
    def __init__(self, run, size, number):
        self.run, self.size, self.number, self.stage = run, size, number, 0
        lines = range(0, size, LINE)
        self.inward = [(b, b + 1) for b in lines] + [(b + 3, b + 2) for b in lines]
        self.across = [(b + 1, b + 2) for b in lines] + [(b + 2, b + 1) for b in lines]
        self.outward = [(b + 1, b) for b in lines] + [(b + 2, b + 3) for b in lines]
        place = lax.axis_index("mp") % LINE
        self.inner = (place == 1) | (place == 2)
        self.flag = self.inner.astype(jnp.int32).reshape(1)
        self.partial = self.sum = self.crossed = self.swapped = None
        self.done = []

    def step(self, partial=None, finish=None, extra=(), part=0):
        stage, number = self.stage, self.number
        self.stage += 1

        def move(partial, old, swapped, sum_, crossed):
            if crossed is None:
                add = lambda a, b: (a.astype(F32) + b.astype(F32)).astype(BF16)
                return partial, None if old is None else add(old, swapped)
            bit = LINE
            while bit < self.size:
                sum_ = (sum_.astype(F32) + crossed.astype(F32)).astype(BF16)
                pairs = [(i, i ^ bit) for i in range(self.size) if i % LINE in (1, 2)]
                crossed = lax.ppermute(sum_, "mp", pairs)
                bit *= 2
            arrays = (partial, old, None if old is None else swapped, sum_, crossed)
            outs = move_call(self.flag, arrays, finish, extra, part)
            return outs if len(outs) == 2 else (outs[0], None)

        old = self.partial if 1 <= stage <= number else None
        crossed = self.crossed if 2 <= stage else None
        send, total = self.run(move, partial, old, self.swapped, self.sum, crossed)
        pairs = (self.inward if stage < number else []) + (self.outward if stage >= 2 else [])
        self.swapped = lax.ppermute(send, "mp", pairs)
        if total is not None:
            self.crossed = lax.ppermute(total, "mp", self.across)
        self.partial, self.sum = partial, total
        if stage >= 2:
            self.done.append((send, self.swapped))


def shards(
    dp,
    mp,
    inputs,
    segment_ids,
    pad_count,
    layer_norm_gain,
    layer_norm_bias,
    qkv_weight,
    qkv_bias,
    out_weight,
    gateup_weight,
    down_weight,
    y_grad,
):
    count, width = inputs.shape
    local = qkv_weight.shape[2]
    parts = 2
    rows = count // parts

    seg = segment_ids[0]
    steps = jnp.arange(count, dtype=jnp.int32)
    start = jnp.sum((seg[None, :] < seg[:, None]).astype(jnp.int32), axis=1)
    valid = steps < count - pad_count[0]
    low = jnp.where(valid, start, steps)[None, :]
    valid_row = valid.astype(F32)[None, :]
    lane = jnp.arange(128, dtype=jnp.int32) % HEAD_DIM
    half = ROT // 2
    freq = jnp.power(10000.0, -2.0 * (lane % half).astype(F32) / ROT)
    freq = jnp.where(lane < ROT, freq, 0.0)
    angle = (steps - start).astype(F32)[:, None] * freq[None, :]
    sign = jnp.where(lane < half, -1.0, 1.0)
    cosine = jnp.cos(angle)
    sine = jnp.sin(angle) * sign[None, :]

    xf = inputs.astype(F32)
    mean = jnp.mean(xf, axis=-1, keepdims=True)
    removed = xf - mean
    inv = lax.rsqrt(jnp.mean(removed * removed, axis=-1, keepdims=True) + EPS)
    normed = (removed * inv * layer_norm_gain + layer_norm_bias).astype(BF16)

    stats = jnp.concatenate([mean, inv], axis=1)

    wqkv = jnp.transpose(qkv_weight, (1, 0, 2))

    def cotangent(y_grad, out_weight):
        d_attn = lax.dot_general(y_grad, out_weight, NT, preferred_element_type=F32).astype(BF16)
        return d_attn * valid.astype(BF16)[:, None]

    run = Order()
    weight = run(lambda a: jnp.transpose(a, (1, 0, 2)), gateup_weight)
    lines = Lines(run, mp, 2 * parts)
    old = None
    qs, ks, vs, os, lses, hs, dgs, dus = ([] for _ in range(8))
    for part in range(parts):
        span = slice(part * rows, (part + 1) * rows)

        def attend(normed, old, span=span, part=part):
            tables = cosine[span], sine[span], low[:, span], valid_row[:, span]
            return attn_fwd(normed, wqkv, qkv_bias, *tables, old, part)

        q, k, v, o, lse = run(attend, normed, old)
        old = (k, v)
        h, dg, du = run(
            lambda *a, part=part: mlp(*a, part, parts), normed, y_grad, weight, down_weight
        )
        for stack, item in zip((qs, ks, vs, os, lses, hs, dgs, dus), (q, k, v, o, lse, h, dg, du)):
            stack.append(item)
        partial = run(lambda *a: out_partial(*a, 0, width), o, h, out_weight, down_weight)
        if part == parts - 1:
            d_attn = run(cotangent, y_grad, out_weight)
        lines.step(partial)

    def finish_out(total, x):
        return x.astype(F32) + total

    gateup = Scatter(run, dp, [normed], [dgs, dus], (0, 0), (1, 1), (False, True))

    def emit(part):
        call = lambda dqkv, dg, du: dxn_partial(
            dqkv, dg, du, wqkv, weight, inputs, stats, part
        )
        return run(call, dqkv, dgs[part], dus[part])

    def finish_grad(total, x, dy, stats, gain):
        mean, inv = stats[:, :1], stats[:, 1:]
        hat = (x.astype(F32) - mean) * inv
        scaled = total * gain
        average = jnp.mean(scaled, axis=1, keepdims=True)
        slope = jnp.mean(scaled * hat, axis=1, keepdims=True)
        return dy.astype(F32) + inv * (scaled - average - hat * slope)

    grad_extra = (inputs, y_grad, stats, layer_norm_gain[None, :])

    def store(target, part, mine, received):
        step = lambda target, mine, received: lax.dynamic_update_slice(
            target, jnp.where(lines.inner, mine, received), (part * rows, 0)
        )
        return run(step, target, mine, received)

    blank = jnp.zeros((count, width), BF16)
    hidden = down_weight.shape[0]
    *dqkv, bias_grad = run(lambda *a: attn_bwd(*a, cosine, sine, low), qs, ks, vs, lses, d_attn)
    rest = Scatter(
        run,
        dp,
        [y_grad, normed],
        [hs, os] + [[a] for a in dqkv],
        (0, 0, 1, 1, 1),
        (2, 3),
        (True, False),
    )
    partial, columns = emit(0)
    lines.step(partial, finish_out, (inputs,), 0)
    partial, columns1 = emit(1)

    def small_step(value, axis, bit):
        size = {"dp": dp, "mp": mp}[axis]
        return run(jnp.add, value, lax.ppermute(value, axis, flip(size, bit)))

    small = run(
        lambda a, b, c: jnp.concatenate([(a + b).reshape(-1), c.reshape(-1)]),
        columns,
        columns1,
        bias_grad,
    )
    small = small_step(small, "dp", 1)
    gateup.send()
    bit = 2
    while bit < dp // 2:
        small = small_step(small, "dp", bit)
        bit *= 2
    rest.send()
    while bit < dp:
        small = small_step(small, "dp", bit)
        bit *= 2
    column_sums = small[: 2 * width]
    bias_sum = small[2 * width :].reshape(bias_grad.shape)
    lines.step(partial, finish_out, (inputs,), 1)
    run.mark()
    gateup.keep()
    rest.keep()
    result = store(blank, 0, *lines.done[0])
    lines.step(None, finish_grad, grad_extra, 0)
    gateup.next(MARK)
    result = store(result, 1, *lines.done[1])
    rest.next()
    column_sums = small_step(column_sums, "mp", 1)
    lines.step(None, finish_grad, grad_extra, 1)
    x_grad = store(blank, 0, *lines.done[2])
    (gateup_grad,) = gateup.last((((hidden, False),), ((hidden, False),)))
    down_grad, out_grad, qkv_grad = rest.last(
        (((hidden, True), (local, True)), ((local, False),) * 3)
    )
    qkv_grad = jnp.transpose(qkv_grad, (1, 0, 2))
    bit = 2
    while bit < mp:
        column_sums = small_step(column_sums, "mp", bit)
        bit *= 2
    column_sums = column_sums.reshape(2, width)
    column_sums = after(column_sums, run.token)
    x_grad = store(x_grad, 1, *lines.done[3])
    return (
        result,
        x_grad,
        column_sums[0],
        column_sums[1],
        qkv_grad,
        bias_sum,
        out_grad,
        gateup_grad,
        down_grad,
    )


def solution(mesh):
    placed = (
        P("dp", None),
        P("dp", None),
        P("dp"),
        P(),
        P(),
        P(None, None, "mp"),
        P(None, "mp"),
        P("mp", None),
        P(None, None, "mp"),
        P("mp", None),
        P("dp", None),
    )
    return jax.shard_map(
        functools.partial(shards, mesh.shape["dp"], mesh.shape["mp"]),
        mesh=mesh,
        in_specs=placed,
        out_specs=(
            P("dp", None),
            P("dp", None),
            P(),
            P(),
            P("dp", None, "mp"),
            P(None, "mp"),
            P("mp", "dp"),
            P("dp", None, "mp"),
            P("mp", "dp"),
        ),
        check_vma=False,
    )
```

```python
import functools
import math

import jax
import jax.numpy as jnp
import numpy as np
from jax import lax
from jax.experimental import pallas as pl
from jax.experimental.pallas import tpu as pltpu
from jax.sharding import PartitionSpec as P

HEAD_DIM = 64
ROT = 16
DOCS = 4
DOC_MOST = 512
EPS = 1e-05
BQ = 256
LOG2E = math.log2(math.e)
SCALE2 = HEAD_DIM ** (-0.5) * LOG2E
F32 = jnp.float32
BF16 = jnp.bfloat16
NT = (((1,), (1,)), ((), ()))
TN = (((0,), (0,)), ((), ()))
COST = pl.CostEstimate(flops=1000, bytes_accessed=1000, transcendentals=0)
MARK = pl.CostEstimate(flops=10**12, bytes_accessed=10**9, transcendentals=0)


def dot(a, b, dims=(((1,), (0,)), ((), ()))):
    return lax.dot_general(a, b, dims, preferred_element_type=F32)


def turn(x, cosine, sine):
    lane = lax.broadcasted_iota(jnp.int32, x.shape, 1) % HEAD_DIM
    other = jnp.where(
        lane < ROT // 2, pltpu.roll(x, 128 - ROT // 2, 1), pltpu.roll(x, ROT // 2, 1)
    )
    return x * cosine + other * sine


def head_masks(x):
    low = lax.broadcasted_iota(jnp.int32, x.shape, 1) < HEAD_DIM
    zero = jnp.zeros_like(x)
    return (jnp.where(low, x, zero), jnp.where(low, zero, x))


def key_range(block):
    first = max(0, block - DOC_MOST // BQ)
    return first * BQ, (block + 1) * BQ


def masked_scores(keys, query, first, block, low_row):
    score = dot(keys, query, NT) * SCALE2
    before = score.shape[0] - BQ

    def mask(values, other):
        row = lax.broadcasted_iota(jnp.int32, (BQ, BQ), 0)
        column = lax.broadcasted_iota(jnp.int32, (BQ, BQ), 1)
        last = (row >= low_row - block * BQ) & (row <= column)
        pieces = [jnp.where(last, values[before:], other)]
        if before:
            row = lax.broadcasted_iota(jnp.int32, (before, BQ), 0)
            pieces.insert(0, jnp.where(row >= low_row - first, values[:before], other))
        return pieces[0] if len(pieces) == 1 else jnp.concatenate(pieces, axis=0)

    return score, mask


def attn_fwd_body(before, x_in, w_in, bias, cosine, sine, low, valid, *rest):
    if before:
        old_k, old_v, q_out, k_out, v_out, o_out, lse_out, k_all, vt_all = rest
    else:
        q_out, k_out, v_out, o_out, lse_out, k_all, vt_all = rest
    count = x_in.shape[0]
    qkv = dot(x_in[...], jnp.concatenate([w_in[0], w_in[1], w_in[2]], axis=1))
    cos_t, sin_t = cosine[...], sine[...]
    query = turn(qkv[:, :128] + bias[0:1], cos_t, sin_t).astype(BF16)
    key = turn(qkv[:, 128:256] + bias[1:2], cos_t, sin_t).astype(BF16)
    value = (qkv[:, 256:] + bias[2:3]).astype(BF16)
    q_out[...] = query
    k_out[...] = key
    v_out[...] = value
    if before:
        k_all[:before] = old_k[...]
        vt_all[:, :before] = old_v[...].T
    k_all[before:] = key
    vt_all[:, before:] = value.T
    for local in range(count // BQ):
        block = before // BQ + local
        first, last = key_range(block)
        span = slice(local * BQ, (local + 1) * BQ)
        low_row = low[:, span]
        outs = []
        for head, part in enumerate(head_masks(q_out[span])):
            score, mask = masked_scores(k_all[first:last], part, first, block, low_row)
            score = mask(score, -1e30)
            top = jnp.max(score, axis=0, keepdims=True)
            expo = jnp.exp2(score - top)
            total = jnp.sum(expo, axis=0, keepdims=True)
            prob = (expo * (1.0 / total)).astype(BF16)
            outs.append(dot(vt_all[:, first:last], prob))
            lse_out[0, head : head + 1, span] = top + jnp.log2(total)
        upper = lax.broadcasted_iota(jnp.int32, outs[0].shape, 0) < HEAD_DIM
        joined = jnp.where(upper, outs[0], outs[1]) * valid[:, span]
        o_out[span] = joined.T.astype(BF16)


def attn_fwd(normed, weight, bias, cosine, sine, low, valid, old, part):
    width, local = weight.shape[1:]
    count = cosine.shape[0]
    before = 0 if old is None else old[0].shape[0]
    pairs = local // 128
    row = lambda n: pl.BlockSpec((n, 128), lambda i: (0, i))
    whole = lambda a: pl.BlockSpec(a.shape, lambda i: (0,) * a.ndim)
    args = [normed, weight, bias, cosine, sine, low, valid] + ([] if old is None else list(old))
    specs = [
        pl.BlockSpec((count, width), lambda i: (part, 0)),
        pl.BlockSpec((3, width, 128), lambda i: (0, 0, i)),
        row(3),
        *map(whole, (cosine, sine, low, valid)),
    ]
    specs += [row(before)] * (0 if old is None else 2)
    flat = jax.ShapeDtypeStruct((count, local), BF16)
    return pl.pallas_call(
        functools.partial(attn_fwd_body, before),
        grid=(pairs,),
        in_specs=specs,
        out_specs=[row(count)] * 4 + [pl.BlockSpec((1, 2, count), lambda i: (i, 0, 0))],
        out_shape=[flat] * 4 + [jax.ShapeDtypeStruct((pairs, 2, count), F32)],
        scratch_shapes=[
            pltpu.VMEM((before + count, 128), BF16),
            pltpu.VMEM((128, before + count), BF16),
        ],
        cost_estimate=COST,
        name="attn_fwd",
    )(*args)


def attn_bwd_body(parts, *refs):
    qs, ks, vs = refs[:parts], refs[parts : 2 * parts], refs[2 * parts : 3 * parts]
    lses = refs[3 * parts : 4 * parts]
    do_in, cosine, sine, low, dq_out, dk_out, dv_out, bias_out, kt_all, dk_acc, dv_acc = refs[
        4 * parts :
    ]
    each = qs[0].shape[0]

    def rows(refs_of, first, last):
        pieces = []
        for part, ref in enumerate(refs_of):
            lo, hi = max(first, part * each), min(last, (part + 1) * each)
            if lo < hi:
                pieces.append(ref[lo - part * each : hi - part * each])
        return pieces[0] if len(pieces) == 1 else jnp.concatenate(pieces, axis=0)

    for part in range(parts):
        kt_all[:, part * each : (part + 1) * each] = ks[part][...].T
    dk_acc[...] = jnp.zeros_like(dk_acc)
    dv_acc[...] = jnp.zeros_like(dv_acc)
    sums = [jnp.zeros((1, 128), F32) for _ in range(3)]
    blocks = parts * each // BQ
    for block in range(blocks):
        first, last = key_range(block)
        span = slice(block * BQ, (block + 1) * BQ)
        low_row = low[:, span]
        part, inside = block * BQ // each, block * BQ % each
        queries = head_masks(rows(qs, span.start, span.stop))
        d_outs = head_masks(do_in[span])
        keys, values = rows(ks, first, last), rows(vs, first, last)
        probs, d_scores, d_queries = [], [], []
        for head in range(2):
            score, mask = masked_scores(keys, queries[head], first, block, low_row)
            lse = lses[part][0, head : head + 1, inside : inside + BQ]
            prob = mask(jnp.exp2(score - lse), 0.0)
            d_prob = dot(values, d_outs[head], NT)
            delta = jnp.sum(prob * d_prob, axis=0, keepdims=True)
            d_score = (prob * (d_prob - delta)).astype(BF16)
            probs.append(prob.astype(BF16))
            d_scores.append(d_score)
            d_queries.append(dot(kt_all[:, first:last], d_score))
        wide = slice(first, last)
        dv_acc[wide] += dot(jnp.concatenate(probs, 1), jnp.concatenate(d_outs, 0))
        dk_acc[wide] += dot(jnp.concatenate(d_scores, 1), jnp.concatenate(queries, 0))
        upper = lax.broadcasted_iota(jnp.int32, d_queries[0].shape, 0) < HEAD_DIM
        d_query = jnp.where(upper, d_queries[0], d_queries[1]).T * HEAD_DIM ** (-0.5)
        d_query = turn(d_query, cosine[span], -sine[span]).astype(BF16)
        dq_out[span] = d_query
        sums[0] += jnp.sum(d_query.astype(F32), axis=0, keepdims=True)
        done = [block - DOC_MOST // BQ] if block + 1 < blocks else range(block - DOC_MOST // BQ, blocks)
        for old in done:
            if old < 0:
                continue
            there = slice(old * BQ, (old + 1) * BQ)
            d_key = dk_acc[there] * HEAD_DIM ** (-0.5)
            d_key = turn(d_key, cosine[there], -sine[there]).astype(BF16)
            d_value = dv_acc[there].astype(BF16)
            dk_out[there] = d_key
            dv_out[there] = d_value
            sums[1] += jnp.sum(d_key.astype(F32), axis=0, keepdims=True)
            sums[2] += jnp.sum(d_value.astype(F32), axis=0, keepdims=True)
    bias_out[...] = jnp.concatenate(sums, axis=0)


def attn_bwd(qs, ks, vs, lses, d_out, cosine, sine, low):
    parts = len(qs)
    each, local = qs[0].shape
    count = parts * each
    row = lambda n: pl.BlockSpec((n, 128), lambda i: (0, i))
    whole = lambda a: pl.BlockSpec(a.shape, lambda i: (0,) * a.ndim)
    flat = jax.ShapeDtypeStruct((count, local), BF16)
    return pl.pallas_call(
        functools.partial(attn_bwd_body, parts),
        grid=(local // 128,),
        in_specs=[row(each)] * (3 * parts)
        + [pl.BlockSpec((1, 2, each), lambda i: (i, 0, 0))] * parts
        + [row(count), whole(cosine), whole(sine), whole(low)],
        out_specs=[row(count)] * 3 + [row(3)],
        out_shape=[flat] * 3 + [jax.ShapeDtypeStruct((3, local), F32)],
        scratch_shapes=[
            pltpu.VMEM((128, count), BF16),
            pltpu.VMEM((count, 128), F32),
            pltpu.VMEM((count, 128), F32),
        ],
        cost_estimate=MARK,
        name="attn_bwd",
    )(*qs, *ks, *vs, *lses, d_out, cosine, sine, low)


def mlp_body(x_in, dy_in, w_in, down_in, h_out, dg_out, du_out):
    for start in range(0, x_in.shape[0], 256):
        span = slice(start, start + 256)
        gate = dot(x_in[span], w_in[0])
        upper = dot(x_in[span], w_in[1])
        d_hidden = dot(dy_in[span], down_in[...], NT)
        sigma = jax.nn.sigmoid(gate)
        active = gate * sigma
        h_out[span] = (active * upper).astype(BF16)
        du_out[span] = (d_hidden * active).astype(BF16)
        dg_out[span] = (d_hidden * upper * sigma * (1.0 + gate * (1.0 - sigma))).astype(BF16)


def mlp(normed, y_grad, weight, down, part, parts):
    count, width = normed.shape
    rows = count // parts
    hidden = down.shape[0]
    step = min(256, hidden)
    fixed = pl.BlockSpec((rows, width), lambda i: (part, 0))
    return pl.pallas_call(
        mlp_body,
        grid=(pl.cdiv(hidden, step),),
        in_specs=[
            fixed,
            fixed,
            pl.BlockSpec((2, width, step), lambda i: (0, 0, i)),
            pl.BlockSpec((step, width), lambda i: (i, 0)),
        ],
        out_specs=[pl.BlockSpec((rows, step), lambda i: (0, i))] * 3,
        out_shape=[jax.ShapeDtypeStruct((rows, hidden), BF16)] * 3,
        cost_estimate=COST,
        name="mlp",
    )(normed, y_grad, weight, down)


def out_body(o_in, h_in, wo_in, wd_in, out):
    out[...] = (dot(o_in[...], wo_in[...]) + dot(h_in[...], wd_in[...])).astype(BF16)


def out_partial(o, h, out_weight, down, start, cols):
    rows, local = o.shape
    hidden = h.shape[1]
    step = min(512, cols)
    base = start // step
    return pl.pallas_call(
        out_body,
        grid=(cols // step,),
        in_specs=[
            pl.BlockSpec((rows, local), lambda i: (0, 0)),
            pl.BlockSpec((rows, hidden), lambda i: (0, 0)),
            pl.BlockSpec((local, step), lambda i: (0, base + i)),
            pl.BlockSpec((hidden, step), lambda i: (0, base + i)),
        ],
        out_specs=pl.BlockSpec((rows, step), lambda i: (0, i)),
        out_shape=jax.ShapeDtypeStruct((rows, cols), BF16),
        cost_estimate=COST,
        name="out_partial",
    )(o, h, out_weight, down)


def dxn_body(*refs):
    dq_in, dk_in, dv_in, dg_in, du_in = refs[:5]
    wqkv_in, w_in, x_in, stats_in, out, col_out = refs[5:]
    shift_sum = jnp.zeros((1, x_in.shape[1]), F32)
    gain_sum = jnp.zeros((1, x_in.shape[1]), F32)
    for start in range(0, x_in.shape[0], 256):
        span = slice(start, start + 256)
        total = dot(dq_in[span], wqkv_in[0], NT)
        total += dot(dk_in[span], wqkv_in[1], NT)
        total += dot(dv_in[span], wqkv_in[2], NT)
        total += dot(dg_in[span], w_in[0], NT)
        total += dot(du_in[span], w_in[1], NT)
        out[span] = total.astype(BF16)
        hat = (x_in[span].astype(F32) - stats_in[span, :1]) * stats_in[span, 1:]
        shift_sum += jnp.sum(total, axis=0, keepdims=True)
        gain_sum += jnp.sum(total * hat, axis=0, keepdims=True)
    col_out[...] = jnp.concatenate([gain_sum, shift_sum], axis=0)


def dxn_partial(dqkv, dg, du, wqkv, weight, x, stats, part):
    rows, hidden = dg.shape
    local, width = dqkv[0].shape[1], x.shape[1]
    step = min(256, width)
    whole = lambda a: pl.BlockSpec(a.shape, lambda i: (0,) * a.ndim)
    return pl.pallas_call(
        dxn_body,
        grid=(width // step,),
        in_specs=[pl.BlockSpec((rows, local), lambda i: (part, 0))] * 3
        + [
            whole(dg),
            whole(du),
            pl.BlockSpec((3, step, local), lambda i: (0, i, 0)),
            pl.BlockSpec((2, step, hidden), lambda i: (0, i, 0)),
            pl.BlockSpec((rows, step), lambda i: (part, i)),
            pl.BlockSpec((rows, 2), lambda i: (part, 0)),
        ],
        out_specs=[
            pl.BlockSpec((rows, step), lambda i: (0, i)),
            pl.BlockSpec((2, step), lambda i: (0, i)),
        ],
        out_shape=[
            jax.ShapeDtypeStruct((rows, width), BF16),
            jax.ShapeDtypeStruct((2, width), F32),
        ],
        cost_estimate=MARK if part else COST,
        name="dxn_partial",
    )(*dqkv, dg, du, wqkv, weight, x, stats)


def dw_sum(groups, lefts, rhs):
    position = 0
    for which, parts in groups:
        lhs = lefts[which]
        each = lhs.shape[0] // parts
        total = None
        for part in range(parts):
            piece = dot(lhs[part * each : (part + 1) * each], rhs[position][...], TN)
            total = piece if total is None else total + piece
            position += 1
        yield total


def dw_send_body(groups, order, *refs):
    *refs, out = refs
    number = len({which for which, _ in groups})
    start = 0
    for total in dw_sum(groups, refs[:number], refs[number:]):
        out[0, :, start : start + total.shape[1]] = total.astype(BF16)
        start += total.shape[1]


def dw_keep_body(groups, bundles, order, slots, *refs):
    number = len({which for which, _ in groups})
    lefts, refs = refs[:number], refs[number:]
    number = sum(parts for _, parts in groups)
    rhs, (received, *refs) = refs[:number], refs[number:]
    sends, keeps = refs[: len(bundles)], refs[len(bundles) :]
    step = pl.program_id(0)
    totals = dw_sum(groups, lefts, rhs)
    start = 0
    for number, bundle in enumerate(bundles):
        away = slots[3 * number, step] == 1
        pieces = []
        for _ in range(bundle):
            total = next(totals)
            stop = start + total.shape[1]
            pieces.append((total + received[0, :, start:stop].astype(F32)).astype(BF16))
            start = stop
        total = pieces[0] if bundle == 1 else jnp.concatenate(pieces, axis=1)

        @pl.when(away)
        def _(number=number, total=total):
            sends[number][0] = total

        @pl.when(jnp.logical_not(away))
        def _(number=number, total=total):
            keeps[number][0] = total


def dw_call(order, lefts, rhs, which, number, bundles, received=None, slots=None):
    count, width = lefts[0].shape
    step = width // (2 * number)
    groups = tuple((w, len(group)) for w, group in zip(which, rhs))
    flat = [part for group in rhs for part in group]
    columns = [group[0].shape[1] for group in rhs]
    scalars = [order] if slots is None else [order, slots]
    args = scalars + [*lefts, *flat]
    specs = [pl.BlockSpec((count, step), lambda i, order, *_: (0, order[i])) for _ in lefts]
    specs += [pl.BlockSpec(a.shape, lambda i, *_: (0, 0)) for a in flat]
    block = pl.BlockSpec((1, step, sum(columns)), lambda i, *_: (i, 0, 0))
    if received is None:
        body = functools.partial(dw_send_body, groups)
        out_specs = [block]
        shapes = [jax.ShapeDtypeStruct((number, step, sum(columns)), BF16)]
    else:
        body = functools.partial(dw_keep_body, groups, bundles)
        args.append(received)
        specs.append(block)
        ends = np.cumsum([0, *bundles])
        joined = [sum(columns[a:b]) for a, b in zip(ends, ends[1:])]
        out_specs = [
            pl.BlockSpec((1, step, c), lambda i, order, slots, r=3 * g + kind: (slots[r, i], 0, 0))
            for kind in (1, 2)
            for g, c in enumerate(joined)
        ]
        shapes = [jax.ShapeDtypeStruct((number // 2, step, c), BF16) for c in joined] * 2
    return pl.pallas_call(
        body,
        grid_spec=pltpu.PrefetchScalarGridSpec(
            num_scalar_prefetch=len(scalars), grid=(number,), in_specs=specs, out_specs=out_specs
        ),
        out_shape=shapes,
        cost_estimate=COST,
        name="weight_grad",
    )(*args)


def flip(size, bit):
    return [(i, i ^ bit) for i in range(size)]


class Order:
    def __init__(self):
        self.token = jnp.zeros((8, 128), F32)

    def __call__(self, function, *args):
        args, token = lax.optimization_barrier((args, self.token))
        out, self.token = lax.optimization_barrier((function(*args), token))
        return out

    def mark(self):
        self.token = mark(self.token)


def mark_body(seen, out):
    out[...] = seen[...]


def mark(seen):
    return pl.pallas_call(
        mark_body,
        out_shape=jax.ShapeDtypeStruct(seen.shape, seen.dtype),
        cost_estimate=MARK,
        name="mark",
    )(seen)


def after_body(value, seen, out):
    out[...] = value[...]


def after(value, seen):
    return pl.pallas_call(
        after_body,
        out_shape=jax.ShapeDtypeStruct(value.shape, value.dtype),
        cost_estimate=COST,
        name="after",
    )(value, seen)


def halving_order(bits):
    order = [0]
    for bit in reversed(bits):
        order = [offset ^ bit for offset in order] + order
    return order


class Scatter:
    def __init__(self, run, devices, lefts, rhs, which, bundles, swaps):
        self.run, self.devices, self.lefts, self.rhs = run, devices, lefts, rhs
        self.which, self.bundles = which, bundles
        bits = [1 << i for i in range(devices.bit_length() - 1)]
        self.offsets = halving_order(bits)
        self.order = lax.axis_index("dp").astype(jnp.int32) ^ jnp.asarray(self.offsets, jnp.int32)
        self.bits = []
        for swap in swaps:
            rest = bits[1:]
            if swap and len(rest) > 1:
                rest[0], rest[1] = rest[1], rest[0]
            self.bits.append(rest)

    def send(self):
        half = self.devices // 2
        call = lambda lefts, rhs: dw_call(
            self.order[:half], lefts, rhs, self.which, half, self.bundles
        )
        (sent,) = self.run(call, self.lefts, self.rhs)
        self.received = lax.ppermute(sent, "dp", flip(self.devices, 1))

    def keep(self):
        half = self.devices // 2
        kept = self.offsets[half:]
        rows, self.left = [], []
        for bits in self.bits:
            away = [int(offset & bits[0] != 0) for offset in kept]
            place = lambda flags: [max(0, sum(flags[: i + 1]) - 1) for i in range(half)]
            rows += [away, place(away), place([1 - a for a in away])]
            self.left.append([offset for offset in kept if not offset & bits[0]])
        slots = jnp.asarray(np.array(rows), jnp.int32)
        call = lambda lefts, rhs, received: dw_call(
            self.order[half:], lefts, rhs, self.which, half, self.bundles, received, slots
        )
        outs = self.run(call, self.lefts, self.rhs, self.received)
        number = len(self.bits)
        self.kept = outs[number:]
        self.received = [
            lax.ppermute(s, "dp", flip(self.devices, bits[0])) for s, bits in zip(outs, self.bits)
        ]
        self.stage = 1

    def next(self, cost=COST):
        rows = []
        for group, bits in enumerate(self.bits):
            bit = bits[self.stage]
            for away in (True, False):
                rows.append([i for i, o in enumerate(self.left[group]) if bool(o & bit) == away])
            self.left[group] = [o for o in self.left[group] if not o & bit]
        slots = jnp.asarray(np.array(rows), jnp.int32)
        call = lambda kept, received: next_call(kept, received, slots, len(rows[0]), cost)
        outs = self.run(call, self.kept, self.received)
        number = len(self.bits)
        self.kept = outs[number:]
        self.received = [
            lax.ppermute(s, "dp", flip(self.devices, bits[self.stage]))
            for s, bits in zip(outs, self.bits)
        ]
        self.stage += 1

    def last(self, pieces):
        while self.stage < len(self.bits[0]):
            self.next()
        call = lambda kept, received: last_call(kept, received, pieces)
        return self.run(call, self.kept, self.received)


def next_body(slots, *refs):
    number = len(refs) // 6
    for n in range(2 * number):
        pair, out = refs[2 * n : 2 * n + 2], refs[4 * number + n]
        out[0] = (pair[0][0].astype(F32) + pair[1][0].astype(F32)).astype(BF16)


def next_call(kept, received, slots, pieces, cost):
    rows = kept[0].shape[1]
    step = min(64, rows)
    args, specs, outs, shapes = [], [], [], []
    for away in (0, 1):
        for group, pair in enumerate(zip(kept, received)):
            columns = pair[0].shape[2]
            place = lambda i, j, slots, r=2 * group + away: (slots[r, i], j, 0)
            args += pair
            specs += [pl.BlockSpec((1, step, columns), place)] * 2
            outs.append(pl.BlockSpec((1, step, columns), lambda i, j, slots: (i, j, 0)))
            shapes.append(jax.ShapeDtypeStruct((pieces, rows, columns), BF16))
    return pl.pallas_call(
        next_body,
        grid_spec=pltpu.PrefetchScalarGridSpec(
            num_scalar_prefetch=1, grid=(pieces, rows // step), in_specs=specs, out_specs=outs
        ),
        out_shape=shapes,
        cost_estimate=cost,
        name="next",
    )(slots, *args)


def last_body(pieces, *refs):
    outs = iter(refs[2 * len(pieces) :])
    stacked = None
    place = 0
    for n, widths in enumerate(pieces):
        kept, received = refs[2 * n], refs[2 * n + 1]
        start = 0
        for width, turned in widths:
            span = slice(start, start + width)
            start += width
            total = kept[0, :, span].astype(F32) + received[0, :, span].astype(F32)
            if turned:
                next(outs)[...] = total.T
                continue
            stacked = next(outs) if stacked is None else stacked
            if stacked.shape[0] == total.shape[0]:
                stacked[:, place] = total
            else:
                stacked[place] = total
            place += 1


def last_call(kept, received, pieces):
    rows = kept[0].shape[1]
    step = min(128, rows)
    args, specs, outs, shapes, stacked = [], [], [], [], []
    for pair, widths in zip(zip(kept, received), pieces):
        args += pair
        specs += [pl.BlockSpec((1, step, pair[0].shape[2]), lambda i: (0, i, 0))] * 2
        for width, turned in widths:
            if turned:
                outs.append(pl.BlockSpec((width, step), lambda i: (0, i)))
                shapes.append(jax.ShapeDtypeStruct((width, rows), F32))
            else:
                stacked.append(width)
    if len(stacked) == 2:
        outs.append(pl.BlockSpec((step, 2, stacked[0]), lambda i: (i, 0, 0)))
        shapes.append(jax.ShapeDtypeStruct((rows, 2, stacked[0]), F32))
    elif stacked:
        outs.append(pl.BlockSpec((len(stacked), step, stacked[0]), lambda i: (0, i, 0)))
        shapes.append(jax.ShapeDtypeStruct((len(stacked), rows, stacked[0]), F32))
    return pl.pallas_call(
        functools.partial(last_body, pieces),
        grid=(rows // step,),
        in_specs=specs,
        out_specs=outs,
        out_shape=shapes,
        cost_estimate=COST,
        name="last",
    )(*args)


LINE = 4


def move_body(has, finish, inner, *refs):
    refs = iter(refs)
    partial, old, swapped, sum_, crossed = (next(refs) if given else None for given in has)
    *extra, send, total = refs if old is not None else (*refs, None)
    slab = 16

    def rows(i, carry):
        span = pl.ds(pl.multiple_of(i * slab, slab), slab)
        if old is not None:
            total[span] = (old[span].astype(F32) + swapped[span].astype(F32)).astype(BF16)
        added = sum_[span].astype(F32) + crossed[span].astype(F32)
        mine = finish(added, *(e[...] if e.shape[0] == 1 else e[span] for e in extra)).astype(BF16)
        if partial is not None:
            mine = jnp.where(inner[0] == 1, mine, partial[span])
        send[span] = mine
        return carry

    lax.fori_loop(0, send.shape[0] // slab, rows, 0, unroll=2)


def move_call(inner, arrays, finish, extra, part):
    has = [a is not None for a in arrays]
    given = [a for a in arrays if a is not None]
    rows, width = given[0].shape
    step = min(128, rows)
    base = part * (rows // step)
    fixed = lambda i, inner: jnp.where(inner[0] == 1, i, 0)

    def spec(a):
        if a.shape[0] == 1:
            return pl.BlockSpec(a.shape, lambda i, inner: (0, 0))
        return pl.BlockSpec((step, a.shape[1]), lambda i, inner: (base + fixed(i, inner), 0))

    block = pl.BlockSpec((step, width), lambda i, inner: (i, 0))
    in_block = pl.BlockSpec((step, width), lambda i, inner: (fixed(i, inner), 0))
    out_block = pl.BlockSpec((step, width), lambda i, inner: (jnp.where(inner[0] == 1, 0, i), 0))
    in_specs = [out_block if a is arrays[0] else in_block for a in given]
    number = 2 if has[1] else 1
    return pl.pallas_call(
        functools.partial(move_body, has, finish),
        grid_spec=pltpu.PrefetchScalarGridSpec(
            num_scalar_prefetch=1,
            grid=(rows // step,),
            in_specs=in_specs + [spec(a) for a in extra],
            out_specs=[block] * number,
        ),
        out_shape=[jax.ShapeDtypeStruct((rows, width), BF16)] * number,
        cost_estimate=COST,
        name="move",
    )(inner, *given, *extra)


class Lines:
    def __init__(self, run, size, number):
        self.run, self.size, self.number, self.stage = run, size, number, 0
        lines = range(0, size, LINE)
        self.inward = [(b, b + 1) for b in lines] + [(b + 3, b + 2) for b in lines]
        self.across = [(b + 1, b + 2) for b in lines] + [(b + 2, b + 1) for b in lines]
        self.outward = [(b + 1, b) for b in lines] + [(b + 2, b + 3) for b in lines]
        place = lax.axis_index("mp") % LINE
        self.inner = (place == 1) | (place == 2)
        self.flag = self.inner.astype(jnp.int32).reshape(1)
        self.partial = self.sum = self.crossed = self.swapped = None
        self.done = []

    def step(self, partial=None, finish=None, extra=(), part=0):
        stage, number = self.stage, self.number
        self.stage += 1

        def move(partial, old, swapped, sum_, crossed):
            if crossed is None:
                add = lambda a, b: (a.astype(F32) + b.astype(F32)).astype(BF16)
                return partial, None if old is None else add(old, swapped)
            bit = LINE
            while bit < self.size:
                sum_ = (sum_.astype(F32) + crossed.astype(F32)).astype(BF16)
                pairs = [(i, i ^ bit) for i in range(self.size) if i % LINE in (1, 2)]
                crossed = lax.ppermute(sum_, "mp", pairs)
                bit *= 2
            arrays = (partial, old, None if old is None else swapped, sum_, crossed)
            outs = move_call(self.flag, arrays, finish, extra, part)
            return outs if len(outs) == 2 else (outs[0], None)

        old = self.partial if 1 <= stage <= number else None
        crossed = self.crossed if 2 <= stage else None
        send, total = self.run(move, partial, old, self.swapped, self.sum, crossed)
        pairs = (self.inward if stage < number else []) + (self.outward if stage >= 2 else [])
        self.swapped = lax.ppermute(send, "mp", pairs)
        if total is not None:
            self.crossed = lax.ppermute(total, "mp", self.across)
        self.partial, self.sum = partial, total
        if stage >= 2:
            self.done.append((send, self.swapped))


def shards(
    dp,
    mp,
    inputs,
    segment_ids,
    pad_count,
    layer_norm_gain,
    layer_norm_bias,
    qkv_weight,
    qkv_bias,
    out_weight,
    gateup_weight,
    down_weight,
    y_grad,
):
    count, width = inputs.shape
    local = qkv_weight.shape[2]
    parts = 2
    rows = count // parts

    seg = segment_ids[0]
    steps = jnp.arange(count, dtype=jnp.int32)
    start = jnp.sum((seg[None, :] < seg[:, None]).astype(jnp.int32), axis=1)
    valid = steps < count - pad_count[0]
    low = jnp.where(valid, start, steps)[None, :]
    valid_row = valid.astype(F32)[None, :]
    lane = jnp.arange(128, dtype=jnp.int32) % HEAD_DIM
    half = ROT // 2
    freq = jnp.power(10000.0, -2.0 * (lane % half).astype(F32) / ROT)
    freq = jnp.where(lane < ROT, freq, 0.0)
    angle = (steps - start).astype(F32)[:, None] * freq[None, :]
    sign = jnp.where(lane < half, -1.0, 1.0)
    cosine = jnp.cos(angle)
    sine = jnp.sin(angle) * sign[None, :]

    xf = inputs.astype(F32)
    mean = jnp.mean(xf, axis=-1, keepdims=True)
    removed = xf - mean
    inv = lax.rsqrt(jnp.mean(removed * removed, axis=-1, keepdims=True) + EPS)
    normed = (removed * inv * layer_norm_gain + layer_norm_bias).astype(BF16)

    stats = jnp.concatenate([mean, inv], axis=1)

    wqkv = jnp.transpose(qkv_weight, (1, 0, 2))

    def cotangent(y_grad, out_weight):
        d_attn = lax.dot_general(y_grad, out_weight, NT, preferred_element_type=F32).astype(BF16)
        return d_attn * valid.astype(BF16)[:, None]

    run = Order()
    tables = (normed, cosine, sine, low, valid_row)
    weight, tables = run(
        lambda a, tables: (jnp.transpose(a, (1, 0, 2)), tables), gateup_weight, tables
    )
    normed, cosine, sine, low, valid_row = tables
    lines = Lines(run, mp, 2 * parts)
    old = None
    qs, ks, vs, os, lses, hs, dgs, dus = ([] for _ in range(8))
    for part in range(parts):
        span = slice(part * rows, (part + 1) * rows)

        def attend(normed, old, span=span, part=part):
            tables = cosine[span], sine[span], low[:, span], valid_row[:, span]
            return attn_fwd(normed, wqkv, qkv_bias, *tables, old, part)

        q, k, v, o, lse = run(attend, normed, old)
        old = (k, v)
        h, dg, du = run(
            lambda *a, part=part: mlp(*a, part, parts), normed, y_grad, weight, down_weight
        )
        for stack, item in zip((qs, ks, vs, os, lses, hs, dgs, dus), (q, k, v, o, lse, h, dg, du)):
            stack.append(item)
        partial = run(lambda *a: out_partial(*a, 0, width), o, h, out_weight, down_weight)
        if part == parts - 1:
            d_attn = run(cotangent, y_grad, out_weight)
        lines.step(partial)

    def finish_out(total, x):
        return x.astype(F32) + total

    gateup = Scatter(run, dp, [normed], [dgs, dus], (0, 0), (1, 1), (False, True))

    def emit(part):
        call = lambda dqkv, dg, du: dxn_partial(
            dqkv, dg, du, wqkv, weight, inputs, stats, part
        )
        return run(call, dqkv, dgs[part], dus[part])

    def finish_grad(total, x, dy, stats, gain):
        mean, inv = stats[:, :1], stats[:, 1:]
        hat = (x.astype(F32) - mean) * inv
        scaled = total * gain
        average = jnp.mean(scaled, axis=1, keepdims=True)
        slope = jnp.mean(scaled * hat, axis=1, keepdims=True)
        return dy.astype(F32) + inv * (scaled - average - hat * slope)

    grad_extra = (inputs, y_grad, stats, layer_norm_gain[None, :])

    def store(target, part, mine, received):
        step = lambda target, mine, received: lax.dynamic_update_slice(
            target, jnp.where(lines.inner, mine, received), (part * rows, 0)
        )
        return run(step, target, mine, received)

    blank = jnp.zeros((count, width), BF16)
    hidden = down_weight.shape[0]
    *dqkv, bias_grad = run(lambda *a: attn_bwd(*a, cosine, sine, low), qs, ks, vs, lses, d_attn)
    rest = Scatter(
        run,
        dp,
        [y_grad, normed],
        [hs, os] + [[a] for a in dqkv],
        (0, 0, 1, 1, 1),
        (2, 3),
        (True, False),
    )
    partial, columns = emit(0)
    lines.step(partial, finish_out, (inputs,), 0)
    partial, columns1 = emit(1)

    def small_step(value, axis, bit):
        size = {"dp": dp, "mp": mp}[axis]
        return run(jnp.add, value, lax.ppermute(value, axis, flip(size, bit)))

    small = run(
        lambda a, b, c: jnp.concatenate([(a + b).reshape(-1), c.reshape(-1)]),
        columns,
        columns1,
        bias_grad,
    )
    small = small_step(small, "dp", 1)
    gateup.send()
    bit = 2
    while bit < dp // 2:
        small = small_step(small, "dp", bit)
        bit *= 2
    rest.send()
    while bit < dp:
        small = small_step(small, "dp", bit)
        bit *= 2
    column_sums = small[: 2 * width]
    bias_sum = small[2 * width :].reshape(bias_grad.shape)
    lines.step(partial, finish_out, (inputs,), 1)
    run.mark()
    gateup.keep()
    rest.keep()
    result = store(blank, 0, *lines.done[0])
    lines.step(None, finish_grad, grad_extra, 0)
    gateup.next(MARK)
    result = store(result, 1, *lines.done[1])
    rest.next()
    column_sums = small_step(column_sums, "mp", 1)
    lines.step(None, finish_grad, grad_extra, 1)
    x_grad = store(blank, 0, *lines.done[2])
    (gateup_grad,) = gateup.last((((hidden, False),), ((hidden, False),)))
    down_grad, out_grad, qkv_grad = rest.last(
        (((hidden, True), (local, True)), ((local, False),) * 3)
    )
    qkv_grad = jnp.transpose(qkv_grad, (1, 0, 2))
    bit = 2
    while bit < mp:
        column_sums = small_step(column_sums, "mp", bit)
        bit *= 2
    column_sums = column_sums.reshape(2, width)
    column_sums = after(column_sums, run.token)
    x_grad = store(x_grad, 1, *lines.done[3])
    return (
        result,
        x_grad,
        column_sums[0],
        column_sums[1],
        qkv_grad,
        bias_sum,
        out_grad,
        gateup_grad,
        down_grad,
    )


def solution(mesh):
    placed = (
        P("dp", None),
        P("dp", None),
        P("dp"),
        P(),
        P(),
        P(None, None, "mp"),
        P(None, "mp"),
        P("mp", None),
        P(None, None, "mp"),
        P("mp", None),
        P("dp", None),
    )
    return jax.shard_map(
        functools.partial(shards, mesh.shape["dp"], mesh.shape["mp"]),
        mesh=mesh,
        in_specs=placed,
        out_specs=(
            P("dp", None),
            P("dp", None),
            P(),
            P(),
            P("dp", None, "mp"),
            P(None, "mp"),
            P("mp", "dp"),
            P("dp", None, "mp"),
            P("mp", "dp"),
        ),
        check_vma=False,
    )
```

```python
import functools
import math

import jax
import jax.numpy as jnp
import numpy as np
from jax import lax
from jax.experimental import pallas as pl
from jax.experimental.pallas import tpu as pltpu
from jax.sharding import PartitionSpec as P

HEAD_DIM = 64
ROT = 16
DOCS = 4
DOC_MOST = 512
EPS = 1e-05
BQ = 256
LOG2E = math.log2(math.e)
SCALE2 = HEAD_DIM ** (-0.5) * LOG2E
F32 = jnp.float32
BF16 = jnp.bfloat16
NT = (((1,), (1,)), ((), ()))
TN = (((0,), (0,)), ((), ()))
COST = pl.CostEstimate(flops=1000, bytes_accessed=1000, transcendentals=0)
MARK = pl.CostEstimate(flops=10**12, bytes_accessed=10**9, transcendentals=0)


def dot(a, b, dims=(((1,), (0,)), ((), ()))):
    return lax.dot_general(a, b, dims, preferred_element_type=F32)


def turn(x, cosine, sine):
    lane = lax.broadcasted_iota(jnp.int32, x.shape, 1) % HEAD_DIM
    other = jnp.where(
        lane < ROT // 2, pltpu.roll(x, 128 - ROT // 2, 1), pltpu.roll(x, ROT // 2, 1)
    )
    return x * cosine + other * sine


def head_masks(x):
    low = lax.broadcasted_iota(jnp.int32, x.shape, 1) < HEAD_DIM
    zero = jnp.zeros_like(x)
    return (jnp.where(low, x, zero), jnp.where(low, zero, x))


def key_range(block):
    first = max(0, block - DOC_MOST // BQ)
    return first * BQ, (block + 1) * BQ


def masked_scores(keys, query, first, block, low_row):
    score = dot(keys, query, NT) * SCALE2
    before = score.shape[0] - BQ

    def mask(values, other):
        row = lax.broadcasted_iota(jnp.int32, (BQ, BQ), 0)
        column = lax.broadcasted_iota(jnp.int32, (BQ, BQ), 1)
        last = (row >= low_row - block * BQ) & (row <= column)
        pieces = [jnp.where(last, values[before:], other)]
        if before:
            row = lax.broadcasted_iota(jnp.int32, (before, BQ), 0)
            pieces.insert(0, jnp.where(row >= low_row - first, values[:before], other))
        return pieces[0] if len(pieces) == 1 else jnp.concatenate(pieces, axis=0)

    return score, mask


def attn_fwd_body(before, x_in, w_in, bias, cosine, sine, low, valid, *rest):
    if before:
        old_k, old_v, q_out, k_out, v_out, o_out, lse_out, k_all, vt_all = rest
    else:
        q_out, k_out, v_out, o_out, lse_out, k_all, vt_all = rest
    count = x_in.shape[0]
    qkv = dot(x_in[...], jnp.concatenate([w_in[0], w_in[1], w_in[2]], axis=1))
    cos_t, sin_t = cosine[...], sine[...]
    query = turn(qkv[:, :128] + bias[0:1], cos_t, sin_t).astype(BF16)
    key = turn(qkv[:, 128:256] + bias[1:2], cos_t, sin_t).astype(BF16)
    value = (qkv[:, 256:] + bias[2:3]).astype(BF16)
    q_out[...] = query
    k_out[...] = key
    v_out[...] = value
    if before:
        k_all[:before] = old_k[...]
        vt_all[:, :before] = old_v[...].T
    k_all[before:] = key
    vt_all[:, before:] = value.T
    for local in range(count // BQ):
        block = before // BQ + local
        first, last = key_range(block)
        span = slice(local * BQ, (local + 1) * BQ)
        low_row = low[:, span]
        outs = []
        for head, part in enumerate(head_masks(q_out[span])):
            score, mask = masked_scores(k_all[first:last], part, first, block, low_row)
            score = mask(score, -1e30)
            top = jnp.max(score, axis=0, keepdims=True)
            expo = jnp.exp2(score - top)
            total = jnp.sum(expo, axis=0, keepdims=True)
            prob = (expo * (1.0 / total)).astype(BF16)
            outs.append(dot(vt_all[:, first:last], prob))
            lse_out[0, head : head + 1, span] = top + jnp.log2(total)
        upper = lax.broadcasted_iota(jnp.int32, outs[0].shape, 0) < HEAD_DIM
        joined = jnp.where(upper, outs[0], outs[1]) * valid[:, span]
        o_out[span] = joined.T.astype(BF16)


def attn_fwd(normed, weight, bias, cosine, sine, low, valid, old, part):
    width, local = weight.shape[1:]
    count = cosine.shape[0]
    before = 0 if old is None else old[0].shape[0]
    pairs = local // 128
    row = lambda n: pl.BlockSpec((n, 128), lambda i: (0, i))
    whole = lambda a: pl.BlockSpec(a.shape, lambda i: (0,) * a.ndim)
    args = [normed, weight, bias, cosine, sine, low, valid] + ([] if old is None else list(old))
    specs = [
        pl.BlockSpec((count, width), lambda i: (part, 0)),
        pl.BlockSpec((3, width, 128), lambda i: (0, 0, i)),
        row(3),
        *map(whole, (cosine, sine, low, valid)),
    ]
    specs += [row(before)] * (0 if old is None else 2)
    flat = jax.ShapeDtypeStruct((count, local), BF16)
    return pl.pallas_call(
        functools.partial(attn_fwd_body, before),
        grid=(pairs,),
        in_specs=specs,
        out_specs=[row(count)] * 4 + [pl.BlockSpec((1, 2, count), lambda i: (i, 0, 0))],
        out_shape=[flat] * 4 + [jax.ShapeDtypeStruct((pairs, 2, count), F32)],
        scratch_shapes=[
            pltpu.VMEM((before + count, 128), BF16),
            pltpu.VMEM((128, before + count), BF16),
        ],
        cost_estimate=COST,
        name="attn_fwd",
    )(*args)


def attn_bwd_body(parts, *refs):
    qs, ks, vs = refs[:parts], refs[parts : 2 * parts], refs[2 * parts : 3 * parts]
    lses = refs[3 * parts : 4 * parts]
    do_in, cosine, sine, low, dq_out, dk_out, dv_out, bias_out, kt_all, dk_acc, dv_acc = refs[
        4 * parts :
    ]
    each = qs[0].shape[0]

    def rows(refs_of, first, last):
        pieces = []
        for part, ref in enumerate(refs_of):
            lo, hi = max(first, part * each), min(last, (part + 1) * each)
            if lo < hi:
                pieces.append(ref[lo - part * each : hi - part * each])
        return pieces[0] if len(pieces) == 1 else jnp.concatenate(pieces, axis=0)

    for part in range(parts):
        kt_all[:, part * each : (part + 1) * each] = ks[part][...].T
    dk_acc[...] = jnp.zeros_like(dk_acc)
    dv_acc[...] = jnp.zeros_like(dv_acc)
    sums = [jnp.zeros((1, 128), F32) for _ in range(3)]
    blocks = parts * each // BQ
    for block in range(blocks):
        first, last = key_range(block)
        span = slice(block * BQ, (block + 1) * BQ)
        low_row = low[:, span]
        part, inside = block * BQ // each, block * BQ % each
        queries = head_masks(rows(qs, span.start, span.stop))
        d_outs = head_masks(do_in[span])
        keys, values = rows(ks, first, last), rows(vs, first, last)
        probs, d_scores, d_queries = [], [], []
        for head in range(2):
            score, mask = masked_scores(keys, queries[head], first, block, low_row)
            lse = lses[part][0, head : head + 1, inside : inside + BQ]
            prob = mask(jnp.exp2(score - lse), 0.0)
            d_prob = dot(values, d_outs[head], NT)
            delta = jnp.sum(prob * d_prob, axis=0, keepdims=True)
            d_score = (prob * (d_prob - delta)).astype(BF16)
            probs.append(prob.astype(BF16))
            d_scores.append(d_score)
            d_queries.append(dot(kt_all[:, first:last], d_score))
        wide = slice(first, last)
        dv_acc[wide] += dot(jnp.concatenate(probs, 1), jnp.concatenate(d_outs, 0))
        dk_acc[wide] += dot(jnp.concatenate(d_scores, 1), jnp.concatenate(queries, 0))
        upper = lax.broadcasted_iota(jnp.int32, d_queries[0].shape, 0) < HEAD_DIM
        d_query = jnp.where(upper, d_queries[0], d_queries[1]).T * HEAD_DIM ** (-0.5)
        d_query = turn(d_query, cosine[span], -sine[span]).astype(BF16)
        dq_out[span] = d_query
        sums[0] += jnp.sum(d_query.astype(F32), axis=0, keepdims=True)
        done = [block - DOC_MOST // BQ] if block + 1 < blocks else range(block - DOC_MOST // BQ, blocks)
        for old in done:
            if old < 0:
                continue
            there = slice(old * BQ, (old + 1) * BQ)
            d_key = dk_acc[there] * HEAD_DIM ** (-0.5)
            d_key = turn(d_key, cosine[there], -sine[there]).astype(BF16)
            d_value = dv_acc[there].astype(BF16)
            dk_out[there] = d_key
            dv_out[there] = d_value
            sums[1] += jnp.sum(d_key.astype(F32), axis=0, keepdims=True)
            sums[2] += jnp.sum(d_value.astype(F32), axis=0, keepdims=True)
    bias_out[...] = jnp.concatenate(sums, axis=0)


def attn_bwd(qs, ks, vs, lses, d_out, cosine, sine, low):
    parts = len(qs)
    each, local = qs[0].shape
    count = parts * each
    row = lambda n: pl.BlockSpec((n, 128), lambda i: (0, i))
    whole = lambda a: pl.BlockSpec(a.shape, lambda i: (0,) * a.ndim)
    flat = jax.ShapeDtypeStruct((count, local), BF16)
    return pl.pallas_call(
        functools.partial(attn_bwd_body, parts),
        grid=(local // 128,),
        in_specs=[row(each)] * (3 * parts)
        + [pl.BlockSpec((1, 2, each), lambda i: (i, 0, 0))] * parts
        + [row(count), whole(cosine), whole(sine), whole(low)],
        out_specs=[row(count)] * 3 + [row(3)],
        out_shape=[flat] * 3 + [jax.ShapeDtypeStruct((3, local), F32)],
        scratch_shapes=[
            pltpu.VMEM((128, count), BF16),
            pltpu.VMEM((count, 128), F32),
            pltpu.VMEM((count, 128), F32),
        ],
        cost_estimate=MARK,
        name="attn_bwd",
    )(*qs, *ks, *vs, *lses, d_out, cosine, sine, low)


def mlp_body(x_in, dy_in, w_in, down_in, h_out, dg_out, du_out):
    for start in range(0, x_in.shape[0], 256):
        span = slice(start, start + 256)
        gate = dot(x_in[span], w_in[0])
        upper = dot(x_in[span], w_in[1])
        d_hidden = dot(dy_in[span], down_in[...], NT)
        sigma = jax.nn.sigmoid(gate)
        active = gate * sigma
        h_out[span] = (active * upper).astype(BF16)
        du_out[span] = (d_hidden * active).astype(BF16)
        dg_out[span] = (d_hidden * upper * sigma * (1.0 + gate * (1.0 - sigma))).astype(BF16)


def mlp(normed, y_grad, weight, down, part, parts):
    count, width = normed.shape
    rows = count // parts
    hidden = down.shape[0]
    step = min(256, hidden)
    fixed = pl.BlockSpec((rows, width), lambda i: (part, 0))
    return pl.pallas_call(
        mlp_body,
        grid=(pl.cdiv(hidden, step),),
        in_specs=[
            fixed,
            fixed,
            pl.BlockSpec((2, width, step), lambda i: (0, 0, i)),
            pl.BlockSpec((step, width), lambda i: (i, 0)),
        ],
        out_specs=[pl.BlockSpec((rows, step), lambda i: (0, i))] * 3,
        out_shape=[jax.ShapeDtypeStruct((rows, hidden), BF16)] * 3,
        cost_estimate=COST,
        name="mlp",
    )(normed, y_grad, weight, down)


def out_body(o_in, h_in, wo_in, wd_in, out):
    out[...] = (dot(o_in[...], wo_in[...]) + dot(h_in[...], wd_in[...])).astype(BF16)


def out_partial(o, h, out_weight, down, start, cols):
    rows, local = o.shape
    hidden = h.shape[1]
    step = min(512, cols)
    base = start // step
    return pl.pallas_call(
        out_body,
        grid=(cols // step,),
        in_specs=[
            pl.BlockSpec((rows, local), lambda i: (0, 0)),
            pl.BlockSpec((rows, hidden), lambda i: (0, 0)),
            pl.BlockSpec((local, step), lambda i: (0, base + i)),
            pl.BlockSpec((hidden, step), lambda i: (0, base + i)),
        ],
        out_specs=pl.BlockSpec((rows, step), lambda i: (0, i)),
        out_shape=jax.ShapeDtypeStruct((rows, cols), BF16),
        cost_estimate=COST,
        name="out_partial",
    )(o, h, out_weight, down)


def dxn_body(*refs):
    dq_in, dk_in, dv_in, dg_in, du_in = refs[:5]
    wqkv_in, w_in, x_in, stats_in, out, col_out = refs[5:]
    shift_sum = jnp.zeros((1, x_in.shape[1]), F32)
    gain_sum = jnp.zeros((1, x_in.shape[1]), F32)
    for start in range(0, x_in.shape[0], 256):
        span = slice(start, start + 256)
        total = dot(dq_in[span], wqkv_in[0], NT)
        total += dot(dk_in[span], wqkv_in[1], NT)
        total += dot(dv_in[span], wqkv_in[2], NT)
        total += dot(dg_in[span], w_in[0], NT)
        total += dot(du_in[span], w_in[1], NT)
        out[span] = total.astype(BF16)
        hat = (x_in[span].astype(F32) - stats_in[span, :1]) * stats_in[span, 1:]
        shift_sum += jnp.sum(total, axis=0, keepdims=True)
        gain_sum += jnp.sum(total * hat, axis=0, keepdims=True)
    col_out[...] = jnp.concatenate([gain_sum, shift_sum], axis=0)


def dxn_partial(dqkv, dg, du, wqkv, weight, x, stats, part):
    rows, hidden = dg.shape
    local, width = dqkv[0].shape[1], x.shape[1]
    step = min(512, width)
    whole = lambda a: pl.BlockSpec(a.shape, lambda i: (0,) * a.ndim)
    return pl.pallas_call(
        dxn_body,
        grid=(width // step,),
        in_specs=[pl.BlockSpec((rows, local), lambda i: (part, 0))] * 3
        + [
            whole(dg),
            whole(du),
            pl.BlockSpec((3, step, local), lambda i: (0, i, 0)),
            pl.BlockSpec((2, step, hidden), lambda i: (0, i, 0)),
            pl.BlockSpec((rows, step), lambda i: (part, i)),
            pl.BlockSpec((rows, 2), lambda i: (part, 0)),
        ],
        out_specs=[
            pl.BlockSpec((rows, step), lambda i: (0, i)),
            pl.BlockSpec((2, step), lambda i: (0, i)),
        ],
        out_shape=[
            jax.ShapeDtypeStruct((rows, width), BF16),
            jax.ShapeDtypeStruct((2, width), F32),
        ],
        cost_estimate=MARK if part else COST,
        name="dxn_partial",
    )(*dqkv, dg, du, wqkv, weight, x, stats)


def dw_sum(groups, lefts, rhs):
    position = 0
    for which, parts in groups:
        lhs = lefts[which]
        each = lhs.shape[0] // parts
        total = None
        for part in range(parts):
            piece = dot(lhs[part * each : (part + 1) * each], rhs[position][...], TN)
            total = piece if total is None else total + piece
            position += 1
        yield total


def dw_send_body(groups, order, *refs):
    *refs, out = refs
    number = len({which for which, _ in groups})
    start = 0
    for total in dw_sum(groups, refs[:number], refs[number:]):
        out[0, :, start : start + total.shape[1]] = total.astype(BF16)
        start += total.shape[1]


def dw_keep_body(groups, bundles, order, slots, *refs):
    number = len({which for which, _ in groups})
    lefts, refs = refs[:number], refs[number:]
    number = sum(parts for _, parts in groups)
    rhs, (received, *refs) = refs[:number], refs[number:]
    sends, keeps = refs[: len(bundles)], refs[len(bundles) :]
    step = pl.program_id(0)
    totals = dw_sum(groups, lefts, rhs)
    start = 0
    for number, bundle in enumerate(bundles):
        away = slots[3 * number, step] == 1
        pieces = []
        for _ in range(bundle):
            total = next(totals)
            stop = start + total.shape[1]
            pieces.append((total + received[0, :, start:stop].astype(F32)).astype(BF16))
            start = stop
        total = pieces[0] if bundle == 1 else jnp.concatenate(pieces, axis=1)

        @pl.when(away)
        def _(number=number, total=total):
            sends[number][0] = total

        @pl.when(jnp.logical_not(away))
        def _(number=number, total=total):
            keeps[number][0] = total


def dw_call(order, lefts, rhs, which, number, bundles, received=None, slots=None):
    count, width = lefts[0].shape
    step = width // (2 * number)
    groups = tuple((w, len(group)) for w, group in zip(which, rhs))
    flat = [part for group in rhs for part in group]
    columns = [group[0].shape[1] for group in rhs]
    scalars = [order] if slots is None else [order, slots]
    args = scalars + [*lefts, *flat]
    specs = [pl.BlockSpec((count, step), lambda i, order, *_: (0, order[i])) for _ in lefts]
    specs += [pl.BlockSpec(a.shape, lambda i, *_: (0, 0)) for a in flat]
    block = pl.BlockSpec((1, step, sum(columns)), lambda i, *_: (i, 0, 0))
    if received is None:
        body = functools.partial(dw_send_body, groups)
        out_specs = [block]
        shapes = [jax.ShapeDtypeStruct((number, step, sum(columns)), BF16)]
    else:
        body = functools.partial(dw_keep_body, groups, bundles)
        args.append(received)
        specs.append(block)
        ends = np.cumsum([0, *bundles])
        joined = [sum(columns[a:b]) for a, b in zip(ends, ends[1:])]
        out_specs = [
            pl.BlockSpec((1, step, c), lambda i, order, slots, r=3 * g + kind: (slots[r, i], 0, 0))
            for kind in (1, 2)
            for g, c in enumerate(joined)
        ]
        shapes = [jax.ShapeDtypeStruct((number // 2, step, c), BF16) for c in joined] * 2
    return pl.pallas_call(
        body,
        grid_spec=pltpu.PrefetchScalarGridSpec(
            num_scalar_prefetch=len(scalars), grid=(number,), in_specs=specs, out_specs=out_specs
        ),
        out_shape=shapes,
        cost_estimate=COST,
        name="weight_grad",
    )(*args)


def flip(size, bit):
    return [(i, i ^ bit) for i in range(size)]


class Order:
    def __init__(self):
        self.token = jnp.zeros((8, 128), F32)

    def __call__(self, function, *args):
        args, token = lax.optimization_barrier((args, self.token))
        out, self.token = lax.optimization_barrier((function(*args), token))
        return out

    def mark(self):
        self.token = mark(self.token)


def mark_body(seen, out):
    out[...] = seen[...]


def mark(seen):
    return pl.pallas_call(
        mark_body,
        out_shape=jax.ShapeDtypeStruct(seen.shape, seen.dtype),
        cost_estimate=MARK,
        name="mark",
    )(seen)


def after_body(value, seen, out):
    out[...] = value[...]


def after(value, seen):
    return pl.pallas_call(
        after_body,
        out_shape=jax.ShapeDtypeStruct(value.shape, value.dtype),
        cost_estimate=COST,
        name="after",
    )(value, seen)


def halving_order(bits):
    order = [0]
    for bit in reversed(bits):
        order = [offset ^ bit for offset in order] + order
    return order


class Scatter:
    def __init__(self, run, devices, lefts, rhs, which, bundles, swaps):
        self.run, self.devices, self.lefts, self.rhs = run, devices, lefts, rhs
        self.which, self.bundles = which, bundles
        bits = [1 << i for i in range(devices.bit_length() - 1)]
        self.offsets = halving_order(bits)
        self.order = lax.axis_index("dp").astype(jnp.int32) ^ jnp.asarray(self.offsets, jnp.int32)
        self.bits = []
        for swap in swaps:
            rest = bits[1:]
            if swap and len(rest) > 1:
                rest[0], rest[1] = rest[1], rest[0]
            self.bits.append(rest)

    def send(self):
        half = self.devices // 2
        call = lambda lefts, rhs: dw_call(
            self.order[:half], lefts, rhs, self.which, half, self.bundles
        )
        (sent,) = self.run(call, self.lefts, self.rhs)
        self.received = lax.ppermute(sent, "dp", flip(self.devices, 1))

    def keep(self):
        half = self.devices // 2
        kept = self.offsets[half:]
        rows, self.left = [], []
        for bits in self.bits:
            away = [int(offset & bits[0] != 0) for offset in kept]
            place = lambda flags: [max(0, sum(flags[: i + 1]) - 1) for i in range(half)]
            rows += [away, place(away), place([1 - a for a in away])]
            self.left.append([offset for offset in kept if not offset & bits[0]])
        slots = jnp.asarray(np.array(rows), jnp.int32)
        call = lambda lefts, rhs, received: dw_call(
            self.order[half:], lefts, rhs, self.which, half, self.bundles, received, slots
        )
        outs = self.run(call, self.lefts, self.rhs, self.received)
        number = len(self.bits)
        self.kept = outs[number:]
        self.received = [
            lax.ppermute(s, "dp", flip(self.devices, bits[0])) for s, bits in zip(outs, self.bits)
        ]
        self.stage = 1

    def next(self, cost=COST):
        rows = []
        for group, bits in enumerate(self.bits):
            bit = bits[self.stage]
            for away in (True, False):
                rows.append([i for i, o in enumerate(self.left[group]) if bool(o & bit) == away])
            self.left[group] = [o for o in self.left[group] if not o & bit]
        slots = jnp.asarray(np.array(rows), jnp.int32)
        call = lambda kept, received: next_call(kept, received, slots, len(rows[0]), cost)
        outs = self.run(call, self.kept, self.received)
        number = len(self.bits)
        self.kept = outs[number:]
        self.received = [
            lax.ppermute(s, "dp", flip(self.devices, bits[self.stage]))
            for s, bits in zip(outs, self.bits)
        ]
        self.stage += 1

    def last(self, pieces):
        while self.stage < len(self.bits[0]):
            self.next()
        call = lambda kept, received: last_call(kept, received, pieces)
        return self.run(call, self.kept, self.received)


def next_body(slots, *refs):
    number = len(refs) // 6
    for n in range(2 * number):
        pair, out = refs[2 * n : 2 * n + 2], refs[4 * number + n]
        out[0] = (pair[0][0].astype(F32) + pair[1][0].astype(F32)).astype(BF16)


def next_call(kept, received, slots, pieces, cost):
    rows = kept[0].shape[1]
    step = min(64, rows)
    args, specs, outs, shapes = [], [], [], []
    for away in (0, 1):
        for group, pair in enumerate(zip(kept, received)):
            columns = pair[0].shape[2]
            place = lambda i, j, slots, r=2 * group + away: (slots[r, i], j, 0)
            args += pair
            specs += [pl.BlockSpec((1, step, columns), place)] * 2
            outs.append(pl.BlockSpec((1, step, columns), lambda i, j, slots: (i, j, 0)))
            shapes.append(jax.ShapeDtypeStruct((pieces, rows, columns), BF16))
    return pl.pallas_call(
        next_body,
        grid_spec=pltpu.PrefetchScalarGridSpec(
            num_scalar_prefetch=1, grid=(pieces, rows // step), in_specs=specs, out_specs=outs
        ),
        out_shape=shapes,
        cost_estimate=cost,
        name="next",
    )(slots, *args)


def last_body(pieces, *refs):
    outs = iter(refs[2 * len(pieces) :])
    stacked = None
    place = 0
    for n, widths in enumerate(pieces):
        kept, received = refs[2 * n], refs[2 * n + 1]
        start = 0
        for width, turned in widths:
            span = slice(start, start + width)
            start += width
            total = kept[0, :, span].astype(F32) + received[0, :, span].astype(F32)
            if turned:
                next(outs)[...] = total.T
                continue
            stacked = next(outs) if stacked is None else stacked
            if stacked.shape[0] == total.shape[0]:
                stacked[:, place] = total
            else:
                stacked[place] = total
            place += 1


def last_call(kept, received, pieces):
    rows = kept[0].shape[1]
    step = min(128, rows)
    args, specs, outs, shapes, stacked = [], [], [], [], []
    for pair, widths in zip(zip(kept, received), pieces):
        args += pair
        specs += [pl.BlockSpec((1, step, pair[0].shape[2]), lambda i: (0, i, 0))] * 2
        for width, turned in widths:
            if turned:
                outs.append(pl.BlockSpec((width, step), lambda i: (0, i)))
                shapes.append(jax.ShapeDtypeStruct((width, rows), F32))
            else:
                stacked.append(width)
    if len(stacked) == 2:
        outs.append(pl.BlockSpec((step, 2, stacked[0]), lambda i: (i, 0, 0)))
        shapes.append(jax.ShapeDtypeStruct((rows, 2, stacked[0]), F32))
    elif stacked:
        outs.append(pl.BlockSpec((len(stacked), step, stacked[0]), lambda i: (0, i, 0)))
        shapes.append(jax.ShapeDtypeStruct((len(stacked), rows, stacked[0]), F32))
    return pl.pallas_call(
        functools.partial(last_body, pieces),
        grid=(rows // step,),
        in_specs=specs,
        out_specs=outs,
        out_shape=shapes,
        cost_estimate=COST,
        name="last",
    )(*args)


LINE = 4


def move_body(has, finish, inner, *refs):
    refs = iter(refs)
    partial, old, swapped, sum_, crossed = (next(refs) if given else None for given in has)
    refs = list(refs)
    total = refs.pop() if old is not None else None
    send = refs.pop() if crossed is not None else None
    extra = refs
    slab = 16

    def rows(i, carry):
        span = pl.ds(pl.multiple_of(i * slab, slab), slab)
        if old is not None:
            total[span] = (old[span].astype(F32) + swapped[span].astype(F32)).astype(BF16)
        if crossed is None:
            return carry
        added = sum_[span].astype(F32) + crossed[span].astype(F32)
        mine = finish(added, *(e[...] if e.shape[0] == 1 else e[span] for e in extra)).astype(BF16)
        if partial is not None:
            mine = jnp.where(inner[0] == 1, mine, partial[span])
        send[span] = mine
        return carry

    lax.fori_loop(0, (total if send is None else send).shape[0] // slab, rows, 0, unroll=2)


def move_call(inner, arrays, finish, extra, part):
    has = [a is not None for a in arrays]
    given = [a for a in arrays if a is not None]
    rows, width = given[0].shape
    step = min(128, rows)
    base = part * (rows // step)
    fixed = lambda i, inner: jnp.where(inner[0] == 1, i, 0)

    def spec(a):
        if a.shape[0] == 1:
            return pl.BlockSpec(a.shape, lambda i, inner: (0, 0))
        return pl.BlockSpec((step, a.shape[1]), lambda i, inner: (base + fixed(i, inner), 0))

    block = pl.BlockSpec((step, width), lambda i, inner: (i, 0))
    in_block = pl.BlockSpec((step, width), lambda i, inner: (fixed(i, inner), 0))
    out_block = pl.BlockSpec((step, width), lambda i, inner: (jnp.where(inner[0] == 1, 0, i), 0))
    in_specs = [out_block if a is arrays[0] else in_block for a in given]
    number = has[1] + has[4]
    return pl.pallas_call(
        functools.partial(move_body, has, finish),
        grid_spec=pltpu.PrefetchScalarGridSpec(
            num_scalar_prefetch=1,
            grid=(rows // step,),
            in_specs=in_specs + [spec(a) for a in extra],
            out_specs=[block] * number,
        ),
        out_shape=[jax.ShapeDtypeStruct((rows, width), BF16)] * number,
        cost_estimate=COST,
        name="move",
    )(inner, *given, *extra)


class Lines:
    def __init__(self, run, size, number):
        self.run, self.size, self.number, self.stage = run, size, number, 0
        lines = range(0, size, LINE)
        self.inward = [(b, b + 1) for b in lines] + [(b + 3, b + 2) for b in lines]
        self.across = [(b + 1, b + 2) for b in lines] + [(b + 2, b + 1) for b in lines]
        self.outward = [(b + 1, b) for b in lines] + [(b + 2, b + 3) for b in lines]
        place = lax.axis_index("mp") % LINE
        self.inner = (place == 1) | (place == 2)
        self.flag = self.inner.astype(jnp.int32).reshape(1)
        self.partial = self.sum = self.crossed = self.swapped = None
        self.done = []

    def step(self, partial=None, finish=None, extra=(), part=0):
        stage, number = self.stage, self.number
        self.stage += 1

        def move(partial, old, swapped, sum_, crossed):
            if crossed is None:
                if old is None:
                    return partial, None
                return partial, *move_call(self.flag, (None, old, swapped, None, None), None, (), 0)
            bit = LINE
            while bit < self.size:
                sum_ = (sum_.astype(F32) + crossed.astype(F32)).astype(BF16)
                pairs = [(i, i ^ bit) for i in range(self.size) if i % LINE in (1, 2)]
                crossed = lax.ppermute(sum_, "mp", pairs)
                bit *= 2
            arrays = (partial, old, None if old is None else swapped, sum_, crossed)
            outs = move_call(self.flag, arrays, finish, extra, part)
            return outs if len(outs) == 2 else (outs[0], None)

        old = self.partial if 1 <= stage <= number else None
        crossed = self.crossed if 2 <= stage else None
        send, total = self.run(move, partial, old, self.swapped, self.sum, crossed)
        pairs = (self.inward if stage < number else []) + (self.outward if stage >= 2 else [])
        self.swapped = lax.ppermute(send, "mp", pairs)
        if total is not None:
            self.crossed = lax.ppermute(total, "mp", self.across)
        self.partial, self.sum = partial, total
        if stage >= 2:
            self.done.append((send, self.swapped))


def shards(
    dp,
    mp,
    inputs,
    segment_ids,
    pad_count,
    layer_norm_gain,
    layer_norm_bias,
    qkv_weight,
    qkv_bias,
    out_weight,
    gateup_weight,
    down_weight,
    y_grad,
):
    count, width = inputs.shape
    local = qkv_weight.shape[2]
    parts = 2
    rows = count // parts

    seg = segment_ids[0]
    steps = jnp.arange(count, dtype=jnp.int32)
    start = jnp.sum((seg[None, :] < seg[:, None]).astype(jnp.int32), axis=1)
    valid = steps < count - pad_count[0]
    low = jnp.where(valid, start, steps)[None, :]
    valid_row = valid.astype(F32)[None, :]
    lane = jnp.arange(128, dtype=jnp.int32) % HEAD_DIM
    half = ROT // 2
    freq = jnp.power(10000.0, -2.0 * (lane % half).astype(F32) / ROT)
    freq = jnp.where(lane < ROT, freq, 0.0)
    angle = (steps - start).astype(F32)[:, None] * freq[None, :]
    sign = jnp.where(lane < half, -1.0, 1.0)
    cosine = jnp.cos(angle)
    sine = jnp.sin(angle) * sign[None, :]

    xf = inputs.astype(F32)
    mean = jnp.mean(xf, axis=-1, keepdims=True)
    removed = xf - mean
    inv = lax.rsqrt(jnp.mean(removed * removed, axis=-1, keepdims=True) + EPS)
    normed = (removed * inv * layer_norm_gain + layer_norm_bias).astype(BF16)

    stats = jnp.concatenate([mean, inv], axis=1)

    wqkv = jnp.transpose(qkv_weight, (1, 0, 2))

    def cotangent(y_grad, out_weight):
        d_attn = lax.dot_general(y_grad, out_weight, NT, preferred_element_type=F32).astype(BF16)
        return d_attn * valid.astype(BF16)[:, None]

    run = Order()
    tables = (normed, cosine, sine, low, valid_row)
    weight, tables = run(
        lambda a, tables: (jnp.transpose(a, (1, 0, 2)), tables), gateup_weight, tables
    )
    normed, cosine, sine, low, valid_row = tables
    lines = Lines(run, mp, 2 * parts)
    old = None
    qs, ks, vs, os, lses, hs, dgs, dus = ([] for _ in range(8))
    for part in range(parts):
        span = slice(part * rows, (part + 1) * rows)

        def attend(normed, old, span=span, part=part):
            tables = cosine[span], sine[span], low[:, span], valid_row[:, span]
            return attn_fwd(normed, wqkv, qkv_bias, *tables, old, part)

        q, k, v, o, lse = run(attend, normed, old)
        old = (k, v)
        h, dg, du = run(
            lambda *a, part=part: mlp(*a, part, parts), normed, y_grad, weight, down_weight
        )
        for stack, item in zip((qs, ks, vs, os, lses, hs, dgs, dus), (q, k, v, o, lse, h, dg, du)):
            stack.append(item)
        partial = run(lambda *a: out_partial(*a, 0, width), o, h, out_weight, down_weight)
        if part == parts - 1:
            d_attn = run(cotangent, y_grad, out_weight)
        lines.step(partial)

    def finish_out(total, x):
        return x.astype(F32) + total

    gateup = Scatter(run, dp, [normed], [dgs, dus], (0, 0), (1, 1), (False, True))

    def emit(part):
        call = lambda dqkv, dg, du: dxn_partial(
            dqkv, dg, du, wqkv, weight, inputs, stats, part
        )
        return run(call, dqkv, dgs[part], dus[part])

    def finish_grad(total, x, dy, stats, gain):
        mean, inv = stats[:, :1], stats[:, 1:]
        hat = (x.astype(F32) - mean) * inv
        scaled = total * gain
        average = jnp.mean(scaled, axis=1, keepdims=True)
        slope = jnp.mean(scaled * hat, axis=1, keepdims=True)
        return dy.astype(F32) + inv * (scaled - average - hat * slope)

    grad_extra = (inputs, y_grad, stats, layer_norm_gain[None, :])

    def store(target, part, mine, received):
        step = lambda target, mine, received: lax.dynamic_update_slice(
            target, jnp.where(lines.inner, mine, received), (part * rows, 0)
        )
        return run(step, target, mine, received)

    blank = jnp.zeros((count, width), BF16)
    hidden = down_weight.shape[0]
    *dqkv, bias_grad = run(lambda *a: attn_bwd(*a, cosine, sine, low), qs, ks, vs, lses, d_attn)
    rest = Scatter(
        run,
        dp,
        [y_grad, normed],
        [hs, os] + [[a] for a in dqkv],
        (0, 0, 1, 1, 1),
        (2, 3),
        (True, False),
    )
    partial, columns = emit(0)
    lines.step(partial, finish_out, (inputs,), 0)
    partial, columns1 = emit(1)

    def small_step(value, axis, bit):
        size = {"dp": dp, "mp": mp}[axis]
        return run(jnp.add, value, lax.ppermute(value, axis, flip(size, bit)))

    small = run(
        lambda a, b, c: jnp.concatenate([(a + b).reshape(-1), c.reshape(-1)]),
        columns,
        columns1,
        bias_grad,
    )
    small = small_step(small, "dp", 1)
    gateup.send()
    bit = 2
    while bit < dp // 2:
        small = small_step(small, "dp", bit)
        bit *= 2
    rest.send()
    while bit < dp:
        small = small_step(small, "dp", bit)
        bit *= 2
    column_sums = small[: 2 * width]
    bias_sum = small[2 * width :].reshape(bias_grad.shape)
    lines.step(partial, finish_out, (inputs,), 1)
    run.mark()
    gateup.keep()
    rest.keep()
    result = store(blank, 0, *lines.done[0])
    lines.step(None, finish_grad, grad_extra, 0)
    gateup.next(MARK)
    result = store(result, 1, *lines.done[1])
    rest.next()
    column_sums = small_step(column_sums, "mp", 1)
    lines.step(None, finish_grad, grad_extra, 1)
    x_grad = store(blank, 0, *lines.done[2])
    (gateup_grad,) = gateup.last((((hidden, False),), ((hidden, False),)))
    down_grad, out_grad, qkv_grad = rest.last(
        (((hidden, True), (local, True)), ((local, False),) * 3)
    )
    qkv_grad = jnp.transpose(qkv_grad, (1, 0, 2))
    bit = 2
    while bit < mp:
        column_sums = small_step(column_sums, "mp", bit)
        bit *= 2
    column_sums = column_sums.reshape(2, width)
    column_sums = after(column_sums, run.token)
    x_grad = store(x_grad, 1, *lines.done[3])
    return (
        result,
        x_grad,
        column_sums[0],
        column_sums[1],
        qkv_grad,
        bias_sum,
        out_grad,
        gateup_grad,
        down_grad,
    )


def solution(mesh):
    placed = (
        P("dp", None),
        P("dp", None),
        P("dp"),
        P(),
        P(),
        P(None, None, "mp"),
        P(None, "mp"),
        P("mp", None),
        P(None, None, "mp"),
        P("mp", None),
        P("dp", None),
    )
    return jax.shard_map(
        functools.partial(shards, mesh.shape["dp"], mesh.shape["mp"]),
        mesh=mesh,
        in_specs=placed,
        out_specs=(
            P("dp", None),
            P("dp", None),
            P(),
            P(),
            P("dp", None, "mp"),
            P(None, "mp"),
            P("mp", "dp"),
            P("dp", None, "mp"),
            P("mp", "dp"),
        ),
        check_vma=False,
    )
```

```python
import functools
import math

import jax
import jax.numpy as jnp
import numpy as np
from jax import lax
from jax.experimental import pallas as pl
from jax.experimental.pallas import tpu as pltpu
from jax.sharding import PartitionSpec as P

HEAD_DIM = 64
ROT = 16
DOCS = 4
DOC_MOST = 512
EPS = 1e-05
BQ = 256
LOG2E = math.log2(math.e)
SCALE2 = HEAD_DIM ** (-0.5) * LOG2E
F32 = jnp.float32
BF16 = jnp.bfloat16
NT = (((1,), (1,)), ((), ()))
TN = (((0,), (0,)), ((), ()))
COST = pl.CostEstimate(flops=1000, bytes_accessed=1000, transcendentals=0)
MARK = pl.CostEstimate(flops=10**12, bytes_accessed=10**9, transcendentals=0)


def dot(a, b, dims=(((1,), (0,)), ((), ()))):
    return lax.dot_general(a, b, dims, preferred_element_type=F32)


def turn(x, cosine, sine):
    lane = lax.broadcasted_iota(jnp.int32, x.shape, 1) % HEAD_DIM
    other = jnp.where(
        lane < ROT // 2, pltpu.roll(x, 128 - ROT // 2, 1), pltpu.roll(x, ROT // 2, 1)
    )
    return x * cosine + other * sine


def head_masks(x):
    low = lax.broadcasted_iota(jnp.int32, x.shape, 1) < HEAD_DIM
    zero = jnp.zeros_like(x)
    return (jnp.where(low, x, zero), jnp.where(low, zero, x))


def key_range(block):
    first = max(0, block - DOC_MOST // BQ)
    return first * BQ, (block + 1) * BQ


def masked_scores(keys, query, first, block, low_row):
    score = dot(keys, query, NT) * SCALE2
    before = score.shape[0] - BQ

    def mask(values, other):
        row = lax.broadcasted_iota(jnp.int32, (BQ, BQ), 0)
        column = lax.broadcasted_iota(jnp.int32, (BQ, BQ), 1)
        last = (row >= low_row - block * BQ) & (row <= column)
        pieces = [jnp.where(last, values[before:], other)]
        if before:
            row = lax.broadcasted_iota(jnp.int32, (before, BQ), 0)
            pieces.insert(0, jnp.where(row >= low_row - first, values[:before], other))
        return pieces[0] if len(pieces) == 1 else jnp.concatenate(pieces, axis=0)

    return score, mask


def attn_fwd_body(before, x_in, w_in, bias, cosine, sine, low, valid, *rest):
    if before:
        old_k, old_v, q_out, k_out, v_out, o_out, lse_out, k_all, vt_all = rest
    else:
        q_out, k_out, v_out, o_out, lse_out, k_all, vt_all = rest
    count = x_in.shape[0]
    qkv = dot(x_in[...], jnp.concatenate([w_in[0], w_in[1], w_in[2]], axis=1))
    cos_t, sin_t = cosine[...], sine[...]
    query = turn(qkv[:, :128] + bias[0:1], cos_t, sin_t).astype(BF16)
    key = turn(qkv[:, 128:256] + bias[1:2], cos_t, sin_t).astype(BF16)
    value = (qkv[:, 256:] + bias[2:3]).astype(BF16)
    q_out[...] = query
    k_out[...] = key
    v_out[...] = value
    if before:
        k_all[:before] = old_k[...]
        vt_all[:, :before] = old_v[...].T
    k_all[before:] = key
    vt_all[:, before:] = value.T
    for local in range(count // BQ):
        block = before // BQ + local
        first, last = key_range(block)
        span = slice(local * BQ, (local + 1) * BQ)
        low_row = low[:, span]
        outs = []
        for head, part in enumerate(head_masks(q_out[span])):
            score, mask = masked_scores(k_all[first:last], part, first, block, low_row)
            score = mask(score, -1e30)
            top = jnp.max(score, axis=0, keepdims=True)
            expo = jnp.exp2(score - top)
            total = jnp.sum(expo, axis=0, keepdims=True)
            prob = (expo * (1.0 / total)).astype(BF16)
            outs.append(dot(vt_all[:, first:last], prob))
            lse_out[0, head : head + 1, span] = top + jnp.log2(total)
        upper = lax.broadcasted_iota(jnp.int32, outs[0].shape, 0) < HEAD_DIM
        joined = jnp.where(upper, outs[0], outs[1]) * valid[:, span]
        o_out[span] = joined.T.astype(BF16)


def attn_fwd(normed, weight, bias, cosine, sine, low, valid, old, part):
    width, local = weight.shape[1:]
    count = cosine.shape[0]
    before = 0 if old is None else old[0].shape[0]
    pairs = local // 128
    row = lambda n: pl.BlockSpec((n, 128), lambda i: (0, i))
    whole = lambda a: pl.BlockSpec(a.shape, lambda i: (0,) * a.ndim)
    args = [normed, weight, bias, cosine, sine, low, valid] + ([] if old is None else list(old))
    specs = [
        pl.BlockSpec((count, width), lambda i: (part, 0)),
        pl.BlockSpec((3, width, 128), lambda i: (0, 0, i)),
        row(3),
        *map(whole, (cosine, sine, low, valid)),
    ]
    specs += [row(before)] * (0 if old is None else 2)
    flat = jax.ShapeDtypeStruct((count, local), BF16)
    return pl.pallas_call(
        functools.partial(attn_fwd_body, before),
        grid=(pairs,),
        in_specs=specs,
        out_specs=[row(count)] * 4 + [pl.BlockSpec((1, 2, count), lambda i: (i, 0, 0))],
        out_shape=[flat] * 4 + [jax.ShapeDtypeStruct((pairs, 2, count), F32)],
        scratch_shapes=[
            pltpu.VMEM((before + count, 128), BF16),
            pltpu.VMEM((128, before + count), BF16),
        ],
        cost_estimate=COST,
        name="attn_fwd",
    )(*args)


def attn_bwd_body(parts, *refs):
    qs, ks, vs = refs[:parts], refs[parts : 2 * parts], refs[2 * parts : 3 * parts]
    lses = refs[3 * parts : 4 * parts]
    do_in, cosine, sine, low, dq_out, dk_out, dv_out, bias_out, kt_all, dk_acc, dv_acc = refs[
        4 * parts :
    ]
    each = qs[0].shape[0]

    def rows(refs_of, first, last):
        pieces = []
        for part, ref in enumerate(refs_of):
            lo, hi = max(first, part * each), min(last, (part + 1) * each)
            if lo < hi:
                pieces.append(ref[lo - part * each : hi - part * each])
        return pieces[0] if len(pieces) == 1 else jnp.concatenate(pieces, axis=0)

    for part in range(parts):
        kt_all[:, part * each : (part + 1) * each] = ks[part][...].T
    dk_acc[...] = jnp.zeros_like(dk_acc)
    dv_acc[...] = jnp.zeros_like(dv_acc)
    sums = [jnp.zeros((1, 128), F32) for _ in range(3)]
    blocks = parts * each // BQ
    for block in range(blocks):
        first, last = key_range(block)
        span = slice(block * BQ, (block + 1) * BQ)
        low_row = low[:, span]
        part, inside = block * BQ // each, block * BQ % each
        queries = head_masks(rows(qs, span.start, span.stop))
        d_outs = head_masks(do_in[span])
        keys, values = rows(ks, first, last), rows(vs, first, last)
        probs, d_scores, d_queries = [], [], []
        for head in range(2):
            score, mask = masked_scores(keys, queries[head], first, block, low_row)
            lse = lses[part][0, head : head + 1, inside : inside + BQ]
            prob = mask(jnp.exp2(score - lse), 0.0)
            d_prob = dot(values, d_outs[head], NT)
            delta = jnp.sum(prob * d_prob, axis=0, keepdims=True)
            d_score = (prob * (d_prob - delta)).astype(BF16)
            probs.append(prob.astype(BF16))
            d_scores.append(d_score)
            d_queries.append(dot(kt_all[:, first:last], d_score))
        wide = slice(first, last)
        dv_acc[wide] += dot(jnp.concatenate(probs, 1), jnp.concatenate(d_outs, 0))
        dk_acc[wide] += dot(jnp.concatenate(d_scores, 1), jnp.concatenate(queries, 0))
        upper = lax.broadcasted_iota(jnp.int32, d_queries[0].shape, 0) < HEAD_DIM
        d_query = jnp.where(upper, d_queries[0], d_queries[1]).T * HEAD_DIM ** (-0.5)
        d_query = turn(d_query, cosine[span], -sine[span]).astype(BF16)
        dq_out[span] = d_query
        sums[0] += jnp.sum(d_query.astype(F32), axis=0, keepdims=True)
        done = [block - DOC_MOST // BQ] if block + 1 < blocks else range(block - DOC_MOST // BQ, blocks)
        for old in done:
            if old < 0:
                continue
            there = slice(old * BQ, (old + 1) * BQ)
            d_key = dk_acc[there] * HEAD_DIM ** (-0.5)
            d_key = turn(d_key, cosine[there], -sine[there]).astype(BF16)
            d_value = dv_acc[there].astype(BF16)
            dk_out[there] = d_key
            dv_out[there] = d_value
            sums[1] += jnp.sum(d_key.astype(F32), axis=0, keepdims=True)
            sums[2] += jnp.sum(d_value.astype(F32), axis=0, keepdims=True)
    bias_out[...] = jnp.concatenate(sums, axis=0)


def attn_bwd(qs, ks, vs, lses, d_out, cosine, sine, low):
    parts = len(qs)
    each, local = qs[0].shape
    count = parts * each
    row = lambda n: pl.BlockSpec((n, 128), lambda i: (0, i))
    whole = lambda a: pl.BlockSpec(a.shape, lambda i: (0,) * a.ndim)
    flat = jax.ShapeDtypeStruct((count, local), BF16)
    return pl.pallas_call(
        functools.partial(attn_bwd_body, parts),
        grid=(local // 128,),
        in_specs=[row(each)] * (3 * parts)
        + [pl.BlockSpec((1, 2, each), lambda i: (i, 0, 0))] * parts
        + [row(count), whole(cosine), whole(sine), whole(low)],
        out_specs=[row(count)] * 3 + [row(3)],
        out_shape=[flat] * 3 + [jax.ShapeDtypeStruct((3, local), F32)],
        scratch_shapes=[
            pltpu.VMEM((128, count), BF16),
            pltpu.VMEM((count, 128), F32),
            pltpu.VMEM((count, 128), F32),
        ],
        cost_estimate=MARK,
        name="attn_bwd",
    )(*qs, *ks, *vs, *lses, d_out, cosine, sine, low)


def mlp_body(x_in, dy_in, w_in, down_in, h_out, dg_out, du_out):
    for start in range(0, x_in.shape[0], 512):
        span = slice(start, start + 512)
        gate = dot(x_in[span], w_in[0])
        upper = dot(x_in[span], w_in[1])
        d_hidden = dot(dy_in[span], down_in[...], NT)
        sigma = jax.nn.sigmoid(gate)
        active = gate * sigma
        h_out[span] = (active * upper).astype(BF16)
        du_out[span] = (d_hidden * active).astype(BF16)
        dg_out[span] = (d_hidden * upper * sigma * (1.0 + gate * (1.0 - sigma))).astype(BF16)


def mlp(normed, y_grad, weight, down, part, parts):
    count, width = normed.shape
    rows = count // parts
    hidden = down.shape[0]
    step = min(256, hidden)
    fixed = pl.BlockSpec((rows, width), lambda i: (part, 0))
    return pl.pallas_call(
        mlp_body,
        grid=(pl.cdiv(hidden, step),),
        in_specs=[
            fixed,
            fixed,
            pl.BlockSpec((2, width, step), lambda i: (0, 0, i)),
            pl.BlockSpec((step, width), lambda i: (i, 0)),
        ],
        out_specs=[pl.BlockSpec((rows, step), lambda i: (0, i))] * 3,
        out_shape=[jax.ShapeDtypeStruct((rows, hidden), BF16)] * 3,
        cost_estimate=COST,
        name="mlp",
    )(normed, y_grad, weight, down)


def out_body(o_in, h_in, wo_in, wd_in, out):
    out[...] = (dot(o_in[...], wo_in[...]) + dot(h_in[...], wd_in[...])).astype(BF16)


def out_partial(o, h, out_weight, down, start, cols):
    rows, local = o.shape
    hidden = h.shape[1]
    step = min(512, cols)
    base = start // step
    return pl.pallas_call(
        out_body,
        grid=(cols // step,),
        in_specs=[
            pl.BlockSpec((rows, local), lambda i: (0, 0)),
            pl.BlockSpec((rows, hidden), lambda i: (0, 0)),
            pl.BlockSpec((local, step), lambda i: (0, base + i)),
            pl.BlockSpec((hidden, step), lambda i: (0, base + i)),
        ],
        out_specs=pl.BlockSpec((rows, step), lambda i: (0, i)),
        out_shape=jax.ShapeDtypeStruct((rows, cols), BF16),
        cost_estimate=COST,
        name="out_partial",
    )(o, h, out_weight, down)


def dxn_body(*refs):
    dq_in, dk_in, dv_in, dg_in, du_in = refs[:5]
    wqkv_in, w_in, x_in, stats_in, out, col_out = refs[5:]
    shift_sum = jnp.zeros((1, x_in.shape[1]), F32)
    gain_sum = jnp.zeros((1, x_in.shape[1]), F32)
    for start in range(0, x_in.shape[0], 256):
        span = slice(start, start + 256)
        total = dot(dq_in[span], wqkv_in[0], NT)
        total += dot(dk_in[span], wqkv_in[1], NT)
        total += dot(dv_in[span], wqkv_in[2], NT)
        total += dot(dg_in[span], w_in[0], NT)
        total += dot(du_in[span], w_in[1], NT)
        out[span] = total.astype(BF16)
        hat = (x_in[span].astype(F32) - stats_in[span, :1]) * stats_in[span, 1:]
        shift_sum += jnp.sum(total, axis=0, keepdims=True)
        gain_sum += jnp.sum(total * hat, axis=0, keepdims=True)
    col_out[...] = jnp.concatenate([gain_sum, shift_sum], axis=0)


def dxn_partial(dqkv, dg, du, wqkv, weight, x, stats, part):
    rows, hidden = dg.shape
    local, width = dqkv[0].shape[1], x.shape[1]
    step = min(512, width)
    whole = lambda a: pl.BlockSpec(a.shape, lambda i: (0,) * a.ndim)
    return pl.pallas_call(
        dxn_body,
        grid=(width // step,),
        in_specs=[pl.BlockSpec((rows, local), lambda i: (part, 0))] * 3
        + [
            whole(dg),
            whole(du),
            pl.BlockSpec((3, step, local), lambda i: (0, i, 0)),
            pl.BlockSpec((2, step, hidden), lambda i: (0, i, 0)),
            pl.BlockSpec((rows, step), lambda i: (part, i)),
            pl.BlockSpec((rows, 2), lambda i: (part, 0)),
        ],
        out_specs=[
            pl.BlockSpec((rows, step), lambda i: (0, i)),
            pl.BlockSpec((2, step), lambda i: (0, i)),
        ],
        out_shape=[
            jax.ShapeDtypeStruct((rows, width), BF16),
            jax.ShapeDtypeStruct((2, width), F32),
        ],
        cost_estimate=MARK if part else COST,
        name="dxn_partial",
    )(*dqkv, dg, du, wqkv, weight, x, stats)


def dw_sum(groups, lefts, rhs):
    position = 0
    for which, parts in groups:
        lhs = lefts[which]
        each = lhs.shape[0] // parts
        total = None
        for part in range(parts):
            piece = dot(lhs[part * each : (part + 1) * each], rhs[position][...], TN)
            total = piece if total is None else total + piece
            position += 1
        yield total


def dw_send_body(groups, order, *refs):
    *refs, out = refs
    number = len({which for which, _ in groups})
    start = 0
    for total in dw_sum(groups, refs[:number], refs[number:]):
        out[0, :, start : start + total.shape[1]] = total.astype(BF16)
        start += total.shape[1]


def dw_keep_body(groups, bundles, order, slots, *refs):
    number = len({which for which, _ in groups})
    lefts, refs = refs[:number], refs[number:]
    number = sum(parts for _, parts in groups)
    rhs, (received, *refs) = refs[:number], refs[number:]
    sends, keeps = refs[: len(bundles)], refs[len(bundles) :]
    step = pl.program_id(0)
    totals = dw_sum(groups, lefts, rhs)
    start = 0
    for number, bundle in enumerate(bundles):
        away = slots[3 * number, step] == 1
        pieces = []
        for _ in range(bundle):
            total = next(totals)
            stop = start + total.shape[1]
            pieces.append((total + received[0, :, start:stop].astype(F32)).astype(BF16))
            start = stop
        total = pieces[0] if bundle == 1 else jnp.concatenate(pieces, axis=1)

        @pl.when(away)
        def _(number=number, total=total):
            sends[number][0] = total

        @pl.when(jnp.logical_not(away))
        def _(number=number, total=total):
            keeps[number][0] = total


def dw_call(order, lefts, rhs, which, number, bundles, received=None, slots=None):
    count, width = lefts[0].shape
    step = width // (2 * number)
    groups = tuple((w, len(group)) for w, group in zip(which, rhs))
    flat = [part for group in rhs for part in group]
    columns = [group[0].shape[1] for group in rhs]
    scalars = [order] if slots is None else [order, slots]
    args = scalars + [*lefts, *flat]
    specs = [pl.BlockSpec((count, step), lambda i, order, *_: (0, order[i])) for _ in lefts]
    specs += [pl.BlockSpec(a.shape, lambda i, *_: (0, 0)) for a in flat]
    block = pl.BlockSpec((1, step, sum(columns)), lambda i, *_: (i, 0, 0))
    if received is None:
        body = functools.partial(dw_send_body, groups)
        out_specs = [block]
        shapes = [jax.ShapeDtypeStruct((number, step, sum(columns)), BF16)]
    else:
        body = functools.partial(dw_keep_body, groups, bundles)
        args.append(received)
        specs.append(block)
        ends = np.cumsum([0, *bundles])
        joined = [sum(columns[a:b]) for a, b in zip(ends, ends[1:])]
        out_specs = [
            pl.BlockSpec((1, step, c), lambda i, order, slots, r=3 * g + kind: (slots[r, i], 0, 0))
            for kind in (1, 2)
            for g, c in enumerate(joined)
        ]
        shapes = [jax.ShapeDtypeStruct((number // 2, step, c), BF16) for c in joined] * 2
    return pl.pallas_call(
        body,
        grid_spec=pltpu.PrefetchScalarGridSpec(
            num_scalar_prefetch=len(scalars), grid=(number,), in_specs=specs, out_specs=out_specs
        ),
        out_shape=shapes,
        cost_estimate=COST,
        name="weight_grad",
    )(*args)


def flip(size, bit):
    return [(i, i ^ bit) for i in range(size)]


class Order:
    def __init__(self):
        self.token = jnp.zeros((8, 128), F32)

    def __call__(self, function, *args):
        args, token = lax.optimization_barrier((args, self.token))
        out, self.token = lax.optimization_barrier((function(*args), token))
        return out

    def mark(self):
        self.token = mark(self.token)


def mark_body(seen, out):
    out[...] = seen[...]


def mark(seen):
    return pl.pallas_call(
        mark_body,
        out_shape=jax.ShapeDtypeStruct(seen.shape, seen.dtype),
        cost_estimate=MARK,
        name="mark",
    )(seen)


def after_body(value, seen, out):
    out[...] = value[...]


def after(value, seen):
    return pl.pallas_call(
        after_body,
        out_shape=jax.ShapeDtypeStruct(value.shape, value.dtype),
        cost_estimate=COST,
        name="after",
    )(value, seen)


def halving_order(bits):
    order = [0]
    for bit in reversed(bits):
        order = [offset ^ bit for offset in order] + order
    return order


class Scatter:
    def __init__(self, run, devices, lefts, rhs, which, bundles, swaps):
        self.run, self.devices, self.lefts, self.rhs = run, devices, lefts, rhs
        self.which, self.bundles = which, bundles
        bits = [1 << i for i in range(devices.bit_length() - 1)]
        self.offsets = halving_order(bits)
        self.order = lax.axis_index("dp").astype(jnp.int32) ^ jnp.asarray(self.offsets, jnp.int32)
        self.bits = []
        for swap in swaps:
            rest = bits[1:]
            if swap and len(rest) > 1:
                rest[0], rest[1] = rest[1], rest[0]
            self.bits.append(rest)

    def send(self):
        half = self.devices // 2
        call = lambda lefts, rhs: dw_call(
            self.order[:half], lefts, rhs, self.which, half, self.bundles
        )
        (sent,) = self.run(call, self.lefts, self.rhs)
        self.received = lax.ppermute(sent, "dp", flip(self.devices, 1))

    def keep(self):
        half = self.devices // 2
        kept = self.offsets[half:]
        rows, self.left = [], []
        for bits in self.bits:
            away = [int(offset & bits[0] != 0) for offset in kept]
            place = lambda flags: [max(0, sum(flags[: i + 1]) - 1) for i in range(half)]
            rows += [away, place(away), place([1 - a for a in away])]
            self.left.append([offset for offset in kept if not offset & bits[0]])
        slots = jnp.asarray(np.array(rows), jnp.int32)
        call = lambda lefts, rhs, received: dw_call(
            self.order[half:], lefts, rhs, self.which, half, self.bundles, received, slots
        )
        outs = self.run(call, self.lefts, self.rhs, self.received)
        number = len(self.bits)
        self.kept = outs[number:]
        self.received = [
            lax.ppermute(s, "dp", flip(self.devices, bits[0])) for s, bits in zip(outs, self.bits)
        ]
        self.stage = 1

    def next(self, cost=COST):
        rows = []
        for group, bits in enumerate(self.bits):
            bit = bits[self.stage]
            for away in (True, False):
                rows.append([i for i, o in enumerate(self.left[group]) if bool(o & bit) == away])
            self.left[group] = [o for o in self.left[group] if not o & bit]
        slots = jnp.asarray(np.array(rows), jnp.int32)
        call = lambda kept, received: next_call(kept, received, slots, len(rows[0]), cost)
        outs = self.run(call, self.kept, self.received)
        number = len(self.bits)
        self.kept = outs[number:]
        self.received = [
            lax.ppermute(s, "dp", flip(self.devices, bits[self.stage]))
            for s, bits in zip(outs, self.bits)
        ]
        self.stage += 1

    def last(self, pieces):
        while self.stage < len(self.bits[0]):
            self.next()
        call = lambda kept, received: last_call(kept, received, pieces)
        return self.run(call, self.kept, self.received)


def next_body(slots, *refs):
    number = len(refs) // 6
    for n in range(2 * number):
        pair, out = refs[2 * n : 2 * n + 2], refs[4 * number + n]
        out[0] = (pair[0][0].astype(F32) + pair[1][0].astype(F32)).astype(BF16)


def next_call(kept, received, slots, pieces, cost):
    rows = kept[0].shape[1]
    step = min(64, rows)
    args, specs, outs, shapes = [], [], [], []
    for away in (0, 1):
        for group, pair in enumerate(zip(kept, received)):
            columns = pair[0].shape[2]
            place = lambda i, j, slots, r=2 * group + away: (slots[r, i], j, 0)
            args += pair
            specs += [pl.BlockSpec((1, step, columns), place)] * 2
            outs.append(pl.BlockSpec((1, step, columns), lambda i, j, slots: (i, j, 0)))
            shapes.append(jax.ShapeDtypeStruct((pieces, rows, columns), BF16))
    return pl.pallas_call(
        next_body,
        grid_spec=pltpu.PrefetchScalarGridSpec(
            num_scalar_prefetch=1, grid=(pieces, rows // step), in_specs=specs, out_specs=outs
        ),
        out_shape=shapes,
        cost_estimate=cost,
        name="next",
    )(slots, *args)


def last_body(pieces, *refs):
    outs = iter(refs[2 * len(pieces) :])
    stacked = None
    place = 0
    for n, widths in enumerate(pieces):
        kept, received = refs[2 * n], refs[2 * n + 1]
        start = 0
        for width, turned in widths:
            span = slice(start, start + width)
            start += width
            total = kept[0, :, span].astype(F32) + received[0, :, span].astype(F32)
            if turned:
                next(outs)[...] = total.T
                continue
            stacked = next(outs) if stacked is None else stacked
            if stacked.shape[0] == total.shape[0]:
                stacked[:, place] = total
            else:
                stacked[place] = total
            place += 1


def last_call(kept, received, pieces):
    rows = kept[0].shape[1]
    step = min(128, rows)
    args, specs, outs, shapes, stacked = [], [], [], [], []
    for pair, widths in zip(zip(kept, received), pieces):
        args += pair
        specs += [pl.BlockSpec((1, step, pair[0].shape[2]), lambda i: (0, i, 0))] * 2
        for width, turned in widths:
            if turned:
                outs.append(pl.BlockSpec((width, step), lambda i: (0, i)))
                shapes.append(jax.ShapeDtypeStruct((width, rows), F32))
            else:
                stacked.append(width)
    if len(stacked) == 2:
        outs.append(pl.BlockSpec((step, 2, stacked[0]), lambda i: (i, 0, 0)))
        shapes.append(jax.ShapeDtypeStruct((rows, 2, stacked[0]), F32))
    elif stacked:
        outs.append(pl.BlockSpec((len(stacked), step, stacked[0]), lambda i: (0, i, 0)))
        shapes.append(jax.ShapeDtypeStruct((len(stacked), rows, stacked[0]), F32))
    return pl.pallas_call(
        functools.partial(last_body, pieces),
        grid=(rows // step,),
        in_specs=specs,
        out_specs=outs,
        out_shape=shapes,
        cost_estimate=COST,
        name="last",
    )(*args)


LINE = 4


def move_body(has, finish, inner, *refs):
    refs = iter(refs)
    partial, old, swapped, sum_, crossed = (next(refs) if given else None for given in has)
    refs = list(refs)
    total = refs.pop() if old is not None else None
    send = refs.pop() if crossed is not None else None
    extra = refs
    slab = 16

    def rows(i, carry):
        span = pl.ds(pl.multiple_of(i * slab, slab), slab)
        if old is not None:
            total[span] = (old[span].astype(F32) + swapped[span].astype(F32)).astype(BF16)
        if crossed is None:
            return carry
        added = sum_[span].astype(F32) + crossed[span].astype(F32)
        mine = finish(added, *(e[...] if e.shape[0] == 1 else e[span] for e in extra)).astype(BF16)
        if partial is not None:
            mine = jnp.where(inner[0] == 1, mine, partial[span])
        send[span] = mine
        return carry

    lax.fori_loop(0, (total if send is None else send).shape[0] // slab, rows, 0, unroll=2)


def move_call(inner, arrays, finish, extra, part):
    has = [a is not None for a in arrays]
    given = [a for a in arrays if a is not None]
    rows, width = given[0].shape
    step = min(128, rows)
    base = part * (rows // step)
    fixed = lambda i, inner: jnp.where(inner[0] == 1, i, 0)

    def spec(a):
        if a.shape[0] == 1:
            return pl.BlockSpec(a.shape, lambda i, inner: (0, 0))
        return pl.BlockSpec((step, a.shape[1]), lambda i, inner: (base + fixed(i, inner), 0))

    block = pl.BlockSpec((step, width), lambda i, inner: (i, 0))
    in_block = pl.BlockSpec((step, width), lambda i, inner: (fixed(i, inner), 0))
    out_block = pl.BlockSpec((step, width), lambda i, inner: (jnp.where(inner[0] == 1, 0, i), 0))
    in_specs = [out_block if a is arrays[0] else in_block for a in given]
    number = has[1] + has[4]
    return pl.pallas_call(
        functools.partial(move_body, has, finish),
        grid_spec=pltpu.PrefetchScalarGridSpec(
            num_scalar_prefetch=1,
            grid=(rows // step,),
            in_specs=in_specs + [spec(a) for a in extra],
            out_specs=[block] * number,
        ),
        out_shape=[jax.ShapeDtypeStruct((rows, width), BF16)] * number,
        cost_estimate=COST,
        name="move",
    )(inner, *given, *extra)


class Lines:
    def __init__(self, run, size, number):
        self.run, self.size, self.number, self.stage = run, size, number, 0
        lines = range(0, size, LINE)
        self.inward = [(b, b + 1) for b in lines] + [(b + 3, b + 2) for b in lines]
        self.across = [(b + 1, b + 2) for b in lines] + [(b + 2, b + 1) for b in lines]
        self.outward = [(b + 1, b) for b in lines] + [(b + 2, b + 3) for b in lines]
        place = lax.axis_index("mp") % LINE
        self.inner = (place == 1) | (place == 2)
        self.flag = self.inner.astype(jnp.int32).reshape(1)
        self.partial = self.sum = self.crossed = self.swapped = None
        self.done = []

    def step(self, partial=None, finish=None, extra=(), part=0):
        stage, number = self.stage, self.number
        self.stage += 1

        def move(partial, old, swapped, sum_, crossed):
            if crossed is None:
                if old is None:
                    return partial, None
                return partial, *move_call(self.flag, (None, old, swapped, None, None), None, (), 0)
            bit = LINE
            while bit < self.size:
                sum_ = (sum_.astype(F32) + crossed.astype(F32)).astype(BF16)
                pairs = [(i, i ^ bit) for i in range(self.size) if i % LINE in (1, 2)]
                crossed = lax.ppermute(sum_, "mp", pairs)
                bit *= 2
            arrays = (partial, old, None if old is None else swapped, sum_, crossed)
            outs = move_call(self.flag, arrays, finish, extra, part)
            return outs if len(outs) == 2 else (outs[0], None)

        old = self.partial if 1 <= stage <= number else None
        crossed = self.crossed if 2 <= stage else None
        send, total = self.run(move, partial, old, self.swapped, self.sum, crossed)
        pairs = (self.inward if stage < number else []) + (self.outward if stage >= 2 else [])
        self.swapped = lax.ppermute(send, "mp", pairs)
        if total is not None:
            self.crossed = lax.ppermute(total, "mp", self.across)
        self.partial, self.sum = partial, total
        if stage >= 2:
            self.done.append((send, self.swapped))


def shards(
    dp,
    mp,
    inputs,
    segment_ids,
    pad_count,
    layer_norm_gain,
    layer_norm_bias,
    qkv_weight,
    qkv_bias,
    out_weight,
    gateup_weight,
    down_weight,
    y_grad,
):
    count, width = inputs.shape
    local = qkv_weight.shape[2]
    parts = 2
    rows = count // parts

    seg = segment_ids[0]
    steps = jnp.arange(count, dtype=jnp.int32)
    start = jnp.sum((seg[None, :] < seg[:, None]).astype(jnp.int32), axis=1)
    valid = steps < count - pad_count[0]
    low = jnp.where(valid, start, steps)[None, :]
    valid_row = valid.astype(F32)[None, :]
    lane = jnp.arange(128, dtype=jnp.int32) % HEAD_DIM
    half = ROT // 2
    freq = jnp.power(10000.0, -2.0 * (lane % half).astype(F32) / ROT)
    freq = jnp.where(lane < ROT, freq, 0.0)
    angle = (steps - start).astype(F32)[:, None] * freq[None, :]
    sign = jnp.where(lane < half, -1.0, 1.0)
    cosine = jnp.cos(angle)
    sine = jnp.sin(angle) * sign[None, :]

    xf = inputs.astype(F32)
    mean = jnp.mean(xf, axis=-1, keepdims=True)
    removed = xf - mean
    inv = lax.rsqrt(jnp.mean(removed * removed, axis=-1, keepdims=True) + EPS)
    normed = (removed * inv * layer_norm_gain + layer_norm_bias).astype(BF16)

    stats = jnp.concatenate([mean, inv], axis=1)

    wqkv = jnp.transpose(qkv_weight, (1, 0, 2))

    def cotangent(y_grad, out_weight):
        d_attn = lax.dot_general(y_grad, out_weight, NT, preferred_element_type=F32).astype(BF16)
        return d_attn * valid.astype(BF16)[:, None]

    run = Order()
    tables = (normed, cosine, sine, low, valid_row)
    weight, tables = run(
        lambda a, tables: (jnp.transpose(a, (1, 0, 2)), tables), gateup_weight, tables
    )
    normed, cosine, sine, low, valid_row = tables
    lines = Lines(run, mp, 2 * parts)
    old = None
    qs, ks, vs, os, lses, hs, dgs, dus = ([] for _ in range(8))
    for part in range(parts):
        span = slice(part * rows, (part + 1) * rows)

        def attend(normed, old, span=span, part=part):
            tables = cosine[span], sine[span], low[:, span], valid_row[:, span]
            return attn_fwd(normed, wqkv, qkv_bias, *tables, old, part)

        q, k, v, o, lse = run(attend, normed, old)
        old = (k, v)
        h, dg, du = run(
            lambda *a, part=part: mlp(*a, part, parts), normed, y_grad, weight, down_weight
        )
        for stack, item in zip((qs, ks, vs, os, lses, hs, dgs, dus), (q, k, v, o, lse, h, dg, du)):
            stack.append(item)
        partial = run(lambda *a: out_partial(*a, 0, width), o, h, out_weight, down_weight)
        if part == parts - 1:
            d_attn = run(cotangent, y_grad, out_weight)
        lines.step(partial)

    def finish_out(total, x):
        return x.astype(F32) + total

    gateup = Scatter(run, dp, [normed], [dgs, dus], (0, 0), (1, 1), (False, True))

    def emit(part):
        call = lambda dqkv, dg, du: dxn_partial(
            dqkv, dg, du, wqkv, weight, inputs, stats, part
        )
        return run(call, dqkv, dgs[part], dus[part])

    def finish_grad(total, x, dy, stats, gain):
        mean, inv = stats[:, :1], stats[:, 1:]
        hat = (x.astype(F32) - mean) * inv
        scaled = total * gain
        average = jnp.mean(scaled, axis=1, keepdims=True)
        slope = jnp.mean(scaled * hat, axis=1, keepdims=True)
        return dy.astype(F32) + inv * (scaled - average - hat * slope)

    grad_extra = (inputs, y_grad, stats, layer_norm_gain[None, :])

    def store(target, part, mine, received):
        step = lambda target, mine, received: lax.dynamic_update_slice(
            target, jnp.where(lines.inner, mine, received), (part * rows, 0)
        )
        return run(step, target, mine, received)

    blank = jnp.zeros((count, width), BF16)
    hidden = down_weight.shape[0]
    *dqkv, bias_grad = run(lambda *a: attn_bwd(*a, cosine, sine, low), qs, ks, vs, lses, d_attn)
    rest = Scatter(
        run,
        dp,
        [y_grad, normed],
        [hs, os] + [[a] for a in dqkv],
        (0, 0, 1, 1, 1),
        (2, 3),
        (True, False),
    )
    partial, columns = emit(0)
    lines.step(partial, finish_out, (inputs,), 0)
    partial, columns1 = emit(1)

    def small_step(value, axis, bit):
        size = {"dp": dp, "mp": mp}[axis]
        return run(jnp.add, value, lax.ppermute(value, axis, flip(size, bit)))

    small = run(
        lambda a, b, c: jnp.concatenate([(a + b).reshape(-1), c.reshape(-1)]),
        columns,
        columns1,
        bias_grad,
    )
    small = small_step(small, "dp", 1)
    gateup.send()
    bit = 2
    while bit < dp // 2:
        small = small_step(small, "dp", bit)
        bit *= 2
    rest.send()
    while bit < dp:
        small = small_step(small, "dp", bit)
        bit *= 2
    column_sums = small[: 2 * width]
    bias_sum = small[2 * width :].reshape(bias_grad.shape)
    lines.step(partial, finish_out, (inputs,), 1)
    run.mark()
    gateup.keep()
    rest.keep()
    result = store(blank, 0, *lines.done[0])
    lines.step(None, finish_grad, grad_extra, 0)
    gateup.next(MARK)
    result = store(result, 1, *lines.done[1])
    rest.next()
    column_sums = small_step(column_sums, "mp", 1)
    lines.step(None, finish_grad, grad_extra, 1)
    x_grad = store(blank, 0, *lines.done[2])
    (gateup_grad,) = gateup.last((((hidden, False),), ((hidden, False),)))
    down_grad, out_grad, qkv_grad = rest.last(
        (((hidden, True), (local, True)), ((local, False),) * 3)
    )
    qkv_grad = jnp.transpose(qkv_grad, (1, 0, 2))
    bit = 2
    while bit < mp:
        column_sums = small_step(column_sums, "mp", bit)
        bit *= 2
    column_sums = column_sums.reshape(2, width)
    column_sums = after(column_sums, run.token)
    x_grad = store(x_grad, 1, *lines.done[3])
    return (
        result,
        x_grad,
        column_sums[0],
        column_sums[1],
        qkv_grad,
        bias_sum,
        out_grad,
        gateup_grad,
        down_grad,
    )


def solution(mesh):
    placed = (
        P("dp", None),
        P("dp", None),
        P("dp"),
        P(),
        P(),
        P(None, None, "mp"),
        P(None, "mp"),
        P("mp", None),
        P(None, None, "mp"),
        P("mp", None),
        P("dp", None),
    )
    return jax.shard_map(
        functools.partial(shards, mesh.shape["dp"], mesh.shape["mp"]),
        mesh=mesh,
        in_specs=placed,
        out_specs=(
            P("dp", None),
            P("dp", None),
            P(),
            P(),
            P("dp", None, "mp"),
            P(None, "mp"),
            P("mp", "dp"),
            P("dp", None, "mp"),
            P("mp", "dp"),
        ),
        check_vma=False,
    )
```
